32 devices in a mesh: rep: 2 (over y), seq: 8 (over z, x), head: 2 (over core).
Axes of the slice: x: 2, y: 2, z: 4, core: 2. Of those that a mesh axis runs over, the one named last changes fastest.
Arguments:
- x_in: bfloat16 [1024, 1024], P(('rep', 'seq'), 'head'), parts along dimension 0, may hold values from -6 to 6
- b_in: bfloat16 [1024, 2048], P(('rep', 'seq'), 'head'), parts along dimension 0, may hold values from -6 to 6
- c_in: bfloat16 [1024, 2048], P(('rep', 'seq'), 'head'), parts along dimension 0, may hold values from -6 to 6
- z_in: bfloat16 [1024, 1024], P(('rep', 'seq'), 'head'), parts along dimension 0, may hold values from -6 to 6
- dt_raw: bfloat16 [1024, 16], P(('rep', 'seq'), 'head'), parts along dimension 0, may hold values from -3 to 6
- dt_bias: float32 [16], P('head'), may hold values from -4 to -3
- a_log: float32 [16], P('head')
- d_skip: float32 [16], P('head'), may hold values from 0.5 to 1.5
- conv_x: bfloat16 [4, 1024], P(None, 'head'), may hold values from -3 to 3
- conv_b: bfloat16 [4, 2048], P(None, 'head'), may hold values from -3 to 3
- conv_c: bfloat16 [4, 2048], P(None, 'head'), may hold values from -3 to 3
- norm_gain: float32 [1024], P('head'), may hold values from 0.5 to 1.5
Outputs:
- mixed: bfloat16 [1024, 1024], P(('rep', 'seq'), 'head'), parts along dimension 0
The draws below stay inside these ranges and needn't reach their ends.
There are 2 independent parts, one for each index of `rep`. The reference program is written for one: setup_inputs(seed, part) draws one part's arguments, and reference() takes and returns one part's arrays. A program takes and returns all parts, laid end to end along the dimension named above; an argument that names none is the same for every part. Nothing has to cross between parts.
All inputs are finite; a program needn't handle non-finite values.
Results may differ from the reference program's by a relative error of at most 0.0051.
Values may be sent and summed in bfloat16 or wider, within the bound.
No kernel may reach another device: no remote copies, remote signals or barrier semaphores. Data moves between devices by JAX's collectives and lax.ppermute only.
A program may use at most 64 MiB of HBM per device.

```python
import jax
import jax.numpy as jnp
from jax import lax

HEAD_DIM = 64
STATE = 256
GROUPS = 8
CONV = 4
BLOCK = 256
HEADS = 16
TOKENS = 512


def draw_dt_raw(key, part):
    first_key, second_key = jax.random.split(jax.random.fold_in(key, 11))
    base = jnp.clip(0.5 * jax.random.normal(first_key, (TOKENS, HEADS), jnp.float32), -3.0, 3.0)
    spots = jax.random.randint(second_key, (8,), 0, TOKENS)
    positions = jnp.arange(TOKENS)[:, None]
    struck = jnp.any(positions == spots[None, :], axis=1)
    return (base + jnp.where(struck, 3.0, 0.0)[:, None]).astype(jnp.bfloat16)


def draw_a_log(key, part):
    first_key, second_key, third_key = jax.random.split(jax.random.fold_in(key, 23), 3)
    slow = jax.random.randint(first_key, (HEADS,), 0, 2) == 0
    slow_rate = jax.random.uniform(second_key, (HEADS,), jnp.float32, 0.3, 1.0) / (0.03 * TOKENS)
    fast_rate = jax.random.uniform(third_key, (HEADS,), jnp.float32, 0.5, 1.5)
    return jnp.log(jnp.where(slow, slow_rate, fast_rate))


def shard_levels(own_key, shape, pieces, smallest, high):
    loudness, own = 1.0, jax.random.fold_in(own_key, 6)
    for position, shards_of in pieces:
        heights = jnp.exp(jax.random.uniform(jax.random.fold_in(own, position), (shards_of,), jnp.float32, smallest / len(pieces), high / len(pieces)))
        loudness = loudness * jnp.repeat(heights, shape[position] // shards_of).reshape([-1 if axis == position else 1 for axis in range(len(shape))])
    return loudness


def gaussian(rng, dims, deviation, most, cuts=(), kind=jnp.bfloat16):
    level = shard_levels(rng, dims, cuts, -0.22, 0.18) if cuts else 1.0
    drawn = jax.random.normal(rng, dims, jnp.float32) * deviation * level
    return jnp.minimum(jnp.maximum(drawn, -most), most).astype(kind)


def setup_inputs(seed: int = 0, part: int = 0) -> dict:
    streams_of = jax.random.split(jax.random.key(seed), 13)
    part_splits = jax.random.split(jax.random.fold_in(streams_of[12], part), 13)
    x_in = gaussian(part_splits[0], (TOKENS, HEADS * HEAD_DIM), 1.0, 6.0, ((0, 8), (1, 2)))
    b_in = gaussian(part_splits[1], (TOKENS, GROUPS * STATE), 1.0, 6.0, ((0, 8), (1, 2)))
    c_in = gaussian(part_splits[2], (TOKENS, GROUPS * STATE), 1.0, 6.0, ((0, 8), (1, 2)))
    z_in = gaussian(part_splits[3], (TOKENS, HEADS * HEAD_DIM), 1.0, 6.0, ((0, 8), (1, 2)))
    dt_raw = draw_dt_raw(jax.random.fold_in(jax.random.fold_in(streams_of[12], part), 71), part)
    dt_bias = jnp.clip(-4.0 + 1.0 * jax.random.uniform(streams_of[5], (HEADS,), jnp.float32) ** shard_levels(streams_of[5], (HEADS,), ((0, 2),), -0.2, 0.2), -4.0, -3.0)
    a_log = draw_a_log(jax.random.fold_in(streams_of[12], 71), part)
    d_skip = jnp.clip(0.5 + 1.0 * jax.random.uniform(streams_of[7], (HEADS,), jnp.float32) ** shard_levels(streams_of[7], (HEADS,), ((0, 2),), -0.2, 0.2), 0.5, 1.5)
    conv_x = gaussian(streams_of[8], (CONV, HEADS * HEAD_DIM), CONV ** -0.5, 3.0, ((1, 2),))
    conv_b = gaussian(streams_of[9], (CONV, GROUPS * STATE), CONV ** -0.5, 3.0, ((1, 2),))
    conv_c = gaussian(streams_of[10], (CONV, GROUPS * STATE), CONV ** -0.5, 3.0, ((1, 2),))
    norm_gain = jnp.clip(1.0 + 0.1 * jax.random.normal(streams_of[11], (HEADS * HEAD_DIM,), jnp.float32), 0.5, 1.5)
    return {"x_in": x_in, "b_in": b_in, "c_in": c_in, "z_in": z_in, "dt_raw": dt_raw, "dt_bias": dt_bias, "a_log": a_log, "d_skip": d_skip, "conv_x": conv_x, "conv_b": conv_b, "conv_c": conv_c, "norm_gain": norm_gain}


def causal_conv(signal, kernel):
    taps_total = kernel.shape[0]
    length = signal.shape[0]
    padded = jnp.pad(signal, ((taps_total - 1, 0), (0, 0)))
    summed = jnp.zeros(signal.shape, jnp.float32)
    for offset in range(taps_total):
        summed = summed + kernel[offset].astype(jnp.float32) * padded[offset:offset + length].astype(jnp.float32)
    return jax.nn.silu(summed).astype(jnp.bfloat16)

def blockwise_scan(x_head, b_head, c_head, rates, decays):
    length = x_head.shape[0]
    blocks = length // BLOCK
    x_part = x_head.reshape(blocks, BLOCK, -1).astype(jnp.float32)
    b_part = b_head.reshape(blocks, BLOCK, -1).astype(jnp.float32)
    c_part = c_head.reshape(blocks, BLOCK, -1).astype(jnp.float32)
    rate_part = rates.reshape(blocks, BLOCK)
    log_decay = jnp.cumsum(decays.reshape(blocks, BLOCK), axis=1)
    causal = jnp.arange(BLOCK)[:, None] >= jnp.arange(BLOCK)[None, :]
    scores = jnp.einsum('cin,cjn->cij', c_part, b_part, precision=lax.Precision.HIGHEST)
    spread = jnp.where(causal, log_decay[:, :, None] - log_decay[:, None, :], 0.0)
    mixing = jnp.where(causal, scores * jnp.exp(spread) * rate_part[:, None, :], 0.0).astype(jnp.bfloat16)
    mixing = lax.optimization_barrier(mixing).astype(jnp.float32)
    inner = jnp.einsum('cij,cjp->cip', mixing, x_part, precision=lax.Precision.HIGHEST)
    weighted_b = (b_part * (jnp.exp(log_decay[:, -1:] - log_decay) * rate_part)[:, :, None]).astype(jnp.bfloat16)
    weighted_b = lax.optimization_barrier(weighted_b).astype(jnp.float32)
    block_states = jnp.einsum('cjn,cjp->cnp', weighted_b, x_part, precision=lax.Precision.HIGHEST)
    totals = log_decay[:, -1]

    def carry_step(state, pair):
        total, fresh = pair
        return (jnp.exp(total) * state + fresh, state)
    final_state, entering = lax.scan(carry_step, jnp.zeros(block_states.shape[1:], jnp.float32), (totals, block_states))
    entering_low = lax.optimization_barrier(entering.astype(jnp.bfloat16)).astype(jnp.float32)
    outer = jnp.exp(log_decay)[:, :, None] * jnp.einsum('cin,cnp->cip', c_part, entering_low, precision=lax.Precision.HIGHEST)
    return (inner + outer).reshape(length, -1)

def reference(x_in, b_in, c_in, z_in, dt_raw, dt_bias, a_log, d_skip, conv_x, conv_b, conv_c, norm_gain):
    length = x_in.shape[0]
    x_conv = causal_conv(x_in, conv_x)
    b_conv = causal_conv(b_in, conv_b)
    c_conv = causal_conv(c_in, conv_c)
    rates = jax.nn.softplus(dt_raw.astype(jnp.float32) + dt_bias[None, :])
    decays = rates * (-jnp.exp(a_log))[None, :]
    x_heads = x_conv.reshape(length, HEADS, HEAD_DIM)
    b_groups = b_conv.reshape(length, GROUPS, STATE)
    c_groups = c_conv.reshape(length, GROUPS, STATE)
    per_group = HEADS // GROUPS

    def one_head(head_id):
        group_id = head_id // per_group
        x_head = lax.dynamic_index_in_dim(x_heads, head_id, 1, keepdims=False)
        b_head = lax.dynamic_index_in_dim(b_groups, group_id, 1, keepdims=False)
        c_head = lax.dynamic_index_in_dim(c_groups, group_id, 1, keepdims=False)
        rate_head = lax.dynamic_index_in_dim(rates, head_id, 1, keepdims=False)
        decay_head = lax.dynamic_index_in_dim(decays, head_id, 1, keepdims=False)
        scanned = blockwise_scan(x_head, b_head, c_head, rate_head, decay_head)
        skip_head = lax.dynamic_index_in_dim(d_skip, head_id, 0, keepdims=False)
        return (scanned + skip_head * x_head.astype(jnp.float32)).astype(jnp.bfloat16)
    heads_out = lax.map(one_head, jnp.arange(HEADS, dtype=jnp.int32))
    merged = jnp.transpose(heads_out, (1, 0, 2)).reshape(length, HEADS * HEAD_DIM).astype(jnp.float32)
    gated = merged * jax.nn.silu(z_in.astype(jnp.float32))
    grouped = gated.reshape(length, GROUPS, -1)
    mean_square = lax.optimization_barrier(jnp.mean(grouped * grouped, axis=-1, keepdims=True))
    normed = (grouped * lax.rsqrt(mean_square + 1e-05)).reshape(length, -1)
    return (normed * norm_gain[None, :]).astype(jnp.bfloat16)
```

```python
import functools

import jax
import jax.numpy as jnp
from jax import lax
from jax.experimental import pallas as pl
from jax.experimental.pallas import tpu as pltpu
from jax.sharding import PartitionSpec as P

HEAD_DIM = 64
STATE = 256
BLOCK = 256
LANES = 128
HALO = 8
EDGE = 16
F32 = jnp.float32
BF16 = jnp.bfloat16
VMEM = pl.BlockSpec(memory_space=pltpu.VMEM)
SMEM = pl.BlockSpec(memory_space=pltpu.SMEM)
NT = (((1,), (1,)), ((), ()))
TN = (((0,), (0,)), ((), ()))
NN = (((1,), (0,)), ((), ()))


def dot(a, b, dims):
    return lax.dot_general(a, b, dims, preferred_element_type=F32)


class Sizes:
    def __init__(self, x_in, b_in, dt_raw, seq_total, taps):
        self.rows = x_in.shape[0]
        self.heads = dt_raw.shape[1]
        self.groups = b_in.shape[1] // STATE
        self.per_group = self.heads // self.groups
        self.places = BLOCK // self.rows
        self.blocks = seq_total // self.places
        self.taps = taps
        self.x_blocks = self.per_group * HEAD_DIM // LANES
        self.s_blocks = STATE // LANES
        self.cols = self.x_blocks + 2 * self.s_blocks
        self.message = self.rows * self.cols + self.heads
        self.pad_heads = max(8, self.per_group)
        if self.places != self.groups or self.rows * 2 != LANES or self.places != 4:
            raise ValueError("unsupported shapes")


def lane(start):
    return pl.ds(pl.multiple_of(start, LANES), LANES)


def place_of(sz):
    return lax.rem(lax.axis_index("seq"), sz.places)


def silu_half(half):
    return half + half * jnp.tanh(half)


def column_block(sz, group, t):
    if t < sz.x_blocks:
        return 0, (group * sz.x_blocks + t) * LANES
    t -= sz.x_blocks
    which, t = (1, t) if t < sz.s_blocks else (2, t - sz.s_blocks)
    return which, (group * sz.s_blocks + t) * LANES


def pack_kernel(sz, x, b, c, dt, m1, m2, m3, dt_own):
    place = place_of(sz)
    rows = sz.rows
    line = lax.broadcasted_iota(jnp.int32, (rows, LANES), 0)
    spot = lax.broadcasted_iota(jnp.int32, (rows, LANES), 1)
    turned = jnp.where(spot == line + rows * lax.rem(place, 2), 1.0, 0.0).astype(BF16)
    dt_rows = dot(dt[...], turned, TN).astype(BF16)
    dt_own[...] = dt_rows
    for k, m in ((3, m3), (2, m2), (1, m1)):
        group = lax.bitwise_xor(place, k)
        for t in range(sz.cols):
            which, start = column_block(sz, group, t)
            m[t * rows : (t + 1) * rows, :] = (x, b, c)[which][:, lane(start)]
        m[rows * sz.cols :, :] = dt_rows


def conv_block(buffer, at, count, taps, t):
    n = len(taps)
    first = HALO - (n - 1) + at
    cols = slice(t * LANES, (t + 1) * LANES)
    total = taps[0] * buffer[first : first + count, cols]
    for i in range(1, n):
        total = total + taps[i] * buffer[first + i : first + i + count, cols]
    return total


def halved_taps(ref, start, n):
    return [0.5 * ref[i : i + 1, lane(start)].astype(F32) for i in range(n)]


def gather(sz, buffer, place, base, count, own, messages):
    for k in range(sz.places):
        source = lax.bitwise_xor(place, k)
        at = pl.ds(pl.multiple_of(HALO + source * sz.rows, 8), sz.rows)
        for t in range(count):
            if k == 0:
                _, start = column_block(sz, place, base + t)
                part = own[:, lane(start)]
            else:
                row = (base + t) * sz.rows
                part = messages[k - 1][row : row + sz.rows, :]
            buffer[at, t * LANES : (t + 1) * LANES] = part.astype(F32)


def state_kernel(sz, bias, alog, x, b, c, dt_own, m1, m2, m3, conv_x, conv_b, halo,
                 msg, xc, bc, stats, first, xs, bs, dts, ends):
    chain = sz.blocks > 2
    place = place_of(sz)
    rows, messages = sz.rows, (m1, m2, m3)
    near = dt_own[...].astype(F32) + m1[rows * sz.cols :, :].astype(F32)
    far = m2[rows * sz.cols :, :].astype(F32) + m3[rows * sz.cols :, :].astype(F32)
    side = lax.div(place, 2)
    dts[:, lane(side * LANES)] = near
    dts[:, lane((1 - side) * LANES)] = far
    head0 = place * sz.per_group
    raw = pltpu.roll(dts[...], lax.rem(sz.heads - head0, sz.heads), 0)[0 : sz.pad_heads]
    shape = (sz.pad_heads, BLOCK)
    which = lax.broadcasted_iota(jnp.int32, shape, 0)
    shift = jnp.zeros(shape, F32)
    rate_log = jnp.zeros(shape, F32)
    for h in range(sz.per_group):
        shift = jnp.where(which == h, bias[head0 + h], shift)
        rate_log = jnp.where(which == h, alog[head0 + h], rate_log)
    raw = raw + shift
    rates = jnp.maximum(raw, 0.0) + jnp.log1p(jnp.exp(-jnp.abs(raw)))
    decays = -jnp.exp(rate_log) * rates
    high = decays.astype(BF16).astype(F32)
    middle = (decays - high).astype(BF16).astype(F32)
    low = decays - high - middle
    parts = jnp.concatenate([high, middle, low], axis=0).astype(BF16)
    line = lax.broadcasted_iota(jnp.int32, (BLOCK, BLOCK), 0)
    spot = lax.broadcasted_iota(jnp.int32, (BLOCK, BLOCK), 1)
    upto = jnp.where(line <= spot, 1.0, 0.0).astype(BF16)
    sums = dot(parts, upto, NN)
    n = sz.pad_heads
    log_decay = sums[0:n] + sums[n : 2 * n] + sums[2 * n : 3 * n]
    weight = jnp.exp(log_decay[:, BLOCK - 1 : BLOCK] - log_decay) * rates
    g = sz.per_group
    stats[0:g, :] = log_decay[0:g]
    stats[g : 2 * g, :] = rates[0:g]
    stats[2 * g : 3 * g, :] = jnp.exp(log_decay)[0:g]
    stats[3 * g : 4 * g, :] = weight[0:g]
    gather(sz, xs, place, 0, sz.x_blocks, x, messages)
    gather(sz, bs, place, sz.x_blocks, sz.s_blocks, b, messages)
    for t in range(sz.x_blocks + sz.s_blocks):
        buffer, u = (xs, t) if t < sz.x_blocks else (bs, t - sz.x_blocks)
        cols = slice(u * LANES, (u + 1) * LANES)
        if chain:
            buffer[0:HALO, cols] = halo[t * HALO : (t + 1) * HALO, :]
        else:
            buffer[0:HALO, cols] = jnp.zeros((HALO, LANES), F32)
    for t in range(sz.s_blocks):
        _, start = column_block(sz, place, sz.x_blocks + t)
        taps = halved_taps(conv_b, start, sz.taps)
        cols = slice(t * LANES, (t + 1) * LANES)
        bc[:, cols] = silu_half(conv_block(bs, 0, BLOCK, taps, t)).astype(BF16)
    states = []
    for t in range(sz.x_blocks):
        _, start = column_block(sz, place, t)
        taps = halved_taps(conv_x, start, sz.taps)
        cols = slice(t * LANES, (t + 1) * LANES)
        value = silu_half(conv_block(xs, 0, BLOCK, taps, t)).astype(BF16)
        xc[:, cols] = value
        turned = jnp.transpose(value.astype(F32))
        up = turned[0:HEAD_DIM] * weight[2 * t : 2 * t + 1]
        down = turned[HEAD_DIM:LANES] * weight[2 * t + 1 : 2 * t + 2]
        weighted = jnp.concatenate([up, down], axis=0).astype(BF16)
        states.append(dot(weighted, bc[...], NN))
    for t in range(sz.x_blocks):
        for s in range(sz.s_blocks):
            row = (t * sz.s_blocks + s) * LANES
            part = states[t][:, s * LANES : (s + 1) * LANES]
            msg[row : row + LANES, :] = part.astype(msg.dtype)
    base = sz.x_blocks * STATE
    for t in range(sz.cols):
        if t < sz.x_blocks + sz.s_blocks:
            buffer, u = (xs, t) if t < sz.x_blocks else (bs, t - sz.x_blocks)
            cols = slice(u * LANES, (u + 1) * LANES)
            head, tail = buffer[HALO : 2 * HALO, cols], buffer[BLOCK : BLOCK + HALO, cols]
        else:
            _, start = column_block(sz, place, t)
            own = c[:, lane(start)].astype(F32)
            for k in range(sz.places):
                source = lax.bitwise_xor(place, k)
                row = t * rows
                part = own if k == 0 else messages[k - 1][row : row + rows, :].astype(F32)
                at = pl.multiple_of(source * 2 * HALO, 8)
                ends[pl.ds(at, HALO), :] = part[0:HALO]
                ends[pl.ds(at + HALO, HALO), :] = part[rows - HALO :]
            head = ends[0:HALO, :]
            tail = ends[sz.places * 2 * HALO - HALO :, :]
        first[t * HALO : (t + 1) * HALO, :] = head
        msg[base + t * HALO : base + (t + 1) * HALO, :] = tail.astype(msg.dtype)


def inner_kernel(sz, c, m1, m2, m3, conv_c, xc, bc, stats, halo, inner, cc, columns, cs):
    chain = sz.blocks > 2
    place = place_of(sz)
    base = sz.x_blocks + sz.s_blocks
    g = sz.per_group
    columns[...] = jnp.transpose(stats[...])
    gather(sz, cs, place, base, sz.s_blocks, c, (m1, m2, m3))
    for t in range(sz.s_blocks):
        cols = slice(t * LANES, (t + 1) * LANES)
        if chain:
            cs[0:HALO, cols] = halo[(base + t) * HALO : (base + t + 1) * HALO, :]
        else:
            cs[0:HALO, cols] = jnp.zeros((HALO, LANES), F32)
        _, start = column_block(sz, place, base + t)
        taps = halved_taps(conv_c, start, sz.taps)
        cc[:, cols] = silu_half(conv_block(cs, 0, BLOCK, taps, t)).astype(BF16)
    half = BLOCK // 2
    skip = 0 if chain else EDGE
    for r in range(2):
        width = half * (r + 1)
        at = slice(r * half, (r + 1) * half)
        scores = dot(cc[at, :], bc[0:width, :], NT)
        line = lax.broadcasted_iota(jnp.int32, (half, width), 0) + r * half
        spot = lax.broadcasted_iota(jnp.int32, (half, width), 1)
        keep = (spot <= line) & (spot >= skip)
        low_lanes = lax.broadcasted_iota(jnp.int32, (half, LANES), 1) < HEAD_DIM
        for t in range(sz.x_blocks):
            cols = slice(t * LANES, (t + 1) * LANES)
            sums = []
            for h in (2 * t, 2 * t + 1):
                spread = columns[at, h : h + 1] - stats[h : h + 1, 0:width]
                rate = stats[g + h : g + h + 1, 0:width]
                mixing = scores * jnp.exp(jnp.where(keep, spread, -1e30)) * rate
                sums.append(dot(mixing.astype(BF16), xc[0:width, cols], NN))
            inner[at, cols] = jnp.where(low_lanes, sums[0], sums[1])


def outer_kernel(sz, skip, conv_x, conv_b, conv_c, xc, bc, cc, stats, columns, first, inner, arrived,
                 o0, o1, o2, o3, edge, x_all, c_all, total):
    chain = sz.blocks > 2
    place = place_of(sz)
    later = lax.axis_index("seq") >= sz.places
    g, rows = sz.per_group, sz.rows
    head0 = place * g
    low_lanes = lax.broadcasted_iota(jnp.int32, (BLOCK, LANES), 1) < HEAD_DIM
    if chain:
        x_all[...] = xc[...]
        c_all[...] = cc[...]
    else:
        base = sz.x_blocks * STATE
        renewed = []
        for t in range(sz.cols):
            ahead = arrived[base + t * HALO : base + (t + 1) * HALO, :].astype(F32)
            edge[0:HALO, :] = jnp.where(later, ahead, 0.0)
            edge[HALO : 2 * HALO, :] = first[t * HALO : (t + 1) * HALO, :]
            which, start = column_block(sz, place, t)
            taps = halved_taps((conv_x, conv_b, conv_c)[which], start, sz.taps)
            fresh = silu_half(conv_block(edge, 0, HALO, taps, 0))
            u = t - (0, sz.x_blocks, sz.x_blocks + sz.s_blocks)[which]
            old = (xc, bc, cc)[which][0:EDGE, u * LANES : (u + 1) * LANES].astype(F32)
            renewed.append(jnp.concatenate([fresh, old[HALO:EDGE]], axis=0).astype(BF16))
        for t in range(sz.x_blocks):
            cols = slice(t * LANES, (t + 1) * LANES)
            x_all[EDGE:, cols] = xc[EDGE:, cols]
            x_all[0:EDGE, cols] = renewed[t]
        for t in range(sz.s_blocks):
            cols = slice(t * LANES, (t + 1) * LANES)
            c_all[EDGE:, cols] = cc[EDGE:, cols]
            c_all[0:EDGE, cols] = renewed[sz.x_blocks + sz.s_blocks + t]
        b_edge = jnp.concatenate(renewed[sz.x_blocks : sz.x_blocks + sz.s_blocks], axis=1)
        edge_scores = dot(b_edge, c_all[...], NT)
        line = lax.broadcasted_iota(jnp.int32, (EDGE, BLOCK), 0)
        spot = lax.broadcasted_iota(jnp.int32, (EDGE, BLOCK), 1)
        keep = spot >= line
    for t in range(sz.x_blocks):
        cols = slice(t * LANES, (t + 1) * LANES)
        state = jnp.concatenate(
            [arrived[(t * sz.s_blocks + s) * LANES : (t * sz.s_blocks + s + 1) * LANES, :] for s in range(sz.s_blocks)],
            axis=1,
        )
        state = jnp.where(later, state.astype(F32), 0.0).astype(BF16)
        outer = dot(c_all[...], state, NT)
        growth = jnp.where(
            low_lanes,
            columns[:, 2 * g + 2 * t : 2 * g + 2 * t + 1],
            columns[:, 2 * g + 2 * t + 1 : 2 * g + 2 * t + 2],
        )
        gain = jnp.where(low_lanes, skip[head0 + 2 * t], skip[head0 + 2 * t + 1])
        out = inner[:, cols] + outer * growth + gain * x_all[:, cols].astype(F32)
        if not chain:
            mixed, values = [], []
            edge_low = lax.broadcasted_iota(jnp.int32, (EDGE, LANES), 1) < HEAD_DIM
            x_edge = renewed[t].astype(F32)
            for h in (2 * t, 2 * t + 1):
                spread = stats[h : h + 1, :] - columns[0:EDGE, h : h + 1]
                rate = columns[0:EDGE, g + h : g + h + 1]
                mixed.append(edge_scores * jnp.exp(jnp.where(keep, spread, -1e30)) * rate)
                mine = edge_low if h == 2 * t else jnp.logical_not(edge_low)
                values.append(jnp.where(mine, x_edge, 0.0))
            mixed = jnp.concatenate(mixed, axis=0).astype(BF16)
            values = jnp.concatenate(values, axis=0).astype(BF16)
            out = out + dot(mixed, values, TN)
        total[:, cols] = out
    for k, o in enumerate((o0, o1, o2, o3)):
        target = lax.bitwise_xor(place, k)
        o[...] = total[pl.ds(pl.multiple_of(target * rows, 8), rows), :].astype(BF16)


def norm_kernel(sz, o0, r1, r2, r3, z, gain, out):
    place = place_of(sz)
    width = sz.x_blocks * LANES
    for k, part in enumerate((o0, r1, r2, r3)):
        group = lax.bitwise_xor(place, k)
        at = pl.ds(pl.multiple_of(group * width, LANES), width)
        gate = 0.5 * z[:, at].astype(F32)
        value = part[...].astype(F32) * silu_half(gate)
        mean = jnp.sum(value * value, axis=-1, keepdims=True) * (1.0 / width)
        out[:, at] = (value * lax.rsqrt(mean + 1e-05) * gain[0:1, at]).astype(BF16)


def call(kernel, sz, outs, scratch, specs, name, flops=0, touched=0):
    return pl.pallas_call(
        functools.partial(kernel, sz),
        out_shape=[jax.ShapeDtypeStruct(s, d) for s, d in outs],
        in_specs=specs,
        out_specs=[VMEM] * len(outs),
        scratch_shapes=[pltpu.VMEM(s, d) for s, d in scratch],
        compiler_params=pltpu.CompilerParams(vmem_limit_bytes=24 << 20),
        cost_estimate=pl.CostEstimate(flops=flops, bytes_accessed=touched, transcendentals=0),
        name=name,
    )


def body(x_in, b_in, c_in, z_in, dt_raw, dt_bias, a_log, d_skip, conv_x, conv_b, conv_c, norm_gain):
    seq_total = lax.axis_size("seq")
    sz = Sizes(x_in, b_in, dt_raw, seq_total, conv_x.shape[0])
    n, rows = sz.places, sz.rows
    chain = sz.blocks > 2

    def swap(k):
        return [(i, i - i % n + ((i % n) ^ k)) for i in range(seq_total)]

    def onward(k, wrap):
        pairs = [(i, i + n * k) for i in range(seq_total)]
        return [(i, j % seq_total) for i, j in pairs if wrap or j < seq_total]

    message = ((sz.message, LANES), BF16)
    sent = call(pack_kernel, sz, [message] * 3 + [((sz.heads, LANES), BF16)], [], [VMEM] * 4, "pack")(
        x_in, b_in, c_in, dt_raw
    )
    dt_own = sent[3]
    came = [None] * 3
    for k in (3, 2, 1):
        came[k - 1] = lax.ppermute(sent[k - 1], "seq", swap(k))

    width = sz.x_blocks * LANES
    padded = BLOCK + HALO
    edge_rows = sz.cols * HALO
    if chain:
        own = []
        place = lax.rem(lax.axis_index("seq"), n)
        for t in range(sz.cols):
            which, start = column_block(sz, place, t)
            own.append(lax.dynamic_slice_in_dim((x_in, b_in, c_in)[which], start, LANES, 1)[rows - HALO :])
        tails = [jnp.concatenate(own, axis=0)]
        for k in range(1, n):
            tails.append(
                came[k - 1][: sz.cols * rows].reshape(sz.cols, rows, LANES)[:, rows - HALO :].reshape(-1, LANES)
            )
        tail = lax.dynamic_index_in_dim(
            jnp.stack(tails), lax.bitwise_xor(place, n - 1), 0, keepdims=False
        )
        halo = lax.ppermute(tail, "seq", onward(1, False)).astype(F32)
    else:
        halo = jnp.zeros((8, LANES), F32)

    stat_rows = 4 * sz.per_group
    msg, xc, bc, stats, first = call(
        state_kernel,
        sz,
        [
            ((sz.x_blocks * STATE + edge_rows, LANES), F32 if chain else BF16),
            ((BLOCK, width), BF16),
            ((BLOCK, STATE), BF16),
            ((stat_rows, BLOCK), F32),
            ((edge_rows, LANES), F32),
        ],
        [
            ((padded, width), F32),
            ((padded, STATE), F32),
            ((sz.heads, BLOCK), F32),
            ((n * 2 * HALO, LANES), F32),
        ],
        [SMEM] * 2 + [VMEM] * 10,
        "state",
    )(dt_bias, a_log, x_in, b_in, c_in, dt_own, *came, conv_x, conv_b, halo)

    if chain:
        cut = sz.x_blocks * STATE
        grown = msg[:cut].reshape(sz.x_blocks, sz.s_blocks, 2, HEAD_DIM, LANES)
        fade = jnp.exp(stats[: sz.per_group, BLOCK - 1]).reshape(sz.x_blocks, 1, 2, 1, 1)
        k = 1
        while k < sz.blocks:
            grown = grown + fade * lax.ppermute(grown, "seq", onward(k, False))
            fade = fade * lax.ppermute(fade, "seq", onward(k, False))
            k *= 2
        msg = jnp.concatenate([grown.reshape(cut, LANES), msg[cut:]], axis=0).astype(BF16)
    arrived = lax.ppermute(msg, "seq", onward(1, True))

    inner, cc, columns = call(
        inner_kernel,
        sz,
        [((BLOCK, width), F32), ((BLOCK, STATE), BF16), ((BLOCK, stat_rows), F32)],
        [((padded, STATE), F32)],
        [VMEM] * 9,
        "inner",
        flops=1 << 30,
        touched=1 << 22,
    )(c_in, *came, conv_c, xc, bc, stats, halo)

    piece = ((rows, width), BF16)
    back = call(
        outer_kernel,
        sz,
        [piece] * 4,
        [
            ((2 * HALO, LANES), F32),
            ((BLOCK, width), BF16),
            ((BLOCK, STATE), BF16),
            ((BLOCK, width), F32),
        ],
        [SMEM] + [VMEM] * 11,
        "outer",
    )(d_skip, conv_x, conv_b, conv_c, xc, bc, cc, stats, columns, first, inner, arrived)
    home = [None] * 3
    for k in (3, 2, 1):
        home[k - 1] = lax.ppermute(back[k], "seq", swap(k))

    out = call(norm_kernel, sz, [(x_in.shape, BF16)], [], [VMEM] * 6, "norm")(
        back[0], *home, z_in, norm_gain.reshape(1, -1)
    )
    return out[0]


def solution(mesh):
    rows, wide = P(("rep", "seq"), "head"), P(None, "head")
    placed = (rows,) * 5 + (P("head"),) * 3 + (wide,) * 3 + (P("head"),)
    return jax.shard_map(body, mesh=mesh, in_specs=placed, out_specs=rows, check_vma=False)
```

```python
import functools

import jax
import jax.numpy as jnp
from jax import lax
from jax.experimental import pallas as pl
from jax.experimental.pallas import tpu as pltpu
from jax.sharding import PartitionSpec as P

HEAD_DIM = 64
STATE = 256
BLOCK = 256
LANES = 128
HALO = 8
EDGE = 16
F32 = jnp.float32
BF16 = jnp.bfloat16
VMEM = pl.BlockSpec(memory_space=pltpu.VMEM)
HBM = pl.BlockSpec(memory_space=pltpu.HBM)
NT = (((1,), (1,)), ((), ()))
TN = (((0,), (0,)), ((), ()))
NN = (((1,), (0,)), ((), ()))


def dot(a, b, dims):
    return lax.dot_general(a, b, dims, preferred_element_type=F32)


class Sizes:
    def __init__(self, x_in, b_in, dt_raw, seq_total, taps):
        self.rows = x_in.shape[0]
        self.heads = dt_raw.shape[1]
        self.groups = b_in.shape[1] // STATE
        self.per_group = self.heads // self.groups
        self.places = BLOCK // self.rows
        self.blocks = seq_total // self.places
        self.taps = taps
        self.x_blocks = self.per_group * HEAD_DIM // LANES
        self.s_blocks = STATE // LANES
        self.base = self.x_blocks + self.s_blocks
        self.cols = self.base + self.s_blocks
        self.tail_at = self.rows * self.base
        self.dt_at = self.tail_at + self.s_blocks * HALO
        self.message = self.dt_at + self.heads
        self.message_c = self.rows * self.s_blocks
        self.pad_heads = max(8, self.per_group)
        self.stat_rows = 4 * self.per_group
        if self.places != self.groups or self.rows * 2 != LANES or self.places != 4:
            raise ValueError("unsupported shapes")


def lane(start):
    return pl.ds(pl.multiple_of(start, LANES), LANES)


def place_of(sz):
    return lax.rem(lax.axis_index("seq"), sz.places)


def silu_half(half):
    return half + half * jnp.tanh(half)


def column_block(sz, group, t):
    if t < sz.x_blocks:
        return 0, (group * sz.x_blocks + t) * LANES
    t -= sz.x_blocks
    which, t = (1, t) if t < sz.s_blocks else (2, t - sz.s_blocks)
    return which, (group * sz.s_blocks + t) * LANES


def pack_kernel(sz, x, b, c, dt, m0, m1, m2, m3, c0, c1, c2, c3, dt_here, sem):
    place = place_of(sz)
    rows = sz.rows
    copies = []

    def fetch(source, target):
        copies.append(pltpu.make_async_copy(source, target, sem.at[len(copies)]))
        copies[-1].start()

    fetch(dt, dt_here)
    for k, m, mc in ((3, m3, c3), (2, m2, c2), (1, m1, c1), (0, m0, c0)):
        group = lax.bitwise_xor(place, k)
        for t in range(sz.cols):
            which, start = column_block(sz, group, t)
            source = (x, b, c)[which].at[:, lane(start)]
            if t < sz.base:
                fetch(source, m.at[t * rows : (t + 1) * rows, :])
            else:
                u = t - sz.base
                fetch(source, mc.at[u * rows : (u + 1) * rows, :])
                at = sz.tail_at + u * HALO
                fetch(c.at[rows - HALO :, lane(start)], m.at[at : at + HALO, :])
    copies[0].wait()
    here = dt_here[...].astype(F32)
    twice = jnp.concatenate([here, here], axis=1)
    spot = lax.broadcasted_iota(jnp.int32, twice.shape, 1)
    mine = lax.div(spot, rows) == lax.rem(place, 2)
    dt_rows = jnp.where(mine, twice, 0.0).astype(BF16)
    for m in (m0, m1, m2, m3):
        m[sz.dt_at :, :] = dt_rows
    for copy in copies[1:]:
        copy.wait()


def conv_block(buffer, count, taps, t):
    n = len(taps)
    first = HALO - (n - 1)
    cols = slice(t * LANES, (t + 1) * LANES)
    total = taps[0] * buffer[first : first + count, cols]
    for i in range(1, n):
        total = total + taps[i] * buffer[first + i : first + i + count, cols]
    return total


def halved_taps(ref, start, n):
    return [0.5 * ref[i : i + 1, lane(start)].astype(F32) for i in range(n)]


def gather(sz, buffer, place, base, count, messages):
    for k, m in enumerate(messages):
        source = lax.bitwise_xor(place, k)
        at = pl.ds(pl.multiple_of(HALO + source * sz.rows, 8), sz.rows)
        for t in range(count):
            row = (base + t) * sz.rows
            buffer[at, t * LANES : (t + 1) * LANES] = m[row : row + sz.rows, :].astype(F32)


def of_heads(sz, ref, head0):
    shape = (sz.pad_heads, sz.heads)
    line = lax.broadcasted_iota(jnp.int32, shape, 0)
    spot = lax.broadcasted_iota(jnp.int32, shape, 1)
    row = jnp.broadcast_to(ref[...], shape)
    return jnp.sum(jnp.where(spot == line + head0, row, 0.0), axis=1, keepdims=True)


def state_kernel(sz, bias, alog, m0, m1, m2, m3, conv_x, conv_b, halo,
                 msg, xc, bc, stats, first, xs, bs, dts, tails):
    chain = sz.blocks > 2
    place = place_of(sz)
    messages = (m0, m1, m2, m3)
    near, far = (
        p[sz.dt_at :, :].astype(F32) + q[sz.dt_at :, :].astype(F32) for p, q in ((m0, m1), (m2, m3))
    )
    side = lax.div(place, 2)
    dts[:, lane(side * LANES)] = near
    dts[:, lane((1 - side) * LANES)] = far
    head0 = place * sz.per_group
    raw = pltpu.roll(dts[...], lax.rem(sz.heads - head0, sz.heads), 0)[0 : sz.pad_heads]
    raw = raw + of_heads(sz, bias, head0)
    rates = jnp.maximum(raw, 0.0) + jnp.log1p(jnp.exp(-jnp.abs(raw)))
    decays = -jnp.exp(of_heads(sz, alog, head0)) * rates
    high = decays.astype(BF16).astype(F32)
    middle = (decays - high).astype(BF16).astype(F32)
    low = decays - high - middle
    parts = jnp.concatenate([high, middle, low], axis=0).astype(BF16)
    line = lax.broadcasted_iota(jnp.int32, (BLOCK, BLOCK), 0)
    spot = lax.broadcasted_iota(jnp.int32, (BLOCK, BLOCK), 1)
    upto = jnp.where(line <= spot, 1.0, 0.0).astype(BF16)
    sums = dot(parts, upto, NN)
    n = sz.pad_heads
    log_decay = sums[0:n] + sums[n : 2 * n] + sums[2 * n : 3 * n]
    weight = jnp.exp(log_decay[:, BLOCK - 1 : BLOCK] - log_decay) * rates
    g = sz.per_group
    stats[0:g, :] = log_decay[0:g]
    stats[g : 2 * g, :] = rates[0:g]
    stats[2 * g : 3 * g, :] = jnp.exp(log_decay)[0:g]
    stats[3 * g : 4 * g, :] = weight[0:g]
    gather(sz, xs, place, 0, sz.x_blocks, messages)
    gather(sz, bs, place, sz.x_blocks, sz.s_blocks, messages)
    for t in range(sz.base):
        buffer, u = (xs, t) if t < sz.x_blocks else (bs, t - sz.x_blocks)
        cols = slice(u * LANES, (u + 1) * LANES)
        if chain:
            buffer[0:HALO, cols] = halo[t * HALO : (t + 1) * HALO, :]
        else:
            buffer[0:HALO, cols] = jnp.zeros((HALO, LANES), F32)
    for t in range(sz.s_blocks):
        _, start = column_block(sz, place, sz.x_blocks + t)
        taps = halved_taps(conv_b, start, sz.taps)
        cols = slice(t * LANES, (t + 1) * LANES)
        bc[:, cols] = silu_half(conv_block(bs, BLOCK, taps, t)).astype(BF16)
    states = []
    for t in range(sz.x_blocks):
        _, start = column_block(sz, place, t)
        taps = halved_taps(conv_x, start, sz.taps)
        cols = slice(t * LANES, (t + 1) * LANES)
        value = silu_half(conv_block(xs, BLOCK, taps, t)).astype(BF16)
        xc[:, cols] = value
        turned = jnp.transpose(value.astype(F32))
        up = turned[0:HEAD_DIM] * weight[2 * t : 2 * t + 1]
        down = turned[HEAD_DIM:LANES] * weight[2 * t + 1 : 2 * t + 2]
        weighted = jnp.concatenate([up, down], axis=0).astype(BF16)
        states.append(dot(weighted, bc[...], NN))
    for t in range(sz.x_blocks):
        for s in range(sz.s_blocks):
            row = (t * sz.s_blocks + s) * LANES
            part = states[t][:, s * LANES : (s + 1) * LANES]
            msg[row : row + LANES, :] = part.astype(msg.dtype)
    base = sz.x_blocks * STATE
    for t in range(sz.base):
        buffer, u = (xs, t) if t < sz.x_blocks else (bs, t - sz.x_blocks)
        cols = slice(u * LANES, (u + 1) * LANES)
        first[t * HALO : (t + 1) * HALO, :] = buffer[HALO : 2 * HALO, cols]
        msg[base + t * HALO : base + (t + 1) * HALO, :] = buffer[BLOCK : BLOCK + HALO, cols].astype(msg.dtype)
    size = sz.s_blocks * HALO
    for k, m in enumerate(messages):
        source = lax.bitwise_xor(place, k)
        at = pl.ds(pl.multiple_of(source * size, 8), size)
        tails[at, :] = m[sz.tail_at : sz.tail_at + size, :].astype(F32)
    last = tails[(sz.places - 1) * size :, :]
    msg[base + sz.base * HALO :, :] = last.astype(msg.dtype)


def inner_kernel(sz, skip, c0, c1, c2, c3, conv_c, xc, bc, stats, halo,
                 out, growth, gains, cc, columns, first_c, cs, turned):
    chain = sz.blocks > 2
    place = place_of(sz)
    g = sz.per_group
    turned[...] = jnp.transpose(stats[...])
    columns[...] = turned[0:EDGE, :]
    skips = of_heads(sz, skip, place * g)
    gather(sz, cs, place, 0, sz.s_blocks, (c0, c1, c2, c3))
    for t in range(sz.s_blocks):
        cols = slice(t * LANES, (t + 1) * LANES)
        if chain:
            cs[0:HALO, cols] = halo[(sz.base + t) * HALO : (sz.base + t + 1) * HALO, :]
        else:
            cs[0:HALO, cols] = jnp.zeros((HALO, LANES), F32)
        first_c[t * HALO : (t + 1) * HALO, :] = cs[HALO : 2 * HALO, cols]
        _, start = column_block(sz, place, sz.base + t)
        taps = halved_taps(conv_c, start, sz.taps)
        cc[:, cols] = silu_half(conv_block(cs, BLOCK, taps, t)).astype(BF16)
    half = BLOCK // 2
    skip_keys = 0 if chain else EDGE
    low_lanes = lax.broadcasted_iota(jnp.int32, (half, LANES), 1) < HEAD_DIM
    for t in range(sz.x_blocks):
        cols = slice(t * LANES, (t + 1) * LANES)
        gains[:, cols] = jnp.where(low_lanes[0:8], skips[2 * t : 2 * t + 1], skips[2 * t + 1 : 2 * t + 2])
    for r in range(2):
        width = half * (r + 1)
        at = slice(r * half, (r + 1) * half)
        scores = dot(cc[at, :], bc[0:width, :], NT)
        line = lax.broadcasted_iota(jnp.int32, (half, width), 0) + r * half
        spot = lax.broadcasted_iota(jnp.int32, (half, width), 1)
        keep = (spot <= line) & (spot >= skip_keys)
        for t in range(sz.x_blocks):
            cols = slice(t * LANES, (t + 1) * LANES)
            sums = []
            for h in (2 * t, 2 * t + 1):
                spread = turned[at, h : h + 1] - stats[h : h + 1, 0:width]
                rate = stats[g + h : g + h + 1, 0:width]
                mixing = scores * jnp.exp(jnp.where(keep, spread, -1e30)) * rate
                sums.append(dot(mixing.astype(BF16), xc[0:width, cols], NN))
            both = jnp.where(low_lanes, sums[0], sums[1])
            out[at, cols] = both + gains[0:1, cols] * xc[at, cols].astype(F32)
            rise = 2 * g + 2 * t
            growth[at, cols] = jnp.where(low_lanes, turned[at, rise : rise + 1], turned[at, rise + 1 : rise + 2])


def outer_kernel(sz, conv_x, conv_b, conv_c, xc, bc, cc, stats, columns, first, first_c, growth, gains,
                 inner, arrived, o0, o1, o2, o3, edge, c_all, total):
    chain = sz.blocks > 2
    place = place_of(sz)
    later = lax.axis_index("seq") >= sz.places
    g, rows = sz.per_group, sz.rows
    if chain:
        c_all[...] = cc[...]
    else:
        base = sz.x_blocks * STATE
        renewed = []
        for t in range(sz.cols):
            cols = slice(t * LANES, (t + 1) * LANES)
            ahead = arrived[base + t * HALO : base + (t + 1) * HALO, :].astype(F32)
            edge[0:HALO, cols] = jnp.where(later, ahead, 0.0)
            u = t - sz.base
            edge[HALO : 2 * HALO, cols] = (
                first[t * HALO : (t + 1) * HALO, :] if u < 0 else first_c[u * HALO : (u + 1) * HALO, :]
            )
        for t in range(sz.cols):
            which, start = column_block(sz, place, t)
            taps = halved_taps((conv_x, conv_b, conv_c)[which], start, sz.taps)
            fresh = silu_half(conv_block(edge, HALO, taps, t))
            u = t - (0, sz.x_blocks, sz.base)[which]
            old = (xc, bc, cc)[which][0:EDGE, u * LANES : (u + 1) * LANES].astype(F32)
            renewed.append(jnp.concatenate([fresh, old[HALO:EDGE]], axis=0).astype(BF16))
        for t in range(sz.s_blocks):
            cols = slice(t * LANES, (t + 1) * LANES)
            c_all[EDGE:, cols] = cc[EDGE:, cols]
            c_all[0:EDGE, cols] = renewed[sz.base + t]
        b_edge = jnp.concatenate(renewed[sz.x_blocks : sz.base], axis=1)
        edge_scores = dot(b_edge, c_all[...], NT)
        line = lax.broadcasted_iota(jnp.int32, (EDGE, BLOCK), 0)
        spot = lax.broadcasted_iota(jnp.int32, (EDGE, BLOCK), 1)
        keep = spot >= line
    for t in range(sz.x_blocks):
        cols = slice(t * LANES, (t + 1) * LANES)
        pieces = [
            arrived[(t * sz.s_blocks + s) * LANES : (t * sz.s_blocks + s + 1) * LANES, :]
            for s in range(sz.s_blocks)
        ]
        state = jnp.where(later, jnp.concatenate(pieces, axis=1).astype(F32), 0.0).astype(BF16)
        out = inner[:, cols] + dot(c_all[...], state, NT) * growth[:, cols]
        if not chain:
            mixed, values = [], []
            edge_low = lax.broadcasted_iota(jnp.int32, (EDGE, LANES), 1) < HEAD_DIM
            x_edge = renewed[t].astype(F32)
            for h in (2 * t, 2 * t + 1):
                spread = stats[h : h + 1, :] - columns[:, h : h + 1]
                rate = columns[:, g + h : g + h + 1]
                mixed.append(edge_scores * jnp.exp(jnp.where(keep, spread, -1e30)) * rate)
                mine = edge_low if h == 2 * t else jnp.logical_not(edge_low)
                values.append(jnp.where(mine, x_edge, 0.0))
            mixed = jnp.concatenate(mixed, axis=0).astype(BF16)
            values = jnp.concatenate(values, axis=0).astype(BF16)
            out = out + dot(mixed, values, TN)
            change = gains[0:1, cols] * (x_edge - xc[0:EDGE, cols].astype(F32))
            total[:, cols] = out
            total[0:EDGE, cols] = out[0:EDGE] + change
        else:
            total[:, cols] = out
    for k, o in enumerate((o0, o1, o2, o3)):
        target = lax.bitwise_xor(place, k)
        o[...] = total[pl.ds(pl.multiple_of(target * rows, 8), rows), :].astype(BF16)


def norm_kernel(sz, o0, r1, r2, r3, z, gain, out):
    place = place_of(sz)
    width = sz.x_blocks * LANES
    for k, part in enumerate((o0, r1, r2, r3)):
        group = lax.bitwise_xor(place, k)
        at = pl.ds(pl.multiple_of(group * width, LANES), width)
        gate = 0.5 * z[:, at].astype(F32)
        value = part[...].astype(F32) * silu_half(gate)
        mean = jnp.sum(value * value, axis=-1, keepdims=True) * (1.0 / width)
        out[:, at] = (value * lax.rsqrt(mean + 1e-05) * gain[0:1, at]).astype(BF16)


def call(kernel, sz, outs, scratch, specs, name, flops=0, touched=0):
    return pl.pallas_call(
        functools.partial(kernel, sz),
        out_shape=[jax.ShapeDtypeStruct(s, d) for s, d in outs],
        in_specs=specs,
        out_specs=[VMEM] * len(outs),
        scratch_shapes=[s if not isinstance(s, tuple) else pltpu.VMEM(*s) for s in scratch],
        compiler_params=pltpu.CompilerParams(vmem_limit_bytes=24 << 20),
        cost_estimate=pl.CostEstimate(flops=flops, bytes_accessed=touched, transcendentals=0),
        name=name,
    )


def body(x_in, b_in, c_in, z_in, dt_raw, dt_bias, a_log, d_skip, conv_x, conv_b, conv_c, norm_gain):
    seq_total = lax.axis_size("seq")
    sz = Sizes(x_in, b_in, dt_raw, seq_total, conv_x.shape[0])
    n, rows = sz.places, sz.rows
    chain = sz.blocks > 2

    def swap(k):
        return [(i, i - i % n + ((i % n) ^ k)) for i in range(seq_total)]

    def onward(k, wrap):
        pairs = [(i, i + n * k) for i in range(seq_total)]
        return [(i, j % seq_total) for i, j in pairs if wrap or j < seq_total]

    copies = 1 + n * (sz.cols + sz.s_blocks)
    sent = call(
        pack_kernel,
        sz,
        [((sz.message, LANES), BF16)] * n + [((sz.message_c, LANES), BF16)] * n,
        [((sz.heads, rows), BF16), pltpu.SemaphoreType.DMA((copies,))],
        [HBM] * 4,
        "pack",
    )(*(pltpu.with_memory_space_constraint(a, pltpu.HBM) for a in (x_in, b_in, c_in, dt_raw.T)))
    came, came_c = [sent[0]], [sent[n]]
    for k in range(1, n):
        came.append(lax.ppermute(sent[k], "seq", swap(k)))
    for k in range(1, n):
        came_c.append(lax.ppermute(sent[n + k], "seq", swap(k)))

    width = sz.x_blocks * LANES
    padded = BLOCK + HALO
    edge_rows = sz.cols * HALO
    if chain:
        place = lax.rem(lax.axis_index("seq"), n)
        ends = []
        for m in came:
            body_rows = m[: sz.tail_at].reshape(sz.base, rows, LANES)[:, rows - HALO :]
            ends.append(jnp.concatenate([body_rows.reshape(-1, LANES), m[sz.tail_at : sz.dt_at]], axis=0))
        tail = lax.dynamic_index_in_dim(jnp.stack(ends), lax.bitwise_xor(place, n - 1), 0, keepdims=False)
        halo = lax.ppermute(tail, "seq", onward(1, False)).astype(F32)
    else:
        halo = jnp.zeros((8, LANES), F32)

    msg, xc, bc, stats, first = call(
        state_kernel,
        sz,
        [
            ((sz.x_blocks * STATE + edge_rows, LANES), F32 if chain else BF16),
            ((BLOCK, width), BF16),
            ((BLOCK, STATE), BF16),
            ((sz.stat_rows, BLOCK), F32),
            ((sz.base * HALO, LANES), F32),
        ],
        [
            ((padded, width), F32),
            ((padded, STATE), F32),
            ((sz.heads, BLOCK), F32),
            ((n * sz.s_blocks * HALO, LANES), F32),
        ],
        [VMEM] * 9,
        "state",
    )(dt_bias.reshape(1, -1), a_log.reshape(1, -1), *came, conv_x, conv_b, halo)

    if chain:
        cut = sz.x_blocks * STATE
        grown = msg[:cut].reshape(sz.x_blocks, sz.s_blocks, 2, HEAD_DIM, LANES)
        fade = jnp.exp(stats[: sz.per_group, BLOCK - 1]).reshape(sz.x_blocks, 1, 2, 1, 1)
        k = 1
        while k < sz.blocks:
            grown = grown + fade * lax.ppermute(grown, "seq", onward(k, False))
            fade = fade * lax.ppermute(fade, "seq", onward(k, False))
            k *= 2
        msg = jnp.concatenate([grown.reshape(cut, LANES), msg[cut:]], axis=0).astype(BF16)
    arrived = lax.ppermute(msg, "seq", onward(1, True))

    inner, growth, gains, cc, columns, first_c = call(
        inner_kernel,
        sz,
        [
            ((BLOCK, width), F32),
            ((BLOCK, width), F32),
            ((8, width), F32),
            ((BLOCK, STATE), BF16),
            ((EDGE, sz.stat_rows), F32),
            ((sz.s_blocks * HALO, LANES), F32),
        ],
        [((padded, STATE), F32), ((BLOCK, sz.stat_rows), F32)],
        [VMEM] * 10,
        "inner",
        flops=1 << 30,
        touched=1 << 22,
    )(d_skip.reshape(1, -1), *came_c, conv_c, xc, bc, stats, halo)

    back = call(
        outer_kernel,
        sz,
        [((rows, width), BF16)] * 4,
        [
            ((2 * HALO, sz.cols * LANES), F32),
            ((BLOCK, STATE), BF16),
            ((BLOCK, width), F32),
        ],
        [VMEM] * 14,
        "outer",
    )(conv_x, conv_b, conv_c, xc, bc, cc, stats, columns, first, first_c, growth, gains, inner, arrived)
    home = [lax.ppermute(back[k], "seq", swap(k)) for k in range(1, n)]

    out = call(norm_kernel, sz, [(x_in.shape, BF16)], [], [VMEM] * 6, "norm")(
        back[0], *home, z_in, norm_gain.reshape(1, -1)
    )
    return out[0]


def solution(mesh):
    rows, wide = P(("rep", "seq"), "head"), P(None, "head")
    placed = (rows,) * 5 + (P("head"),) * 3 + (wide,) * 3 + (P("head"),)
    return jax.shard_map(body, mesh=mesh, in_specs=placed, out_specs=rows, check_vma=False)
```

```python
import functools

import jax
import jax.numpy as jnp
from jax import lax
from jax.experimental import pallas as pl
from jax.experimental.pallas import tpu as pltpu
from jax.sharding import PartitionSpec as P

HEAD_DIM = 64
STATE = 256
BLOCK = 256
LANES = 128
HALO = 8
EDGE = 16
F32 = jnp.float32
BF16 = jnp.bfloat16
VMEM = pl.BlockSpec(memory_space=pltpu.VMEM)
HBM = pl.BlockSpec(memory_space=pltpu.HBM)
NT = (((1,), (1,)), ((), ()))
TN = (((0,), (0,)), ((), ()))
NN = (((1,), (0,)), ((), ()))


def dot(a, b, dims):
    return lax.dot_general(a, b, dims, preferred_element_type=F32)


class Sizes:
    def __init__(self, x_in, b_in, dt_raw, seq_total, taps):
        self.rows = x_in.shape[0]
        self.heads = dt_raw.shape[1]
        self.groups = b_in.shape[1] // STATE
        self.per_group = self.heads // self.groups
        self.places = BLOCK // self.rows
        self.blocks = seq_total // self.places
        self.taps = taps
        self.x_blocks = self.per_group * HEAD_DIM // LANES
        self.s_blocks = STATE // LANES
        self.base = self.x_blocks + self.s_blocks
        self.cols = self.base + self.s_blocks
        self.message = (self.rows + max(HALO, self.heads), self.base * LANES)
        self.dt_lanes = slice((self.base - 1) * LANES, self.base * LANES)
        self.halo_rows = -(-self.cols * (taps - 1) // 16) * 16
        self.pad_heads = max(8, self.per_group)
        self.stat_rows = 4 * self.per_group
        if self.places != self.groups or self.rows * 2 != LANES or self.places != 4:
            raise ValueError("unsupported shapes")


def lane(start):
    return pl.ds(pl.multiple_of(start, LANES), LANES)


def place_of(sz):
    return lax.rem(lax.axis_index("seq"), sz.places)


def silu_half(half):
    return half + half * jnp.tanh(half)


def lanes_of(array, group, width):
    return array.at[:, pl.ds(pl.multiple_of(group * width, LANES), width)]


def fetch_all(pairs, sem):
    copies = [pltpu.make_async_copy(source, target, sem.at[i]) for i, (source, target) in enumerate(pairs)]
    for copy in copies:
        copy.start()
    return copies


def message_parts(sz, group, x, b, c, m, mc):
    rows, wide = sz.rows, sz.x_blocks * LANES
    tail = lanes_of(c, group, STATE).at[rows - HALO :, :]
    return [
        (lanes_of(x, group, wide), m.at[0:rows, 0:wide]),
        (lanes_of(b, group, STATE), m.at[0:rows, wide:]),
        (tail, m.at[rows : rows + HALO, 0:STATE]),
        (lanes_of(c, group, STATE), mc),
    ]


def pack_kernel(sz, x, b, c, dt, m1, m2, m3, c1, c2, c3, dt_rows, dt_here, sem):
    place = place_of(sz)
    pairs = [(dt, dt_here)]
    for k, m, mc in ((3, m3, c3), (2, m2, c2), (1, m1, c1)):
        pairs += message_parts(sz, lax.bitwise_xor(place, k), x, b, c, m, mc)
    copies = fetch_all(pairs, sem)
    copies[0].wait()
    here = dt_here[...].astype(F32)
    twice = jnp.concatenate([here, here], axis=1)
    spot = lax.broadcasted_iota(jnp.int32, twice.shape, 1)
    mine = lax.div(spot, sz.rows) == lax.rem(place, 2)
    spread = jnp.where(mine, twice, 0.0).astype(BF16)
    dt_rows[...] = spread
    for m in (m1, m2, m3):
        m[sz.rows : sz.rows + sz.heads, sz.dt_lanes] = spread
    for copy in copies[1:]:
        copy.wait()


def own_kernel(sz, x, b, c, conv_x, conv_b, conv_c, bias, alog, skip, dt_rows,
               m0, c0, taps_x, taps_b, taps_c, bias_here, alog_here, skip_here, sem):
    place = place_of(sz)
    pairs = message_parts(sz, place, x, b, c, m0, c0) + [
        (lanes_of(conv_x, place, sz.x_blocks * LANES), taps_x),
        (lanes_of(conv_b, place, STATE), taps_b),
        (lanes_of(conv_c, place, STATE), taps_c),
        (bias, bias_here),
        (alog, alog_here),
        (skip, skip_here),
    ]
    copies = fetch_all(pairs, sem)
    m0[sz.rows : sz.rows + sz.heads, sz.dt_lanes] = dt_rows[...]
    for copy in copies:
        copy.wait()


def conv_block(buffer, count, taps, t):
    n = len(taps)
    first = HALO - (n - 1)
    cols = slice(t * LANES, (t + 1) * LANES)
    total = taps[0] * buffer[first : first + count, cols]
    for i in range(1, n):
        total = total + taps[i] * buffer[first + i : first + i + count, cols]
    return total


def halved_taps(ref, t, n):
    return [0.5 * ref[i : i + 1, t * LANES : (t + 1) * LANES].astype(F32) for i in range(n)]


def gather(sz, buffer, place, base, count, messages):
    for k, m in enumerate(messages):
        source = lax.bitwise_xor(place, k)
        at = pl.ds(pl.multiple_of(HALO + source * sz.rows, 8), sz.rows)
        for t in range(count):
            cols = slice((base + t) * LANES, (base + t + 1) * LANES)
            buffer[at, t * LANES : (t + 1) * LANES] = m[0 : sz.rows, cols].astype(F32)


def of_heads(sz, ref, head0):
    shape = (sz.pad_heads, sz.heads)
    line = lax.broadcasted_iota(jnp.int32, shape, 0)
    spot = lax.broadcasted_iota(jnp.int32, shape, 1)
    row = jnp.broadcast_to(ref[...], shape)
    return jnp.sum(jnp.where(spot == line + head0, row, 0.0), axis=1, keepdims=True)


def state_kernel(sz, bias, alog, m0, m1, m2, m3, taps_x, taps_b, halo,
                 msg, xc, bc, stats, first, xs, bs, dts, tails, packed):
    chain = sz.blocks > 2
    place = place_of(sz)
    messages = (m0, m1, m2, m3)
    dt_at = slice(sz.rows, sz.rows + sz.heads)
    near, far = (
        p[dt_at, sz.dt_lanes].astype(F32) + q[dt_at, sz.dt_lanes].astype(F32)
        for p, q in ((m0, m1), (m2, m3))
    )
    side = lax.div(place, 2)
    dts[:, lane(side * LANES)] = near
    dts[:, lane((1 - side) * LANES)] = far
    head0 = place * sz.per_group
    raw = pltpu.roll(dts[...], lax.rem(sz.heads - head0, sz.heads), 0)[0 : sz.pad_heads]
    raw = raw + of_heads(sz, bias, head0)
    rates = jnp.maximum(raw, 0.0) + jnp.log1p(jnp.exp(-jnp.abs(raw)))
    decays = -jnp.exp(of_heads(sz, alog, head0)) * rates
    high = decays.astype(BF16).astype(F32)
    middle = (decays - high).astype(BF16).astype(F32)
    low = decays - high - middle
    parts = jnp.concatenate([high, middle, low], axis=0).astype(BF16)
    line = lax.broadcasted_iota(jnp.int32, (BLOCK, BLOCK), 0)
    spot = lax.broadcasted_iota(jnp.int32, (BLOCK, BLOCK), 1)
    upto = jnp.where(line <= spot, 1.0, 0.0).astype(BF16)
    sums = dot(parts, upto, NN)
    n = sz.pad_heads
    log_decay = sums[0:n] + sums[n : 2 * n] + sums[2 * n : 3 * n]
    weight = jnp.exp(log_decay[:, BLOCK - 1 : BLOCK] - log_decay) * rates
    g = sz.per_group
    stats[0:g, :] = log_decay[0:g]
    stats[g : 2 * g, :] = rates[0:g]
    stats[2 * g : 3 * g, :] = jnp.exp(log_decay)[0:g]
    stats[3 * g : 4 * g, :] = weight[0:g]
    gather(sz, xs, place, 0, sz.x_blocks, messages)
    gather(sz, bs, place, sz.x_blocks, sz.s_blocks, messages)
    for t in range(sz.base):
        buffer, u = (xs, t) if t < sz.x_blocks else (bs, t - sz.x_blocks)
        cols = slice(u * LANES, (u + 1) * LANES)
        if chain:
            buffer[0:HALO, cols] = halo[t * HALO : (t + 1) * HALO, :]
        else:
            buffer[0:HALO, cols] = jnp.zeros((HALO, LANES), F32)
    for t in range(sz.s_blocks):
        taps = halved_taps(taps_b, t, sz.taps)
        cols = slice(t * LANES, (t + 1) * LANES)
        bc[:, cols] = silu_half(conv_block(bs, BLOCK, taps, t)).astype(BF16)
    states = []
    for t in range(sz.x_blocks):
        taps = halved_taps(taps_x, t, sz.taps)
        cols = slice(t * LANES, (t + 1) * LANES)
        value = silu_half(conv_block(xs, BLOCK, taps, t)).astype(BF16)
        xc[:, cols] = value
        turned = jnp.transpose(value.astype(F32))
        up = turned[0:HEAD_DIM] * weight[2 * t : 2 * t + 1]
        down = turned[HEAD_DIM:LANES] * weight[2 * t + 1 : 2 * t + 2]
        weighted = jnp.concatenate([up, down], axis=0).astype(BF16)
        states.append(dot(weighted, bc[...], NN))
    for t in range(sz.x_blocks):
        for s in range(sz.s_blocks):
            row = (t * sz.s_blocks + s) * LANES
            part = states[t][:, s * LANES : (s + 1) * LANES]
            msg[row : row + LANES, :] = part.astype(msg.dtype)
    base, over = sz.x_blocks * STATE, sz.taps - 1
    for k, m in enumerate(messages):
        source = lax.bitwise_xor(place, k)
        at = pl.ds(pl.multiple_of(source * HALO, 8), HALO)
        tails[at, :] = m[sz.rows : sz.rows + HALO, 0:STATE].astype(F32)
    packed[...] = jnp.zeros(packed.shape, F32)
    for t in range(sz.cols):
        if t < sz.base:
            buffer, u = (xs, t) if t < sz.x_blocks else (bs, t - sz.x_blocks)
            cols = slice(u * LANES, (u + 1) * LANES)
            first[t * HALO : (t + 1) * HALO, :] = buffer[HALO : 2 * HALO, cols]
            last = buffer[BLOCK : BLOCK + HALO, cols]
        else:
            cols = slice((t - sz.base) * LANES, (t - sz.base + 1) * LANES)
            last = tails[(sz.places - 1) * HALO :, cols]
        packed[t * over : (t + 1) * over, :] = last[HALO - over :]
    msg[base:, :] = packed[...].astype(msg.dtype)


def inner_kernel(sz, skip, c0, c1, c2, c3, taps_c, xc, bc, stats, halo,
                 out, growth, gains, cc, columns, first_c, cs, turned):
    chain = sz.blocks > 2
    place = place_of(sz)
    g = sz.per_group
    turned[...] = jnp.transpose(stats[...])
    columns[...] = turned[0:EDGE, :]
    skips = of_heads(sz, skip, place * g)
    gather(sz, cs, place, 0, sz.s_blocks, (c0, c1, c2, c3))
    for t in range(sz.s_blocks):
        cols = slice(t * LANES, (t + 1) * LANES)
        if chain:
            cs[0:HALO, cols] = halo[(sz.base + t) * HALO : (sz.base + t + 1) * HALO, :]
        else:
            cs[0:HALO, cols] = jnp.zeros((HALO, LANES), F32)
        first_c[t * HALO : (t + 1) * HALO, :] = cs[HALO : 2 * HALO, cols]
        taps = halved_taps(taps_c, t, sz.taps)
        cc[:, cols] = silu_half(conv_block(cs, BLOCK, taps, t)).astype(BF16)
    half = BLOCK // 2
    skip_keys = 0 if chain else EDGE
    low_lanes = lax.broadcasted_iota(jnp.int32, (half, LANES), 1) < HEAD_DIM
    for t in range(sz.x_blocks):
        cols = slice(t * LANES, (t + 1) * LANES)
        gains[:, cols] = jnp.where(low_lanes[0:8], skips[2 * t : 2 * t + 1], skips[2 * t + 1 : 2 * t + 2])
    for r in range(2):
        width = half * (r + 1)
        at = slice(r * half, (r + 1) * half)
        scores = dot(cc[at, :], bc[0:width, :], NT)
        line = lax.broadcasted_iota(jnp.int32, (half, width), 0) + r * half
        spot = lax.broadcasted_iota(jnp.int32, (half, width), 1)
        keep = (spot <= line) & (spot >= skip_keys)
        for t in range(sz.x_blocks):
            cols = slice(t * LANES, (t + 1) * LANES)
            sums = []
            for h in (2 * t, 2 * t + 1):
                spread = turned[at, h : h + 1] - stats[h : h + 1, 0:width]
                rate = stats[g + h : g + h + 1, 0:width]
                mixing = scores * jnp.exp(jnp.where(keep, spread, -1e30)) * rate
                sums.append(dot(mixing.astype(BF16), xc[0:width, cols], NN))
            both = jnp.where(low_lanes, sums[0], sums[1])
            out[at, cols] = both + gains[0:1, cols] * xc[at, cols].astype(F32)
            rise = 2 * g + 2 * t
            growth[at, cols] = jnp.where(low_lanes, turned[at, rise : rise + 1], turned[at, rise + 1 : rise + 2])


def outer_kernel(sz, taps_x, taps_b, taps_c, xc, bc, cc, stats, columns, first, first_c, growth, gains,
                 inner, arrived, o0, o1, o2, o3, edge, ahead, c_all, total):
    chain = sz.blocks > 2
    place = place_of(sz)
    later = lax.axis_index("seq") >= sz.places
    g, rows = sz.per_group, sz.rows
    if chain:
        c_all[...] = cc[...]
    else:
        base = sz.x_blocks * STATE
        renewed, over = [], sz.taps - 1
        ahead[...] = jnp.where(later, arrived[base:, :].astype(F32), 0.0)
        for t in range(sz.cols):
            cols = slice(t * LANES, (t + 1) * LANES)
            edge[HALO - over : HALO, cols] = ahead[t * over : (t + 1) * over, :]
            u = t - sz.base
            edge[HALO : 2 * HALO, cols] = (
                first[t * HALO : (t + 1) * HALO, :] if u < 0 else first_c[u * HALO : (u + 1) * HALO, :]
            )
        for t in range(sz.cols):
            which = (t >= sz.x_blocks) + (t >= sz.base)
            u = t - (0, sz.x_blocks, sz.base)[which]
            taps = halved_taps((taps_x, taps_b, taps_c)[which], u, sz.taps)
            fresh = silu_half(conv_block(edge, HALO, taps, t))
            old = (xc, bc, cc)[which][0:EDGE, u * LANES : (u + 1) * LANES].astype(F32)
            renewed.append(jnp.concatenate([fresh, old[HALO:EDGE]], axis=0).astype(BF16))
        for t in range(sz.s_blocks):
            cols = slice(t * LANES, (t + 1) * LANES)
            c_all[EDGE:, cols] = cc[EDGE:, cols]
            c_all[0:EDGE, cols] = renewed[sz.base + t]
        b_edge = jnp.concatenate(renewed[sz.x_blocks : sz.base], axis=1)
        edge_scores = dot(b_edge, c_all[...], NT)
        line = lax.broadcasted_iota(jnp.int32, (EDGE, BLOCK), 0)
        spot = lax.broadcasted_iota(jnp.int32, (EDGE, BLOCK), 1)
        keep = spot >= line
    for t in range(sz.x_blocks):
        cols = slice(t * LANES, (t + 1) * LANES)
        pieces = [
            arrived[(t * sz.s_blocks + s) * LANES : (t * sz.s_blocks + s + 1) * LANES, :]
            for s in range(sz.s_blocks)
        ]
        state = jnp.where(later, jnp.concatenate(pieces, axis=1).astype(F32), 0.0).astype(BF16)
        out = inner[:, cols] + dot(c_all[...], state, NT) * growth[:, cols]
        if not chain:
            mixed, values = [], []
            edge_low = lax.broadcasted_iota(jnp.int32, (EDGE, LANES), 1) < HEAD_DIM
            x_edge = renewed[t].astype(F32)
            for h in (2 * t, 2 * t + 1):
                spread = stats[h : h + 1, :] - columns[:, h : h + 1]
                rate = columns[:, g + h : g + h + 1]
                mixed.append(edge_scores * jnp.exp(jnp.where(keep, spread, -1e30)) * rate)
                mine = edge_low if h == 2 * t else jnp.logical_not(edge_low)
                values.append(jnp.where(mine, x_edge, 0.0))
            mixed = jnp.concatenate(mixed, axis=0).astype(BF16)
            values = jnp.concatenate(values, axis=0).astype(BF16)
            out = out + dot(mixed, values, TN)
            change = gains[0:1, cols] * (x_edge - xc[0:EDGE, cols].astype(F32))
            total[:, cols] = out
            total[0:EDGE, cols] = out[0:EDGE] + change
        else:
            total[:, cols] = out
    for k, o in enumerate((o0, o1, o2, o3)):
        target = lax.bitwise_xor(place, k)
        o[...] = total[pl.ds(pl.multiple_of(target * rows, 8), rows), :].astype(BF16)


def norm_kernel(sz, o0, r1, r2, r3, z, gain, out):
    place = place_of(sz)
    width = sz.x_blocks * LANES
    for k, part in enumerate((o0, r1, r2, r3)):
        group = lax.bitwise_xor(place, k)
        at = pl.ds(pl.multiple_of(group * width, LANES), width)
        gate = 0.5 * z[:, at].astype(F32)
        value = part[...].astype(F32) * silu_half(gate)
        mean = jnp.sum(value * value, axis=-1, keepdims=True) * (1.0 / width)
        out[:, at] = (value * lax.rsqrt(mean + 1e-05) * gain[0:1, at]).astype(BF16)


def call(kernel, sz, outs, scratch, specs, name, flops=0, touched=0):
    return pl.pallas_call(
        functools.partial(kernel, sz),
        out_shape=[jax.ShapeDtypeStruct(s, d) for s, d in outs],
        in_specs=specs,
        out_specs=[VMEM] * len(outs),
        scratch_shapes=[s if not isinstance(s, tuple) else pltpu.VMEM(*s) for s in scratch],
        compiler_params=pltpu.CompilerParams(vmem_limit_bytes=24 << 20),
        cost_estimate=pl.CostEstimate(flops=flops, bytes_accessed=touched, transcendentals=0),
        name=name,
    )


def body(x_in, b_in, c_in, z_in, dt_raw, dt_bias, a_log, d_skip, conv_x, conv_b, conv_c, norm_gain):
    seq_total = lax.axis_size("seq")
    sz = Sizes(x_in, b_in, dt_raw, seq_total, conv_x.shape[0])
    n, rows = sz.places, sz.rows
    chain = sz.blocks > 2

    def swap(k):
        return [(i, i - i % n + ((i % n) ^ k)) for i in range(seq_total)]

    def onward(k, wrap):
        pairs = [(i, i + n * k) for i in range(seq_total)]
        return [(i, j % seq_total) for i, j in pairs if wrap or j < seq_total]

    def stay(*arrays):
        return [pltpu.with_memory_space_constraint(a, pltpu.HBM) for a in arrays]

    width = sz.x_blocks * LANES
    to_c = ((rows, STATE), BF16)
    *sent, dt_rows = call(
        pack_kernel,
        sz,
        [(sz.message, BF16)] * (n - 1) + [to_c] * (n - 1) + [((sz.heads, LANES), BF16)],
        [((sz.heads, rows), BF16), pltpu.SemaphoreType.DMA((1 + 4 * (n - 1),))],
        [HBM] * 4,
        "pack",
    )(*stay(x_in, b_in, c_in, dt_raw.T))
    arrivals = [lax.ppermute(sent[k], "seq", swap(k % (n - 1) + 1)) for k in range(2 * (n - 1))]
    vectors = [v.reshape(1, -1) for v in (dt_bias, a_log, d_skip)]
    m0, c0, taps_x, taps_b, taps_c, bias, alog, skip = call(
        own_kernel,
        sz,
        [(sz.message, BF16), to_c, ((sz.taps, width), BF16)]
        + [((sz.taps, STATE), BF16)] * 2
        + [((1, sz.heads), F32)] * 3,
        [pltpu.SemaphoreType.DMA((10,))],
        [HBM] * 9 + [VMEM],
        "own",
    )(*stay(x_in, b_in, c_in, conv_x, conv_b, conv_c, *vectors), dt_rows)
    came, came_c = [m0, *arrivals[: n - 1]], [c0, *arrivals[n - 1 :]]

    padded = BLOCK + HALO
    edge_rows = sz.halo_rows
    if chain:
        place = lax.rem(lax.axis_index("seq"), n)
        ends = []
        for m in came:
            both = jnp.concatenate([m[rows - HALO : rows], m[rows : rows + HALO, :STATE]], axis=1)
            ends.append(both.reshape(HALO, sz.cols, LANES).swapaxes(0, 1).reshape(-1, LANES))
        tail = lax.dynamic_index_in_dim(jnp.stack(ends), lax.bitwise_xor(place, n - 1), 0, keepdims=False)
        halo = lax.ppermute(tail, "seq", onward(1, False)).astype(F32)
    else:
        halo = jnp.zeros((8, LANES), F32)

    msg, xc, bc, stats, first = call(
        state_kernel,
        sz,
        [
            ((sz.x_blocks * STATE + edge_rows, LANES), F32 if chain else BF16),
            ((BLOCK, width), BF16),
            ((BLOCK, STATE), BF16),
            ((sz.stat_rows, BLOCK), F32),
            ((sz.base * HALO, LANES), F32),
        ],
        [
            ((padded, width), F32),
            ((padded, STATE), F32),
            ((sz.heads, BLOCK), F32),
            ((n * HALO, STATE), F32),
            ((edge_rows, LANES), F32),
        ],
        [VMEM] * 9,
        "state",
    )(bias, alog, *came, taps_x, taps_b, halo)

    if chain:
        cut = sz.x_blocks * STATE
        grown = msg[:cut].reshape(sz.x_blocks, sz.s_blocks, 2, HEAD_DIM, LANES)
        fade = jnp.exp(stats[: sz.per_group, BLOCK - 1]).reshape(sz.x_blocks, 1, 2, 1, 1)
        k = 1
        while k < sz.blocks:
            grown = grown + fade * lax.ppermute(grown, "seq", onward(k, False))
            fade = fade * lax.ppermute(fade, "seq", onward(k, False))
            k *= 2
        msg = jnp.concatenate([grown.reshape(cut, LANES), msg[cut:]], axis=0).astype(BF16)
    arrived = lax.ppermute(msg, "seq", onward(1, True))

    inner, growth, gains, cc, columns, first_c = call(
        inner_kernel,
        sz,
        [
            ((BLOCK, width), F32),
            ((BLOCK, width), F32),
            ((8, width), F32),
            ((BLOCK, STATE), BF16),
            ((EDGE, sz.stat_rows), F32),
            ((sz.s_blocks * HALO, LANES), F32),
        ],
        [((padded, STATE), F32), ((BLOCK, sz.stat_rows), F32)],
        [VMEM] * 10,
        "inner",
        flops=1 << 30,
        touched=1 << 22,
    )(skip, *came_c, taps_c, xc, bc, stats, halo)

    back = call(
        outer_kernel,
        sz,
        [((rows, width), BF16)] * 4,
        [
            ((2 * HALO, sz.cols * LANES), F32),
            ((edge_rows, LANES), F32),
            ((BLOCK, STATE), BF16),
            ((BLOCK, width), F32),
        ],
        [VMEM] * 14,
        "outer",
    )(taps_x, taps_b, taps_c, xc, bc, cc, stats, columns, first, first_c, growth, gains, inner, arrived)
    home = [lax.ppermute(back[k], "seq", swap(k)) for k in range(1, n)]

    out = call(norm_kernel, sz, [(x_in.shape, BF16)], [], [VMEM] * 6, "norm")(
        back[0], *home, z_in, norm_gain.reshape(1, -1)
    )
    return out[0]


def solution(mesh):
    rows, wide = P(("rep", "seq"), "head"), P(None, "head")
    placed = (rows,) * 5 + (P("head"),) * 3 + (wide,) * 3 + (P("head"),)
    return jax.shard_map(body, mesh=mesh, in_specs=placed, out_specs=rows, check_vma=False)
```

```python
import functools

import jax
import jax.numpy as jnp
from jax import lax
from jax.experimental import pallas as pl
from jax.experimental.pallas import tpu as pltpu
from jax.sharding import PartitionSpec as P

HEAD_DIM = 64
STATE = 256
BLOCK = 256
LANES = 128
HALO = 8
EDGE = 16
ORDER = (3, 1, 2)
F32 = jnp.float32
BF16 = jnp.bfloat16
VMEM = pl.BlockSpec(memory_space=pltpu.VMEM)
HBM = pl.BlockSpec(memory_space=pltpu.HBM)
NT = (((1,), (1,)), ((), ()))
TN = (((0,), (0,)), ((), ()))
NN = (((1,), (0,)), ((), ()))


def dot(a, b, dims):
    return lax.dot_general(a, b, dims, preferred_element_type=F32)


class Sizes:
    def __init__(self, x_in, b_in, dt_raw, seq_total, taps):
        self.rows = x_in.shape[0]
        self.heads = dt_raw.shape[1]
        self.groups = b_in.shape[1] // STATE
        self.per_group = self.heads // self.groups
        self.places = BLOCK // self.rows
        self.blocks = seq_total // self.places
        self.taps = taps
        self.x_blocks = self.per_group * HEAD_DIM // LANES
        self.s_blocks = STATE // LANES
        self.base = self.x_blocks + self.s_blocks
        self.cols = self.base + self.s_blocks
        self.message = (self.rows + max(HALO, self.heads), self.base * LANES)
        self.dt_lanes = slice((self.base - 1) * LANES, self.base * LANES)
        self.halo_rows = -(-self.cols * (taps - 1) // 16) * 16
        self.pad_heads = max(8, self.per_group)
        self.stat_rows = 4 * self.per_group
        if self.places != self.groups or self.rows * 2 != LANES or self.places != 4:
            raise ValueError("unsupported shapes")


def lane(start):
    return pl.ds(pl.multiple_of(start, LANES), LANES)


def place_of(sz):
    return lax.rem(lax.axis_index("seq"), sz.places)


def silu_half(half):
    return half + half * jnp.tanh(half)


def lanes_of(array, group, width):
    return array.at[:, pl.ds(pl.multiple_of(group * width, LANES), width)]


def fetch_all(pairs, sem):
    copies = [pltpu.make_async_copy(source, target, sem.at[i]) for i, (source, target) in enumerate(pairs)]
    for copy in copies:
        copy.start()
    return copies


def message_parts(sz, group, x, b, c, m, mc):
    rows, wide = sz.rows, sz.x_blocks * LANES
    tail = lanes_of(c, group, STATE).at[rows - HALO :, :]
    return [
        (lanes_of(x, group, wide), m.at[0:rows, 0:wide]),
        (lanes_of(b, group, STATE), m.at[0:rows, wide:]),
        (tail, m.at[rows : rows + HALO, 0:STATE]),
        (lanes_of(c, group, STATE), mc),
    ]


def pack_kernel(sz, x, b, c, dt, conv_x, conv_b, conv_c, bias, alog, skip,
                m0, m1, m2, m3, c0, c1, c2, c3, taps_x, taps_b, taps_c, bias_here, alog_here, skip_here,
                dt_here, sem):
    place = place_of(sz)
    pairs = [(dt, dt_here)]
    for k, m, mc in ((3, m3, c3), (1, m1, c1), (2, m2, c2), (0, m0, c0)):
        pairs += message_parts(sz, lax.bitwise_xor(place, k), x, b, c, m, mc)
    pairs += [
        (lanes_of(conv_x, place, sz.x_blocks * LANES), taps_x),
        (lanes_of(conv_b, place, STATE), taps_b),
        (lanes_of(conv_c, place, STATE), taps_c),
        (bias, bias_here),
        (alog, alog_here),
        (skip, skip_here),
    ]
    copies = fetch_all(pairs, sem)
    copies[0].wait()
    here = dt_here[...].astype(F32)
    twice = jnp.concatenate([here, here], axis=1)
    spot = lax.broadcasted_iota(jnp.int32, twice.shape, 1)
    mine = lax.div(spot, sz.rows) == lax.rem(place, 2)
    spread = jnp.where(mine, twice, 0.0).astype(BF16)
    for m in (m0, m1, m2, m3):
        m[sz.rows : sz.rows + sz.heads, sz.dt_lanes] = spread
    for copy in copies[1:]:
        copy.wait()


def conv_block(buffer, count, taps, t):
    n = len(taps)
    first = HALO - (n - 1)
    cols = slice(t * LANES, (t + 1) * LANES)
    total = taps[0] * buffer[first : first + count, cols]
    for i in range(1, n):
        total = total + taps[i] * buffer[first + i : first + i + count, cols]
    return total


def halved_taps(ref, t, n):
    return [0.5 * ref[i : i + 1, t * LANES : (t + 1) * LANES].astype(F32) for i in range(n)]


def gather(sz, buffer, place, base, count, messages):
    for k, m in enumerate(messages):
        source = lax.bitwise_xor(place, k)
        at = pl.ds(pl.multiple_of(HALO + source * sz.rows, 8), sz.rows)
        for t in range(count):
            cols = slice((base + t) * LANES, (base + t + 1) * LANES)
            buffer[at, t * LANES : (t + 1) * LANES] = m[0 : sz.rows, cols].astype(F32)


def of_heads(sz, ref, head0):
    shape = (sz.pad_heads, sz.heads)
    line = lax.broadcasted_iota(jnp.int32, shape, 0)
    spot = lax.broadcasted_iota(jnp.int32, shape, 1)
    row = jnp.broadcast_to(ref[...], shape)
    return jnp.sum(jnp.where(spot == line + head0, row, 0.0), axis=1, keepdims=True)


def state_kernel(sz, bias, alog, m0, m3, m1, m2, taps_x, taps_b, halo,
                 msg, xc, bc, stats, first, xs, bs, dts, tails, packed):
    chain = sz.blocks > 2
    place = place_of(sz)
    messages = (m0, m1, m2, m3)
    dt_at = slice(sz.rows, sz.rows + sz.heads)
    near, far = (
        p[dt_at, sz.dt_lanes].astype(F32) + q[dt_at, sz.dt_lanes].astype(F32)
        for p, q in ((m0, m1), (m2, m3))
    )
    side = lax.div(place, 2)
    dts[:, lane(side * LANES)] = near
    dts[:, lane((1 - side) * LANES)] = far
    head0 = place * sz.per_group
    raw = pltpu.roll(dts[...], lax.rem(sz.heads - head0, sz.heads), 0)[0 : sz.pad_heads]
    raw = raw + of_heads(sz, bias, head0)
    rates = jnp.maximum(raw, 0.0) + jnp.log1p(jnp.exp(-jnp.abs(raw)))
    decays = -jnp.exp(of_heads(sz, alog, head0)) * rates
    high = decays.astype(BF16).astype(F32)
    middle = (decays - high).astype(BF16).astype(F32)
    low = decays - high - middle
    parts = jnp.concatenate([high, middle, low], axis=0).astype(BF16)
    line = lax.broadcasted_iota(jnp.int32, (BLOCK, BLOCK), 0)
    spot = lax.broadcasted_iota(jnp.int32, (BLOCK, BLOCK), 1)
    upto = jnp.where(line <= spot, 1.0, 0.0).astype(BF16)
    sums = dot(parts, upto, NN)
    n = sz.pad_heads
    log_decay = sums[0:n] + sums[n : 2 * n] + sums[2 * n : 3 * n]
    weight = jnp.exp(log_decay[:, BLOCK - 1 : BLOCK] - log_decay) * rates
    g = sz.per_group
    stats[0:g, :] = log_decay[0:g]
    stats[g : 2 * g, :] = rates[0:g]
    stats[2 * g : 3 * g, :] = jnp.exp(log_decay)[0:g]
    stats[3 * g : 4 * g, :] = weight[0:g]
    gather(sz, xs, place, 0, sz.x_blocks, messages)
    gather(sz, bs, place, sz.x_blocks, sz.s_blocks, messages)
    for t in range(sz.base):
        buffer, u = (xs, t) if t < sz.x_blocks else (bs, t - sz.x_blocks)
        cols = slice(u * LANES, (u + 1) * LANES)
        if chain:
            buffer[0:HALO, cols] = halo[t * HALO : (t + 1) * HALO, :]
        else:
            buffer[0:HALO, cols] = jnp.zeros((HALO, LANES), F32)
    for t in range(sz.s_blocks):
        taps = halved_taps(taps_b, t, sz.taps)
        cols = slice(t * LANES, (t + 1) * LANES)
        bc[:, cols] = silu_half(conv_block(bs, BLOCK, taps, t)).astype(BF16)
    states = []
    for t in range(sz.x_blocks):
        taps = halved_taps(taps_x, t, sz.taps)
        cols = slice(t * LANES, (t + 1) * LANES)
        value = silu_half(conv_block(xs, BLOCK, taps, t)).astype(BF16)
        xc[:, cols] = value
        turned = jnp.transpose(value.astype(F32))
        up = turned[0:HEAD_DIM] * weight[2 * t : 2 * t + 1]
        down = turned[HEAD_DIM:LANES] * weight[2 * t + 1 : 2 * t + 2]
        weighted = jnp.concatenate([up, down], axis=0).astype(BF16)
        states.append(dot(weighted, bc[...], NN))
    for t in range(sz.x_blocks):
        for s in range(sz.s_blocks):
            row = (t * sz.s_blocks + s) * LANES
            part = states[t][:, s * LANES : (s + 1) * LANES]
            msg[row : row + LANES, :] = part.astype(msg.dtype)
    base, over = sz.x_blocks * STATE, sz.taps - 1
    for k, m in enumerate(messages):
        source = lax.bitwise_xor(place, k)
        at = pl.ds(pl.multiple_of(source * HALO, 8), HALO)
        tails[at, :] = m[sz.rows : sz.rows + HALO, 0:STATE].astype(F32)
    packed[...] = jnp.zeros(packed.shape, F32)
    for t in range(sz.cols):
        if t < sz.base:
            buffer, u = (xs, t) if t < sz.x_blocks else (bs, t - sz.x_blocks)
            cols = slice(u * LANES, (u + 1) * LANES)
            first[t * HALO : (t + 1) * HALO, :] = buffer[HALO : 2 * HALO, cols]
            last = buffer[BLOCK : BLOCK + HALO, cols]
        else:
            cols = slice((t - sz.base) * LANES, (t - sz.base + 1) * LANES)
            last = tails[(sz.places - 1) * HALO :, cols]
        packed[t * over : (t + 1) * over, :] = last[HALO - over :]
    msg[base:, :] = packed[...].astype(msg.dtype)


def inner_kernel(sz, skip, c0, c3, c1, c2, taps_c, xc, bc, stats, halo,
                 out, growth, gains, cc, columns, first_c, cs, turned):
    chain = sz.blocks > 2
    place = place_of(sz)
    g = sz.per_group
    turned[...] = jnp.transpose(stats[...])
    columns[...] = turned[0:EDGE, :]
    skips = of_heads(sz, skip, place * g)
    gather(sz, cs, place, 0, sz.s_blocks, (c0, c1, c2, c3))
    for t in range(sz.s_blocks):
        cols = slice(t * LANES, (t + 1) * LANES)
        if chain:
            cs[0:HALO, cols] = halo[(sz.base + t) * HALO : (sz.base + t + 1) * HALO, :]
        else:
            cs[0:HALO, cols] = jnp.zeros((HALO, LANES), F32)
        first_c[t * HALO : (t + 1) * HALO, :] = cs[HALO : 2 * HALO, cols]
        taps = halved_taps(taps_c, t, sz.taps)
        cc[:, cols] = silu_half(conv_block(cs, BLOCK, taps, t)).astype(BF16)
    half = BLOCK // 2
    skip_keys = 0 if chain else EDGE
    low_lanes = lax.broadcasted_iota(jnp.int32, (half, LANES), 1) < HEAD_DIM
    for t in range(sz.x_blocks):
        cols = slice(t * LANES, (t + 1) * LANES)
        gains[:, cols] = jnp.where(low_lanes[0:8], skips[2 * t : 2 * t + 1], skips[2 * t + 1 : 2 * t + 2])
    for r in range(2):
        width = half * (r + 1)
        at = slice(r * half, (r + 1) * half)
        scores = dot(cc[at, :], bc[0:width, :], NT)
        line = lax.broadcasted_iota(jnp.int32, (half, width), 0) + r * half
        spot = lax.broadcasted_iota(jnp.int32, (half, width), 1)
        keep = (spot <= line) & (spot >= skip_keys)
        for t in range(sz.x_blocks):
            cols = slice(t * LANES, (t + 1) * LANES)
            sums = []
            for h in (2 * t, 2 * t + 1):
                spread = turned[at, h : h + 1] - stats[h : h + 1, 0:width]
                rate = stats[g + h : g + h + 1, 0:width]
                mixing = scores * jnp.exp(jnp.where(keep, spread, -1e30)) * rate
                sums.append(dot(mixing.astype(BF16), xc[0:width, cols], NN))
            both = jnp.where(low_lanes, sums[0], sums[1])
            out[at, cols] = both + gains[0:1, cols] * xc[at, cols].astype(F32)
            rise = 2 * g + 2 * t
            growth[at, cols] = jnp.where(low_lanes, turned[at, rise : rise + 1], turned[at, rise + 1 : rise + 2])


def outer_kernel(sz, taps_x, taps_b, taps_c, xc, bc, cc, stats, columns, first, first_c, growth, gains,
                 inner, arrived, o0, o1, o2, o3, edge, ahead, c_all, total):
    chain = sz.blocks > 2
    place = place_of(sz)
    later = lax.axis_index("seq") >= sz.places
    g, rows = sz.per_group, sz.rows
    if chain:
        c_all[...] = cc[...]
    else:
        base = sz.x_blocks * STATE
        renewed, over = [], sz.taps - 1
        ahead[...] = jnp.where(later, arrived[base:, :].astype(F32), 0.0)
        for t in range(sz.cols):
            cols = slice(t * LANES, (t + 1) * LANES)
            edge[HALO - over : HALO, cols] = ahead[t * over : (t + 1) * over, :]
            u = t - sz.base
            edge[HALO : 2 * HALO, cols] = (
                first[t * HALO : (t + 1) * HALO, :] if u < 0 else first_c[u * HALO : (u + 1) * HALO, :]
            )
        for t in range(sz.cols):
            which = (t >= sz.x_blocks) + (t >= sz.base)
            u = t - (0, sz.x_blocks, sz.base)[which]
            taps = halved_taps((taps_x, taps_b, taps_c)[which], u, sz.taps)
            fresh = silu_half(conv_block(edge, HALO, taps, t))
            old = (xc, bc, cc)[which][0:EDGE, u * LANES : (u + 1) * LANES].astype(F32)
            renewed.append(jnp.concatenate([fresh, old[HALO:EDGE]], axis=0).astype(BF16))
        for t in range(sz.s_blocks):
            cols = slice(t * LANES, (t + 1) * LANES)
            c_all[EDGE:, cols] = cc[EDGE:, cols]
            c_all[0:EDGE, cols] = renewed[sz.base + t]
        b_edge = jnp.concatenate(renewed[sz.x_blocks : sz.base], axis=1)
        edge_scores = dot(b_edge, c_all[...], NT)
        line = lax.broadcasted_iota(jnp.int32, (EDGE, BLOCK), 0)
        spot = lax.broadcasted_iota(jnp.int32, (EDGE, BLOCK), 1)
        keep = spot >= line
    for t in range(sz.x_blocks):
        cols = slice(t * LANES, (t + 1) * LANES)
        pieces = [
            arrived[(t * sz.s_blocks + s) * LANES : (t * sz.s_blocks + s + 1) * LANES, :]
            for s in range(sz.s_blocks)
        ]
        state = jnp.where(later, jnp.concatenate(pieces, axis=1).astype(F32), 0.0).astype(BF16)
        out = inner[:, cols] + dot(c_all[...], state, NT) * growth[:, cols]
        if not chain:
            mixed, values = [], []
            edge_low = lax.broadcasted_iota(jnp.int32, (EDGE, LANES), 1) < HEAD_DIM
            x_edge = renewed[t].astype(F32)
            for h in (2 * t, 2 * t + 1):
                spread = stats[h : h + 1, :] - columns[:, h : h + 1]
                rate = columns[:, g + h : g + h + 1]
                mixed.append(edge_scores * jnp.exp(jnp.where(keep, spread, -1e30)) * rate)
                mine = edge_low if h == 2 * t else jnp.logical_not(edge_low)
                values.append(jnp.where(mine, x_edge, 0.0))
            mixed = jnp.concatenate(mixed, axis=0).astype(BF16)
            values = jnp.concatenate(values, axis=0).astype(BF16)
            out = out + dot(mixed, values, TN)
            change = gains[0:1, cols] * (x_edge - xc[0:EDGE, cols].astype(F32))
            total[:, cols] = out
            total[0:EDGE, cols] = out[0:EDGE] + change
        else:
            total[:, cols] = out
    for k, o in enumerate((o0, o1, o2, o3)):
        target = lax.bitwise_xor(place, k)
        o[...] = total[pl.ds(pl.multiple_of(target * rows, 8), rows), :].astype(BF16)


def norm_kernel(sz, o0, r3, r1, r2, z, gain, out):
    place = place_of(sz)
    width = sz.x_blocks * LANES
    for k, part in enumerate((o0, r1, r2, r3)):
        group = lax.bitwise_xor(place, k)
        at = pl.ds(pl.multiple_of(group * width, LANES), width)
        gate = 0.5 * z[:, at].astype(F32)
        value = part[...].astype(F32) * silu_half(gate)
        mean = jnp.sum(value * value, axis=-1, keepdims=True) * (1.0 / width)
        out[:, at] = (value * lax.rsqrt(mean + 1e-05) * gain[0:1, at]).astype(BF16)


def call(kernel, sz, outs, scratch, specs, name, flops=0, touched=0):
    return pl.pallas_call(
        functools.partial(kernel, sz),
        out_shape=[jax.ShapeDtypeStruct(s, d) for s, d in outs],
        in_specs=specs,
        out_specs=[VMEM] * len(outs),
        scratch_shapes=[s if not isinstance(s, tuple) else pltpu.VMEM(*s) for s in scratch],
        compiler_params=pltpu.CompilerParams(vmem_limit_bytes=24 << 20),
        cost_estimate=pl.CostEstimate(flops=flops, bytes_accessed=touched, transcendentals=0),
        name=name,
    )


def body(x_in, b_in, c_in, z_in, dt_raw, dt_bias, a_log, d_skip, conv_x, conv_b, conv_c, norm_gain):
    seq_total = lax.axis_size("seq")
    sz = Sizes(x_in, b_in, dt_raw, seq_total, conv_x.shape[0])
    n, rows = sz.places, sz.rows
    chain = sz.blocks > 2

    def swap(k):
        return [(i, i - i % n + ((i % n) ^ k)) for i in range(seq_total)]

    def onward(k, wrap):
        pairs = [(i, i + n * k) for i in range(seq_total)]
        return [(i, j % seq_total) for i, j in pairs if wrap or j < seq_total]

    def ordered(arrays):
        return [arrays[0]] + [arrays[k] for k in ORDER]

    def stay(*arrays):
        return [pltpu.with_memory_space_constraint(a, pltpu.HBM) for a in arrays]

    width = sz.x_blocks * LANES
    to_c = ((rows, STATE), BF16)
    vectors = [v.reshape(1, -1) for v in (dt_bias, a_log, d_skip)]
    *sent, taps_x, taps_b, taps_c, bias, alog, skip = call(
        pack_kernel,
        sz,
        [(sz.message, BF16)] * n
        + [to_c] * n
        + [((sz.taps, width), BF16)]
        + [((sz.taps, STATE), BF16)] * 2
        + [((1, sz.heads), F32)] * 3,
        [((sz.heads, rows), BF16), pltpu.SemaphoreType.DMA((7 + 4 * n,))],
        [HBM] * 10,
        "pack",
    )(*stay(x_in, b_in, c_in, dt_raw.T, conv_x, conv_b, conv_c, *vectors))
    arrivals = {}
    for k in ORDER:
        arrivals[k] = lax.ppermute(sent[k], "seq", swap(k))
    for k in ORDER:
        arrivals[n + k] = lax.ppermute(sent[n + k], "seq", swap(k))
    came = [sent[0]] + [arrivals[k] for k in range(1, n)]
    came_c = [sent[n]] + [arrivals[n + k] for k in range(1, n)]

    padded = BLOCK + HALO
    edge_rows = sz.halo_rows
    if chain:
        place = lax.rem(lax.axis_index("seq"), n)
        ends = []
        for m in came:
            both = jnp.concatenate([m[rows - HALO : rows], m[rows : rows + HALO, :STATE]], axis=1)
            ends.append(both.reshape(HALO, sz.cols, LANES).swapaxes(0, 1).reshape(-1, LANES))
        tail = lax.dynamic_index_in_dim(jnp.stack(ends), lax.bitwise_xor(place, n - 1), 0, keepdims=False)
        halo = lax.ppermute(tail, "seq", onward(1, False)).astype(F32)
    else:
        halo = jnp.zeros((8, LANES), F32)

    msg, xc, bc, stats, first = call(
        state_kernel,
        sz,
        [
            ((sz.x_blocks * STATE + edge_rows, LANES), F32 if chain else BF16),
            ((BLOCK, width), BF16),
            ((BLOCK, STATE), BF16),
            ((sz.stat_rows, BLOCK), F32),
            ((sz.base * HALO, LANES), F32),
        ],
        [
            ((padded, width), F32),
            ((padded, STATE), F32),
            ((sz.heads, BLOCK), F32),
            ((n * HALO, STATE), F32),
            ((edge_rows, LANES), F32),
        ],
        [VMEM] * 9,
        "state",
    )(bias, alog, *ordered(came), taps_x, taps_b, halo)

    if chain:
        cut = sz.x_blocks * STATE
        grown = msg[:cut].reshape(sz.x_blocks, sz.s_blocks, 2, HEAD_DIM, LANES)
        fade = jnp.exp(stats[: sz.per_group, BLOCK - 1]).reshape(sz.x_blocks, 1, 2, 1, 1)
        k = 1
        while k < sz.blocks:
            grown = grown + fade * lax.ppermute(grown, "seq", onward(k, False))
            fade = fade * lax.ppermute(fade, "seq", onward(k, False))
            k *= 2
        msg = jnp.concatenate([grown.reshape(cut, LANES), msg[cut:]], axis=0).astype(BF16)
    arrived = lax.ppermute(msg, "seq", onward(1, True))

    inner, growth, gains, cc, columns, first_c = call(
        inner_kernel,
        sz,
        [
            ((BLOCK, width), F32),
            ((BLOCK, width), F32),
            ((8, width), F32),
            ((BLOCK, STATE), BF16),
            ((EDGE, sz.stat_rows), F32),
            ((sz.s_blocks * HALO, LANES), F32),
        ],
        [((padded, STATE), F32), ((BLOCK, sz.stat_rows), F32)],
        [VMEM] * 10,
        "inner",
        flops=1 << 30,
        touched=1 << 22,
    )(skip, *ordered(came_c), taps_c, xc, bc, stats, halo)

    back = call(
        outer_kernel,
        sz,
        [((rows, width), BF16)] * 4,
        [
            ((2 * HALO, sz.cols * LANES), F32),
            ((edge_rows, LANES), F32),
            ((BLOCK, STATE), BF16),
            ((BLOCK, width), F32),
        ],
        [VMEM] * 14,
        "outer",
    )(taps_x, taps_b, taps_c, xc, bc, cc, stats, columns, first, first_c, growth, gains, inner, arrived)
    home = list(back)
    for k in ORDER:
        home[k] = lax.ppermute(back[k], "seq", swap(k))

    out = call(norm_kernel, sz, [(x_in.shape, BF16)], [], [VMEM] * 6, "norm")(
        *ordered(home), z_in, norm_gain.reshape(1, -1)
    )
    return out[0]


def solution(mesh):
    rows, wide = P(("rep", "seq"), "head"), P(None, "head")
    placed = (rows,) * 5 + (P("head"),) * 3 + (wide,) * 3 + (P("head"),)
    return jax.shard_map(body, mesh=mesh, in_specs=placed, out_specs=rows, check_vma=False)
```

```python
import functools

import jax
import jax.numpy as jnp
from jax import lax
from jax.experimental import pallas as pl
from jax.experimental.pallas import tpu as pltpu
from jax.sharding import PartitionSpec as P

HEAD_DIM = 64
STATE = 256
BLOCK = 256
LANES = 128
HALO = 8
EDGE = 16
ORDER = (3, 1, 2)
RETURN = (3, 1, 2)
SPLIT = (1, 2)
F32 = jnp.float32
BF16 = jnp.bfloat16
VMEM = pl.BlockSpec(memory_space=pltpu.VMEM)
HBM = pl.BlockSpec(memory_space=pltpu.HBM)
NT = (((1,), (1,)), ((), ()))
TN = (((0,), (0,)), ((), ()))
NN = (((1,), (0,)), ((), ()))


def dot(a, b, dims):
    return lax.dot_general(a, b, dims, preferred_element_type=F32)


class Sizes:
    def __init__(self, x_in, b_in, dt_raw, seq_total, taps):
        self.rows = x_in.shape[0]
        self.heads = dt_raw.shape[1]
        self.groups = b_in.shape[1] // STATE
        self.per_group = self.heads // self.groups
        self.places = BLOCK // self.rows
        self.blocks = seq_total // self.places
        self.taps = taps
        self.x_blocks = self.per_group * HEAD_DIM // LANES
        self.s_blocks = STATE // LANES
        self.base = self.x_blocks + self.s_blocks
        self.cols = self.base + self.s_blocks
        self.high = self.rows + max(HALO, self.heads)
        self.dt_lanes = slice((self.base - 1) * LANES, self.base * LANES)
        self.halo_rows = -(-self.cols * (taps - 1) // 16) * 16
        self.pad_heads = max(8, self.per_group)
        self.stat_rows = 4 * self.per_group
        if self.places != self.groups or self.rows * 2 != LANES or self.places != 4:
            raise ValueError("unsupported shapes")


def lane(start):
    return pl.ds(pl.multiple_of(start, LANES), LANES)


def place_of(sz):
    return lax.rem(lax.axis_index("seq"), sz.places)


def by_partner(own, others, order):
    return [own] + [others[order.index(k)] for k in range(1, len(order) + 1)]


def silu_half(half):
    return half + half * jnp.tanh(half)


def lanes_of(array, group, width):
    return array.at[:, pl.ds(pl.multiple_of(group * width, LANES), width)]


def fetch_all(pairs, sem):
    copies = [pltpu.make_async_copy(source, target, sem.at[i]) for i, (source, target) in enumerate(pairs)]
    for copy in copies:
        copy.start()
    return copies


def c_part(sz, k, m, extra):
    if k in SPLIT:
        return extra[SPLIT.index(k)]
    return m.at[0 : sz.rows, sz.base * LANES :]


def message_parts(sz, group, x, b, c, m, mc):
    rows, wide = sz.rows, sz.x_blocks * LANES
    tail = lanes_of(c, group, STATE).at[rows - HALO :, :]
    return [
        (lanes_of(x, group, wide), m.at[0:rows, 0:wide]),
        (lanes_of(b, group, STATE), m.at[0:rows, wide : sz.base * LANES]),
        (tail, m.at[rows : rows + HALO, 0:STATE]),
        (lanes_of(c, group, STATE), mc),
    ]


def pack_kernel(sz, x, b, c, dt, conv_x, conv_b, conv_c, bias, alog, skip,
                m0, m1, m2, m3, *rest):
    extra = rest[: len(SPLIT)]
    taps_x, taps_b, taps_c, bias_here, alog_here, skip_here, dt_here, sem = rest[len(SPLIT) :]
    place = place_of(sz)
    pairs = [(dt, dt_here)]
    sent = (m0, m1, m2, m3)
    for k in (*ORDER, 0):
        m = sent[k]
        pairs += message_parts(sz, lax.bitwise_xor(place, k), x, b, c, m, c_part(sz, k, m, extra))
    pairs += [
        (lanes_of(conv_x, place, sz.x_blocks * LANES), taps_x),
        (lanes_of(conv_b, place, STATE), taps_b),
        (lanes_of(conv_c, place, STATE), taps_c),
        (bias, bias_here),
        (alog, alog_here),
        (skip, skip_here),
    ]
    copies = fetch_all(pairs, sem)
    copies[0].wait()
    here = dt_here[...].astype(F32)
    twice = jnp.concatenate([here, here], axis=1)
    spot = lax.broadcasted_iota(jnp.int32, twice.shape, 1)
    mine = lax.div(spot, sz.rows) == lax.rem(place, 2)
    spread = jnp.where(mine, twice, 0.0).astype(BF16)
    for m in (m0, m1, m2, m3):
        m[sz.rows : sz.rows + sz.heads, sz.dt_lanes] = spread
    for copy in copies[1:]:
        copy.wait()


def conv_block(buffer, count, taps, t):
    n = len(taps)
    first = HALO - (n - 1)
    cols = slice(t * LANES, (t + 1) * LANES)
    total = taps[0] * buffer[first : first + count, cols]
    for i in range(1, n):
        total = total + taps[i] * buffer[first + i : first + i + count, cols]
    return total


def halved_taps(ref, t, n):
    return [0.5 * ref[i : i + 1, t * LANES : (t + 1) * LANES].astype(F32) for i in range(n)]


def gather(sz, buffer, place, base, count, messages):
    for k, m in enumerate(messages):
        source = lax.bitwise_xor(place, k)
        at = pl.ds(pl.multiple_of(HALO + source * sz.rows, 8), sz.rows)
        for t in range(count):
            cols = slice((base + t) * LANES, (base + t + 1) * LANES)
            buffer[at, t * LANES : (t + 1) * LANES] = m[0 : sz.rows, cols].astype(F32)


def of_heads(sz, ref, head0):
    shape = (sz.pad_heads, sz.heads)
    line = lax.broadcasted_iota(jnp.int32, shape, 0)
    spot = lax.broadcasted_iota(jnp.int32, shape, 1)
    row = jnp.broadcast_to(ref[...], shape)
    return jnp.sum(jnp.where(spot == line + head0, row, 0.0), axis=1, keepdims=True)


def convolve(sz, bias, alog, messages, taps_x, taps_b, halo, xc, bc, stats, first, xs, bs, dts):
    chain = sz.blocks > 2
    place = place_of(sz)
    m0, m1, m2, m3 = messages
    dt_at = slice(sz.rows, sz.rows + sz.heads)
    near, far = (
        p[dt_at, sz.dt_lanes].astype(F32) + q[dt_at, sz.dt_lanes].astype(F32)
        for p, q in ((m0, m1), (m2, m3))
    )
    side = lax.div(place, 2)
    dts[:, lane(side * LANES)] = near
    dts[:, lane((1 - side) * LANES)] = far
    head0 = place * sz.per_group
    raw = pltpu.roll(dts[...], lax.rem(sz.heads - head0, sz.heads), 0)[0 : sz.pad_heads]
    raw = raw + of_heads(sz, bias, head0)
    rates = jnp.maximum(raw, 0.0) + jnp.log1p(jnp.exp(-jnp.abs(raw)))
    decays = -jnp.exp(of_heads(sz, alog, head0)) * rates
    high = decays.astype(BF16).astype(F32)
    middle = (decays - high).astype(BF16).astype(F32)
    low = decays - high - middle
    parts = jnp.concatenate([high, middle, low], axis=0).astype(BF16)
    line = lax.broadcasted_iota(jnp.int32, (BLOCK, BLOCK), 0)
    spot = lax.broadcasted_iota(jnp.int32, (BLOCK, BLOCK), 1)
    upto = jnp.where(line <= spot, 1.0, 0.0).astype(BF16)
    sums = dot(parts, upto, NN)
    n = sz.pad_heads
    log_decay = sums[0:n] + sums[n : 2 * n] + sums[2 * n : 3 * n]
    weight = jnp.exp(log_decay[:, BLOCK - 1 : BLOCK] - log_decay) * rates
    g = sz.per_group
    stats[0:g, :] = log_decay[0:g]
    stats[g : 2 * g, :] = rates[0:g]
    stats[2 * g : 3 * g, :] = jnp.exp(log_decay)[0:g]
    stats[3 * g : 4 * g, :] = weight[0:g]
    gather(sz, xs, place, 0, sz.x_blocks, messages)
    gather(sz, bs, place, sz.x_blocks, sz.s_blocks, messages)
    for t in range(sz.base):
        buffer, u = (xs, t) if t < sz.x_blocks else (bs, t - sz.x_blocks)
        cols = slice(u * LANES, (u + 1) * LANES)
        if chain:
            buffer[0:HALO, cols] = halo[t * HALO : (t + 1) * HALO, :]
        else:
            buffer[0:HALO, cols] = jnp.zeros((HALO, LANES), F32)
    for t in range(sz.s_blocks):
        taps = halved_taps(taps_b, t, sz.taps)
        cols = slice(t * LANES, (t + 1) * LANES)
        bc[:, cols] = silu_half(conv_block(bs, BLOCK, taps, t)).astype(BF16)
    for t in range(sz.x_blocks):
        taps = halved_taps(taps_x, t, sz.taps)
        cols = slice(t * LANES, (t + 1) * LANES)
        xc[:, cols] = silu_half(conv_block(xs, BLOCK, taps, t)).astype(BF16)
    for t in range(sz.base):
        buffer, u = (xs, t) if t < sz.x_blocks else (bs, t - sz.x_blocks)
        cols = slice(u * LANES, (u + 1) * LANES)
        first[t * HALO : (t + 1) * HALO, :] = buffer[HALO : 2 * HALO, cols]
    return weight


def in_first(sz):
    return lax.axis_index("seq") < sz.places


def in_last(sz):
    return lax.axis_index("seq") >= (sz.blocks - 1) * sz.places


def state_kernel(sz, bias, alog, m0, ma, mb, mc, taps_x, taps_b, halo,
                 msg, xc, bc, stats, first, xs, bs, dts, tails, packed):
    messages = by_partner(m0, (ma, mb, mc), ORDER)

    def work():
        weight = convolve(sz, bias, alog, messages, taps_x, taps_b, halo, xc, bc, stats, first, xs, bs, dts)
        write_state(sz, messages, weight, msg, xc, bc, xs, bs, tails, packed)

    if sz.blocks > 2:
        work()
    else:
        pl.when(jnp.logical_not(in_last(sz)))(work)

        @pl.when(in_last(sz))
        def _():
            msg[...] = jnp.zeros(msg.shape, msg.dtype)


def write_state(sz, messages, weight, msg, xc, bc, xs, bs, tails, packed):
    place = place_of(sz)
    states = []
    for t in range(sz.x_blocks):
        cols = slice(t * LANES, (t + 1) * LANES)
        turned = jnp.transpose(xc[:, cols].astype(F32))
        up = turned[0:HEAD_DIM] * weight[2 * t : 2 * t + 1]
        down = turned[HEAD_DIM:LANES] * weight[2 * t + 1 : 2 * t + 2]
        weighted = jnp.concatenate([up, down], axis=0).astype(BF16)
        states.append(dot(weighted, bc[...], NN))
    for t in range(sz.x_blocks):
        for s in range(sz.s_blocks):
            row = (t * sz.s_blocks + s) * LANES
            part = states[t][:, s * LANES : (s + 1) * LANES]
            msg[row : row + LANES, :] = part.astype(msg.dtype)
    base, over = sz.x_blocks * STATE, sz.taps - 1
    for k, m in enumerate(messages):
        source = lax.bitwise_xor(place, k)
        at = pl.ds(pl.multiple_of(source * HALO, 8), HALO)
        tails[at, :] = m[sz.rows : sz.rows + HALO, 0:STATE].astype(F32)
    packed[...] = jnp.zeros(packed.shape, F32)
    for t in range(sz.cols):
        if t < sz.base:
            buffer, u = (xs, t) if t < sz.x_blocks else (bs, t - sz.x_blocks)
            cols = slice(u * LANES, (u + 1) * LANES)
            last = buffer[BLOCK : BLOCK + HALO, cols]
        else:
            cols = slice((t - sz.base) * LANES, (t - sz.base + 1) * LANES)
            last = tails[(sz.places - 1) * HALO :, cols]
        packed[t * over : (t + 1) * over, :] = last[HALO - over :]
    msg[base:, :] = packed[...].astype(msg.dtype)


def hand_out(sz, total, outs):
    place = place_of(sz)
    for k, o in enumerate(outs):
        target = lax.bitwise_xor(place, k)
        o[...] = total[pl.ds(pl.multiple_of(target * sz.rows, 8), sz.rows), :].astype(BF16)


def inner_kernel(sz, _xc, _bc, _stats, _first, skip, bias, alog, m0, ma, mb, mc, taps_x, taps_b, taps_c, halo, *rest):
    messages = by_partner(m0, (ma, mb, mc), ORDER)
    extra = rest[: len(SPLIT)]
    xc, bc, stats, first, *early, out, growth, gains, cc, columns, first_c, cs, turned, xs, bs, dts = rest[len(SPLIT) :]
    chain = sz.blocks > 2
    if not chain:

        @pl.when(in_last(sz))
        def _():
            convolve(sz, bias, alog, messages, taps_x, taps_b, halo, xc, bc, stats, first, xs, bs, dts)

    place = place_of(sz)
    g = sz.per_group
    turned[...] = jnp.transpose(stats[...])
    columns[...] = turned[0:EDGE, :]
    skips = of_heads(sz, skip, place * g)
    parts = [c_part(sz, k, m, extra) for k, m in enumerate(messages)]
    gather(sz, cs, place, 0, sz.s_blocks, parts)
    for t in range(sz.s_blocks):
        cols = slice(t * LANES, (t + 1) * LANES)
        if chain:
            cs[0:HALO, cols] = halo[(sz.base + t) * HALO : (sz.base + t + 1) * HALO, :]
        else:
            cs[0:HALO, cols] = jnp.zeros((HALO, LANES), F32)
        first_c[t * HALO : (t + 1) * HALO, :] = cs[HALO : 2 * HALO, cols]
        taps = halved_taps(taps_c, t, sz.taps)
        cc[:, cols] = silu_half(conv_block(cs, BLOCK, taps, t)).astype(BF16)
    half = BLOCK // 2
    skip_keys = 0 if chain else jnp.where(in_first(sz), 0, EDGE)
    low_lanes = lax.broadcasted_iota(jnp.int32, (half, LANES), 1) < HEAD_DIM
    for t in range(sz.x_blocks):
        cols = slice(t * LANES, (t + 1) * LANES)
        gains[:, cols] = jnp.where(low_lanes[0:8], skips[2 * t : 2 * t + 1], skips[2 * t + 1 : 2 * t + 2])
    for r in range(2):
        width = half * (r + 1)
        at = slice(r * half, (r + 1) * half)
        scores = dot(cc[at, :], bc[0:width, :], NT)
        line = lax.broadcasted_iota(jnp.int32, (half, width), 0) + r * half
        spot = lax.broadcasted_iota(jnp.int32, (half, width), 1)
        keep = (spot <= line) & (spot >= skip_keys)
        for t in range(sz.x_blocks):
            cols = slice(t * LANES, (t + 1) * LANES)
            sums = []
            for h in (2 * t, 2 * t + 1):
                spread = turned[at, h : h + 1] - stats[h : h + 1, 0:width]
                rate = stats[g + h : g + h + 1, 0:width]
                mixing = scores * jnp.exp(jnp.where(keep, spread, -1e30)) * rate
                sums.append(dot(mixing.astype(BF16), xc[0:width, cols], NN))
            both = jnp.where(low_lanes, sums[0], sums[1])
            out[at, cols] = both + gains[0:1, cols] * xc[at, cols].astype(F32)
            rise = 2 * g + 2 * t
            growth[at, cols] = jnp.where(low_lanes, turned[at, rise : rise + 1], turned[at, rise + 1 : rise + 2])
    hand_out(sz, out, early)


def outer_kernel(sz, taps_x, taps_b, taps_c, xc, bc, cc, stats, columns, first, first_c, growth, gains,
                 inner, arrived, o0, o1, o2, o3, edge, ahead, c_all, total):
    chain = sz.blocks > 2
    place = place_of(sz)
    g = sz.per_group
    if chain:
        c_all[...] = cc[...]
    else:
        base = sz.x_blocks * STATE
        renewed, over = [], sz.taps - 1
        ahead[...] = arrived[base:, :].astype(F32)
        for t in range(sz.cols):
            cols = slice(t * LANES, (t + 1) * LANES)
            edge[HALO - over : HALO, cols] = ahead[t * over : (t + 1) * over, :]
            u = t - sz.base
            edge[HALO : 2 * HALO, cols] = (
                first[t * HALO : (t + 1) * HALO, :] if u < 0 else first_c[u * HALO : (u + 1) * HALO, :]
            )
        for t in range(sz.cols):
            which = (t >= sz.x_blocks) + (t >= sz.base)
            u = t - (0, sz.x_blocks, sz.base)[which]
            taps = halved_taps((taps_x, taps_b, taps_c)[which], u, sz.taps)
            fresh = silu_half(conv_block(edge, HALO, taps, t))
            old = (xc, bc, cc)[which][0:EDGE, u * LANES : (u + 1) * LANES].astype(F32)
            renewed.append(jnp.concatenate([fresh, old[HALO:EDGE]], axis=0).astype(BF16))
        for t in range(sz.s_blocks):
            cols = slice(t * LANES, (t + 1) * LANES)
            c_all[EDGE:, cols] = cc[EDGE:, cols]
            c_all[0:EDGE, cols] = renewed[sz.base + t]
        b_edge = jnp.concatenate(renewed[sz.x_blocks : sz.base], axis=1)
        edge_scores = dot(b_edge, c_all[...], NT)
        line = lax.broadcasted_iota(jnp.int32, (EDGE, BLOCK), 0)
        spot = lax.broadcasted_iota(jnp.int32, (EDGE, BLOCK), 1)
        keep = spot >= line
    for t in range(sz.x_blocks):
        cols = slice(t * LANES, (t + 1) * LANES)
        pieces = [
            arrived[(t * sz.s_blocks + s) * LANES : (t * sz.s_blocks + s + 1) * LANES, :]
            for s in range(sz.s_blocks)
        ]
        state = jnp.concatenate(pieces, axis=1)
        out = inner[:, cols] + dot(c_all[...], state, NT) * growth[:, cols]
        if not chain:
            mixed, values = [], []
            edge_low = lax.broadcasted_iota(jnp.int32, (EDGE, LANES), 1) < HEAD_DIM
            x_edge = renewed[t].astype(F32)
            for h in (2 * t, 2 * t + 1):
                spread = stats[h : h + 1, :] - columns[:, h : h + 1]
                rate = columns[:, g + h : g + h + 1]
                mixed.append(edge_scores * jnp.exp(jnp.where(keep, spread, -1e30)) * rate)
                mine = edge_low if h == 2 * t else jnp.logical_not(edge_low)
                values.append(jnp.where(mine, x_edge, 0.0))
            mixed = jnp.concatenate(mixed, axis=0).astype(BF16)
            values = jnp.concatenate(values, axis=0).astype(BF16)
            out = out + dot(mixed, values, TN)
            change = gains[0:1, cols] * (x_edge - xc[0:EDGE, cols].astype(F32))
            total[:, cols] = out
            total[0:EDGE, cols] = out[0:EDGE] + change
        else:
            total[:, cols] = out
    hand_out(sz, total, (o0, o1, o2, o3))


def norm_kernel(sz, o0, ra, rb, rc, e0, ea, eb, ec, z, gain, out, ready, sem):
    place = place_of(sz)
    width = sz.x_blocks * LANES
    copies = []
    early = by_partner(e0, (ea, eb, ec), RETURN)
    for k, part in enumerate(by_partner(o0, (ra, rb, rc), RETURN)):
        at = pl.ds(pl.multiple_of(lax.bitwise_xor(place, k) * width, LANES), width)
        gate = 0.5 * z[:, at].astype(F32)
        value = jnp.where(in_first(sz), early[k][...], part[...]).astype(F32) * silu_half(gate)
        mean = jnp.sum(value * value, axis=-1, keepdims=True) * (1.0 / width)
        ready[k] = (value * lax.rsqrt(mean + 1e-05) * gain[0:1, at]).astype(BF16)
        copies.append(pltpu.make_async_copy(ready.at[k], out.at[:, at], sem.at[k]))
        copies[-1].start()
    for copy in copies:
        copy.wait()


def call(kernel, sz, outs, scratch, specs, name, flops=0, touched=0, aliases=None, outputs=None):
    return pl.pallas_call(
        functools.partial(kernel, sz),
        out_shape=[jax.ShapeDtypeStruct(s, d) for s, d in outs],
        in_specs=specs,
        out_specs=outputs or [VMEM] * len(outs),
        input_output_aliases=aliases or {},
        scratch_shapes=[s if not isinstance(s, tuple) else pltpu.VMEM(*s) for s in scratch],
        compiler_params=pltpu.CompilerParams(vmem_limit_bytes=24 << 20),
        cost_estimate=pl.CostEstimate(flops=flops, bytes_accessed=touched, transcendentals=0),
        name=name,
    )


def body(x_in, b_in, c_in, z_in, dt_raw, dt_bias, a_log, d_skip, conv_x, conv_b, conv_c, norm_gain):
    seq_total = lax.axis_size("seq")
    sz = Sizes(x_in, b_in, dt_raw, seq_total, conv_x.shape[0])
    n, rows = sz.places, sz.rows
    chain = sz.blocks > 2
    cores = lax.axis_size("head")

    def swap(k, first=0, end=seq_total):
        pairs = []
        for i in range(seq_total):
            for core in range(cores):
                there = (i - i % n + ((i % n) ^ k), core) if first <= i < end else (i, cores - 1 - core)
                pairs.append((i * cores + core, there[0] * cores + there[1]))
        return pairs

    def onward(k, wrap):
        pairs = [(i, i + n * k) for i in range(seq_total)]
        return [(i, j % seq_total) for i, j in pairs if wrap or j < seq_total]

    def ordered(arrays, order):
        return [arrays[0]] + [arrays[k] for k in order]

    def stay(*arrays):
        return [pltpu.with_memory_space_constraint(a, pltpu.HBM) for a in arrays]

    width = sz.x_blocks * LANES
    vectors = [v.reshape(1, -1) for v in (dt_bias, a_log, d_skip)]
    *sent, taps_x, taps_b, taps_c, bias, alog, skip = call(
        pack_kernel,
        sz,
        [((sz.high, (sz.base + (0 if k in SPLIT else sz.s_blocks)) * LANES), BF16) for k in range(n)]
        + [((rows, STATE), BF16)] * len(SPLIT)
        + [((sz.taps, width), BF16)]
        + [((sz.taps, STATE), BF16)] * 2
        + [((1, sz.heads), F32)] * 3,
        [((sz.heads, rows), BF16), pltpu.SemaphoreType.DMA((7 + 4 * n,))],
        [HBM] * 10,
        "pack",
    )(*stay(x_in, b_in, c_in, dt_raw.T, conv_x, conv_b, conv_c, *vectors))
    came = sent[:n]
    for k in ORDER:
        came[k] = lax.ppermute(sent[k], ("seq", "head"), swap(k))
    extra = [lax.ppermute(sent[n + i], ("seq", "head"), swap(k)) for i, k in enumerate(SPLIT)]

    padded = BLOCK + HALO
    edge_rows = sz.halo_rows
    if chain:
        place = lax.rem(lax.axis_index("seq"), n)
        ends = []
        for m in came:
            both = jnp.concatenate([m[rows - HALO : rows, : sz.base * LANES], m[rows : rows + HALO, :STATE]], axis=1)
            ends.append(both.reshape(HALO, sz.cols, LANES).swapaxes(0, 1).reshape(-1, LANES))
        tail = lax.dynamic_index_in_dim(jnp.stack(ends), lax.bitwise_xor(place, n - 1), 0, keepdims=False)
        halo = lax.ppermute(tail, "seq", onward(1, False)).astype(F32)
    else:
        halo = jnp.zeros((8, LANES), F32)

    convolved = [
        ((BLOCK, width), BF16),
        ((BLOCK, STATE), BF16),
        ((sz.stat_rows, BLOCK), F32),
        ((sz.base * HALO, LANES), F32),
    ]
    buffers = [((padded, width), F32), ((padded, STATE), F32), ((sz.heads, BLOCK), F32)]
    msg, *held = call(
        state_kernel,
        sz,
        [((sz.x_blocks * STATE + edge_rows, LANES), F32 if chain else BF16)] + convolved,
        buffers
        + [
            ((n * HALO, STATE), F32),
            ((edge_rows, LANES), F32),
        ],
        [VMEM] * 9,
        "state",
    )(bias, alog, *ordered(came, ORDER), taps_x, taps_b, halo)

    if chain:
        cut = sz.x_blocks * STATE
        grown = msg[:cut].reshape(sz.x_blocks, sz.s_blocks, 2, HEAD_DIM, LANES)
        fade = jnp.exp(held[2][: sz.per_group, BLOCK - 1]).reshape(sz.x_blocks, 1, 2, 1, 1)
        k = 1
        while k < sz.blocks:
            grown = grown + fade * lax.ppermute(grown, "seq", onward(k, False))
            fade = fade * lax.ppermute(fade, "seq", onward(k, False))
            k *= 2
        msg = jnp.concatenate([grown.reshape(cut, LANES), msg[cut:]], axis=0).astype(BF16)
    arrived = lax.ppermute(msg, "seq", onward(1, True))

    pieces = [((rows, width), BF16)] * n
    xc, bc, stats, first, *early, inner, growth, gains, cc, columns, first_c = call(
        inner_kernel,
        sz,
        convolved
        + pieces
        + [
            ((BLOCK, width), F32),
            ((BLOCK, width), F32),
            ((8, width), F32),
            ((BLOCK, STATE), BF16),
            ((EDGE, sz.stat_rows), F32),
            ((sz.s_blocks * HALO, LANES), F32),
        ],
        [((padded, STATE), F32), ((BLOCK, sz.stat_rows), F32)] + buffers,
        [VMEM] * (15 + len(SPLIT)),
        "inner",
        aliases={i: i for i in range(4)},
        flops=1 << 30,
        touched=1 << 22,
    )(*held, skip, bias, alog, *ordered(came, ORDER), taps_x, taps_b, taps_c, halo, *extra)

    for k in RETURN:
        early[k] = lax.ppermute(early[k], ("seq", "head"), swap(k, 0, n))

    back = call(
        outer_kernel,
        sz,
        pieces,
        [
            ((2 * HALO, sz.cols * LANES), F32),
            ((edge_rows, LANES), F32),
            ((BLOCK, STATE), BF16),
            ((BLOCK, width), F32),
        ],
        [VMEM] * 14,
        "outer",
    )(taps_x, taps_b, taps_c, xc, bc, cc, stats, columns, first, first_c, growth, gains, inner, arrived)
    back = list(back)
    for k in RETURN:
        back[k] = lax.ppermute(back[k], ("seq", "head"), swap(k, n))

    out = call(
        norm_kernel,
        sz,
        [(x_in.shape, BF16)],
        [((n, rows, width), BF16), pltpu.SemaphoreType.DMA((n,))],
        [VMEM] * 10,
        "norm",
        outputs=[HBM],
    )(
        *ordered(back, RETURN), *ordered(early, RETURN), z_in, norm_gain.reshape(1, -1)
    )
    return out[0]


def solution(mesh):
    rows, wide = P(("rep", "seq"), "head"), P(None, "head")
    placed = (rows,) * 5 + (P("head"),) * 3 + (wide,) * 3 + (P("head"),)
    return jax.shard_map(body, mesh=mesh, in_specs=placed, out_specs=rows, check_vma=False)
```

```python
import functools

import jax
import jax.numpy as jnp
from jax import lax
from jax.experimental import pallas as pl
from jax.experimental.pallas import tpu as pltpu
from jax.sharding import PartitionSpec as P

HEAD_DIM = 64
STATE = 256
BLOCK = 256
LANES = 128
HALO = 8
EDGE = 16
ORDER = (3, 1, 2)
RETURN = (3, 1, 2)
SPLIT = (1, 2)
F32 = jnp.float32
BF16 = jnp.bfloat16
VMEM = pl.BlockSpec(memory_space=pltpu.VMEM)
HBM = pl.BlockSpec(memory_space=pltpu.HBM)
NT = (((1,), (1,)), ((), ()))
TN = (((0,), (0,)), ((), ()))
NN = (((1,), (0,)), ((), ()))


def dot(a, b, dims):
    return lax.dot_general(a, b, dims, preferred_element_type=F32)


class Sizes:
    def __init__(self, x_in, b_in, dt_raw, seq_total, taps):
        self.rows = x_in.shape[0]
        self.heads = dt_raw.shape[1]
        self.groups = b_in.shape[1] // STATE
        self.per_group = self.heads // self.groups
        self.places = BLOCK // self.rows
        self.blocks = seq_total // self.places
        self.taps = taps
        self.x_blocks = self.per_group * HEAD_DIM // LANES
        self.s_blocks = STATE // LANES
        self.base = self.x_blocks + self.s_blocks
        self.cols = self.base + self.s_blocks
        self.high = self.rows + max(HALO, self.heads)
        self.dt_lanes = slice((self.base - 1) * LANES, self.base * LANES)
        self.halo_rows = -(-self.cols * (taps - 1) // 16) * 16
        self.pad_heads = max(8, self.per_group)
        self.stat_rows = 4 * self.per_group
        self.late = self.places - 1 if self.blocks == 2 else 0
        if self.places != self.groups or self.rows * 2 != LANES or self.places != 4:
            raise ValueError("unsupported shapes")


def lane(start):
    return pl.ds(pl.multiple_of(start, LANES), LANES)


def place_of(sz):
    return lax.rem(lax.axis_index("seq"), sz.places)


def by_partner(own, others, order):
    return [own] + [others[order.index(k)] for k in range(1, len(order) + 1)]


def silu_half(half):
    return half + half * jnp.tanh(half)


def lanes_of(array, group, width):
    return array.at[:, pl.ds(pl.multiple_of(group * width, LANES), width)]


def fetch_all(pairs, sem):
    copies = [pltpu.make_async_copy(source, target, sem.at[i]) for i, (source, target) in enumerate(pairs)]
    for copy in copies:
        copy.start()
    return copies


def c_part(sz, k, m, extra):
    if extra and k in SPLIT:
        return extra[SPLIT.index(k)]
    return m.at[0 : sz.rows, sz.base * LANES :]


def message_parts(sz, group, x, b, c, m, mc):
    rows, wide = sz.rows, sz.x_blocks * LANES
    tail = lanes_of(c, group, STATE).at[rows - HALO :, :]
    return [
        (lanes_of(x, group, wide), m.at[0:rows, 0:wide]),
        (lanes_of(b, group, STATE), m.at[0:rows, wide : sz.base * LANES]),
        (tail, m.at[rows : rows + HALO, 0:STATE]),
        (lanes_of(c, group, STATE), mc),
    ]


def pack_kernel(sz, x, b, c, dt, conv_x, conv_b, conv_c, bias, alog, skip, gain, m0, m1, m2, m3, *rest):
    extra, rest = rest[: len(SPLIT)], rest[len(SPLIT) :]
    late, rest = rest[: sz.late], rest[sz.late :]
    taps_x, taps_b, taps_c, bias_here, alog_here, skip_here, gain_here, dt_here, sem = rest
    place = place_of(sz)
    shared = [
        (dt, dt_here),
        (lanes_of(conv_x, place, sz.x_blocks * LANES), taps_x),
        (lanes_of(conv_b, place, STATE), taps_b),
        (lanes_of(conv_c, place, STATE), taps_c),
        (bias, bias_here),
        (alog, alog_here),
        (skip, skip_here),
        (gain, gain_here),
    ]

    def fill(messages, split):
        pairs = shared[:1]
        for k in (*ORDER, 0):
            m = messages[k]
            part = c_part(sz, k, m, extra if split else None)
            pairs = pairs + message_parts(sz, lax.bitwise_xor(place, k), x, b, c, m, part)
        copies = fetch_all(pairs + shared[1:], sem)
        copies[0].wait()
        here = dt_here[...].astype(F32)
        twice = jnp.concatenate([here, here], axis=1)
        spot = lax.broadcasted_iota(jnp.int32, twice.shape, 1)
        mine = lax.div(spot, sz.rows) == lax.rem(place, 2)
        spread = jnp.where(mine, twice, 0.0).astype(BF16)
        for m in messages:
            m[sz.rows : sz.rows + sz.heads, sz.dt_lanes] = spread
        for copy in copies[1:]:
            copy.wait()

    if sz.late:
        pl.when(in_first(sz))(lambda: fill((m0, m1, m2, m3), True))
        pl.when(in_last(sz))(lambda: fill((m0, *late), False))
    else:
        fill((m0, m1, m2, m3), True)


def conv_block(buffer, count, taps, t):
    n = len(taps)
    first = HALO - (n - 1)
    cols = slice(t * LANES, (t + 1) * LANES)
    total = taps[0] * buffer[first : first + count, cols]
    for i in range(1, n):
        total = total + taps[i] * buffer[first + i : first + i + count, cols]
    return total


def halved_taps(ref, t, n):
    return [0.5 * ref[i : i + 1, t * LANES : (t + 1) * LANES].astype(F32) for i in range(n)]


def gather(sz, buffer, place, base, count, messages):
    for k, m in enumerate(messages):
        source = lax.bitwise_xor(place, k)
        at = pl.ds(pl.multiple_of(HALO + source * sz.rows, 8), sz.rows)
        for t in range(count):
            cols = slice((base + t) * LANES, (base + t + 1) * LANES)
            buffer[at, t * LANES : (t + 1) * LANES] = m[0 : sz.rows, cols].astype(F32)


def of_heads(sz, ref, head0):
    shape = (sz.pad_heads, sz.heads)
    line = lax.broadcasted_iota(jnp.int32, shape, 0)
    spot = lax.broadcasted_iota(jnp.int32, shape, 1)
    row = jnp.broadcast_to(ref[...], shape)
    return jnp.sum(jnp.where(spot == line + head0, row, 0.0), axis=1, keepdims=True)


def convolve(sz, bias, alog, messages, taps_x, taps_b, halo, xc, bc, stats, first, xs, bs, dts):
    chain = sz.blocks > 2
    place = place_of(sz)
    m0, m1, m2, m3 = messages
    dt_at = slice(sz.rows, sz.rows + sz.heads)
    near, far = (
        p[dt_at, sz.dt_lanes].astype(F32) + q[dt_at, sz.dt_lanes].astype(F32)
        for p, q in ((m0, m1), (m2, m3))
    )
    side = lax.div(place, 2)
    dts[:, lane(side * LANES)] = near
    dts[:, lane((1 - side) * LANES)] = far
    head0 = place * sz.per_group
    raw = pltpu.roll(dts[...], lax.rem(sz.heads - head0, sz.heads), 0)[0 : sz.pad_heads]
    raw = raw + of_heads(sz, bias, head0)
    rates = jnp.maximum(raw, 0.0) + jnp.log1p(jnp.exp(-jnp.abs(raw)))
    decays = -jnp.exp(of_heads(sz, alog, head0)) * rates
    high = decays.astype(BF16).astype(F32)
    middle = (decays - high).astype(BF16).astype(F32)
    low = decays - high - middle
    parts = jnp.concatenate([high, middle, low], axis=0).astype(BF16)
    line = lax.broadcasted_iota(jnp.int32, (BLOCK, BLOCK), 0)
    spot = lax.broadcasted_iota(jnp.int32, (BLOCK, BLOCK), 1)
    upto = jnp.where(line <= spot, 1.0, 0.0).astype(BF16)
    sums = dot(parts, upto, NN)
    n = sz.pad_heads
    log_decay = sums[0:n] + sums[n : 2 * n] + sums[2 * n : 3 * n]
    weight = jnp.exp(log_decay[:, BLOCK - 1 : BLOCK] - log_decay) * rates
    g = sz.per_group
    stats[0:g, :] = log_decay[0:g]
    stats[g : 2 * g, :] = rates[0:g]
    stats[2 * g : 3 * g, :] = jnp.exp(log_decay)[0:g]
    stats[3 * g : 4 * g, :] = weight[0:g]
    gather(sz, xs, place, 0, sz.x_blocks, messages)
    gather(sz, bs, place, sz.x_blocks, sz.s_blocks, messages)
    for t in range(sz.base):
        buffer, u = (xs, t) if t < sz.x_blocks else (bs, t - sz.x_blocks)
        cols = slice(u * LANES, (u + 1) * LANES)
        if chain:
            buffer[0:HALO, cols] = halo[t * HALO : (t + 1) * HALO, :]
        else:
            buffer[0:HALO, cols] = jnp.zeros((HALO, LANES), F32)
    for t in range(sz.s_blocks):
        taps = halved_taps(taps_b, t, sz.taps)
        cols = slice(t * LANES, (t + 1) * LANES)
        bc[:, cols] = silu_half(conv_block(bs, BLOCK, taps, t)).astype(BF16)
    for t in range(sz.x_blocks):
        taps = halved_taps(taps_x, t, sz.taps)
        cols = slice(t * LANES, (t + 1) * LANES)
        xc[:, cols] = silu_half(conv_block(xs, BLOCK, taps, t)).astype(BF16)
    for t in range(sz.base):
        buffer, u = (xs, t) if t < sz.x_blocks else (bs, t - sz.x_blocks)
        cols = slice(u * LANES, (u + 1) * LANES)
        first[t * HALO : (t + 1) * HALO, :] = buffer[HALO : 2 * HALO, cols]
    return weight


def in_first(sz):
    return lax.axis_index("seq") < sz.places


def in_last(sz):
    return lax.axis_index("seq") >= (sz.blocks - 1) * sz.places


def state_kernel(sz, bias, alog, m0, ma, mb, mc, taps_x, taps_b, halo,
                 msg, xc, bc, stats, first, xs, bs, dts, tails, packed):
    messages = by_partner(m0, (ma, mb, mc), ORDER)

    def work():
        weight = convolve(sz, bias, alog, messages, taps_x, taps_b, halo, xc, bc, stats, first, xs, bs, dts)
        write_state(sz, messages, weight, msg, xc, bc, xs, bs, tails, packed)

    if not sz.late:
        work()
    else:
        pl.when(jnp.logical_not(in_last(sz)))(work)

        @pl.when(in_last(sz))
        def _():
            msg[...] = jnp.zeros(msg.shape, msg.dtype)


def write_state(sz, messages, weight, msg, xc, bc, xs, bs, tails, packed):
    place = place_of(sz)
    states = []
    for t in range(sz.x_blocks):
        cols = slice(t * LANES, (t + 1) * LANES)
        turned = jnp.transpose(xc[:, cols].astype(F32))
        up = turned[0:HEAD_DIM] * weight[2 * t : 2 * t + 1]
        down = turned[HEAD_DIM:LANES] * weight[2 * t + 1 : 2 * t + 2]
        weighted = jnp.concatenate([up, down], axis=0).astype(BF16)
        states.append(dot(weighted, bc[...], NN))
    for t in range(sz.x_blocks):
        for s in range(sz.s_blocks):
            row = (t * sz.s_blocks + s) * LANES
            part = states[t][:, s * LANES : (s + 1) * LANES]
            msg[row : row + LANES, :] = part.astype(msg.dtype)
    base, over = sz.x_blocks * STATE, sz.taps - 1
    for k, m in enumerate(messages):
        source = lax.bitwise_xor(place, k)
        at = pl.ds(pl.multiple_of(source * HALO, 8), HALO)
        tails[at, :] = m[sz.rows : sz.rows + HALO, 0:STATE].astype(F32)
    packed[...] = jnp.zeros(packed.shape, F32)
    for t in range(sz.cols):
        if t < sz.base:
            buffer, u = (xs, t) if t < sz.x_blocks else (bs, t - sz.x_blocks)
            cols = slice(u * LANES, (u + 1) * LANES)
            last = buffer[BLOCK : BLOCK + HALO, cols]
        else:
            cols = slice((t - sz.base) * LANES, (t - sz.base + 1) * LANES)
            last = tails[(sz.places - 1) * HALO :, cols]
        packed[t * over : (t + 1) * over, :] = last[HALO - over :]
    msg[base:, :] = packed[...].astype(msg.dtype)


def hand_out(sz, total, outs):
    place = place_of(sz)
    for k, o in enumerate(outs):
        target = lax.bitwise_xor(place, k)
        o[...] = total[pl.ds(pl.multiple_of(target * sz.rows, 8), sz.rows), :].astype(BF16)


def inner_kernel(sz, _xc, _bc, _stats, _first, skip, bias, alog, m0, ma, mb, mc, taps_x, taps_b, taps_c, halo, *rest):
    messages = by_partner(m0, (ma, mb, mc), ORDER)
    extra, rest = rest[: len(SPLIT)], rest[len(SPLIT) :]
    late, rest = rest[: sz.late], rest[sz.late :]
    xc, bc, stats, first, *early, out, growth, gains, cc, columns, first_c, cs, turned, xs, bs, dts = rest
    chain = sz.blocks > 2
    place = place_of(sz)

    def gather_c(messages, split):
        parts = [c_part(sz, k, m, extra if split else None) for k, m in enumerate(messages)]
        gather(sz, cs, place, 0, sz.s_blocks, parts)

    if sz.late:
        pl.when(in_first(sz))(lambda: gather_c(messages, True))

        @pl.when(in_last(sz))
        def _():
            late_messages = by_partner(m0, late, ORDER)
            convolve(sz, bias, alog, late_messages, taps_x, taps_b, halo, xc, bc, stats, first, xs, bs, dts)
            gather_c(late_messages, False)
    else:
        gather_c(messages, True)
    g = sz.per_group
    turned[...] = jnp.transpose(stats[...])
    columns[...] = turned[0:EDGE, :]
    skips = of_heads(sz, skip, place * g)
    for t in range(sz.s_blocks):
        cols = slice(t * LANES, (t + 1) * LANES)
        if chain:
            cs[0:HALO, cols] = halo[(sz.base + t) * HALO : (sz.base + t + 1) * HALO, :]
        else:
            cs[0:HALO, cols] = jnp.zeros((HALO, LANES), F32)
        first_c[t * HALO : (t + 1) * HALO, :] = cs[HALO : 2 * HALO, cols]
        taps = halved_taps(taps_c, t, sz.taps)
        cc[:, cols] = silu_half(conv_block(cs, BLOCK, taps, t)).astype(BF16)
    half = BLOCK // 2
    skip_keys = 0 if chain else jnp.where(in_first(sz), 0, EDGE)
    low_lanes = lax.broadcasted_iota(jnp.int32, (half, LANES), 1) < HEAD_DIM
    for t in range(sz.x_blocks):
        cols = slice(t * LANES, (t + 1) * LANES)
        gains[:, cols] = jnp.where(low_lanes[0:8], skips[2 * t : 2 * t + 1], skips[2 * t + 1 : 2 * t + 2])
    for r in range(2):
        width = half * (r + 1)
        at = slice(r * half, (r + 1) * half)
        scores = dot(cc[at, :], bc[0:width, :], NT)
        line = lax.broadcasted_iota(jnp.int32, (half, width), 0) + r * half
        spot = lax.broadcasted_iota(jnp.int32, (half, width), 1)
        keep = (spot <= line) & (spot >= skip_keys)
        for t in range(sz.x_blocks):
            cols = slice(t * LANES, (t + 1) * LANES)
            sums = []
            for h in (2 * t, 2 * t + 1):
                spread = turned[at, h : h + 1] - stats[h : h + 1, 0:width]
                rate = stats[g + h : g + h + 1, 0:width]
                mixing = scores * jnp.exp(jnp.where(keep, spread, -1e30)) * rate
                sums.append(dot(mixing.astype(BF16), xc[0:width, cols], NN))
            both = jnp.where(low_lanes, sums[0], sums[1])
            out[at, cols] = both + gains[0:1, cols] * xc[at, cols].astype(F32)
            rise = 2 * g + 2 * t
            growth[at, cols] = jnp.where(low_lanes, turned[at, rise : rise + 1], turned[at, rise + 1 : rise + 2])
    hand_out(sz, out, early)


def outer_kernel(sz, taps_x, taps_b, taps_c, xc, bc, cc, stats, columns, first, first_c, growth, gains,
                 inner, arrived, o0, o1, o2, o3, edge, ahead, c_all, total):
    chain = sz.blocks > 2
    place = place_of(sz)
    g = sz.per_group
    if chain:
        c_all[...] = cc[...]
    else:
        base = sz.x_blocks * STATE
        renewed, over = [], sz.taps - 1
        ahead[...] = arrived[base:, :].astype(F32)
        for t in range(sz.cols):
            cols = slice(t * LANES, (t + 1) * LANES)
            edge[HALO - over : HALO, cols] = ahead[t * over : (t + 1) * over, :]
            u = t - sz.base
            edge[HALO : 2 * HALO, cols] = (
                first[t * HALO : (t + 1) * HALO, :] if u < 0 else first_c[u * HALO : (u + 1) * HALO, :]
            )
        for t in range(sz.cols):
            which = (t >= sz.x_blocks) + (t >= sz.base)
            u = t - (0, sz.x_blocks, sz.base)[which]
            taps = halved_taps((taps_x, taps_b, taps_c)[which], u, sz.taps)
            fresh = silu_half(conv_block(edge, HALO, taps, t))
            old = (xc, bc, cc)[which][0:EDGE, u * LANES : (u + 1) * LANES].astype(F32)
            renewed.append(jnp.concatenate([fresh, old[HALO:EDGE]], axis=0).astype(BF16))
        for t in range(sz.s_blocks):
            cols = slice(t * LANES, (t + 1) * LANES)
            c_all[EDGE:, cols] = cc[EDGE:, cols]
            c_all[0:EDGE, cols] = renewed[sz.base + t]
        b_edge = jnp.concatenate(renewed[sz.x_blocks : sz.base], axis=1)
        edge_scores = dot(b_edge, c_all[...], NT)
        line = lax.broadcasted_iota(jnp.int32, (EDGE, BLOCK), 0)
        spot = lax.broadcasted_iota(jnp.int32, (EDGE, BLOCK), 1)
        keep = spot >= line
    for t in range(sz.x_blocks):
        cols = slice(t * LANES, (t + 1) * LANES)
        pieces = [
            arrived[(t * sz.s_blocks + s) * LANES : (t * sz.s_blocks + s + 1) * LANES, :]
            for s in range(sz.s_blocks)
        ]
        state = jnp.concatenate(pieces, axis=1)
        out = inner[:, cols] + dot(c_all[...], state, NT) * growth[:, cols]
        if not chain:
            mixed, values = [], []
            edge_low = lax.broadcasted_iota(jnp.int32, (EDGE, LANES), 1) < HEAD_DIM
            x_edge = renewed[t].astype(F32)
            for h in (2 * t, 2 * t + 1):
                spread = stats[h : h + 1, :] - columns[:, h : h + 1]
                rate = columns[:, g + h : g + h + 1]
                mixed.append(edge_scores * jnp.exp(jnp.where(keep, spread, -1e30)) * rate)
                mine = edge_low if h == 2 * t else jnp.logical_not(edge_low)
                values.append(jnp.where(mine, x_edge, 0.0))
            mixed = jnp.concatenate(mixed, axis=0).astype(BF16)
            values = jnp.concatenate(values, axis=0).astype(BF16)
            out = out + dot(mixed, values, TN)
            change = gains[0:1, cols] * (x_edge - xc[0:EDGE, cols].astype(F32))
            total[:, cols] = out
            total[0:EDGE, cols] = out[0:EDGE] + change
        else:
            total[:, cols] = out
    hand_out(sz, total, (o0, o1, o2, o3))


def norm_kernel(sz, o0, ra, rb, rc, e0, ea, eb, ec, z, gain, out, ready, sem):
    place = place_of(sz)
    width = sz.x_blocks * LANES
    copies = []
    early = by_partner(e0, (ea, eb, ec), RETURN)
    for k, part in enumerate(by_partner(o0, (ra, rb, rc), RETURN)):
        at = pl.ds(pl.multiple_of(lax.bitwise_xor(place, k) * width, LANES), width)
        gate = 0.5 * z[:, at].astype(F32)
        value = jnp.where(in_first(sz), early[k][...], part[...]).astype(F32) * silu_half(gate)
        mean = jnp.sum(value * value, axis=-1, keepdims=True) * (1.0 / width)
        ready[k] = (value * lax.rsqrt(mean + 1e-05) * gain[0:1, at]).astype(BF16)
        copies.append(pltpu.make_async_copy(ready.at[k], out.at[:, at], sem.at[k]))
        copies[-1].start()
    for copy in copies:
        copy.wait()


def call(kernel, sz, outs, scratch, specs, name, flops=0, touched=0, aliases=None, outputs=None):
    return pl.pallas_call(
        functools.partial(kernel, sz),
        out_shape=[jax.ShapeDtypeStruct(s, d) for s, d in outs],
        in_specs=specs,
        out_specs=outputs or [VMEM] * len(outs),
        input_output_aliases=aliases or {},
        scratch_shapes=[s if not isinstance(s, tuple) else pltpu.VMEM(*s) for s in scratch],
        compiler_params=pltpu.CompilerParams(vmem_limit_bytes=24 << 20),
        cost_estimate=pl.CostEstimate(flops=flops, bytes_accessed=touched, transcendentals=0),
        name=name,
    )


def body(x_in, b_in, c_in, z_in, dt_raw, dt_bias, a_log, d_skip, conv_x, conv_b, conv_c, norm_gain):
    seq_total = lax.axis_size("seq")
    sz = Sizes(x_in, b_in, dt_raw, seq_total, conv_x.shape[0])
    n, rows = sz.places, sz.rows
    chain = sz.blocks > 2
    cores = lax.axis_size("head")

    def swap(k, first, end):
        pairs = []
        for i in range(seq_total):
            for core in range(cores):
                there = (i - i % n + ((i % n) ^ k), core) if first <= i < end else (i, cores - 1 - core)
                pairs.append((i * cores + core, there[0] * cores + there[1]))
        return pairs

    def send(array, k, first, end):
        return lax.ppermute(array, ("seq", "head"), swap(k, first, end))

    def onward(k, wrap):
        pairs = [(i, i + n * k) for i in range(seq_total)]
        return [(i, j % seq_total) for i, j in pairs if wrap or j < seq_total]

    def ordered(arrays, order):
        return [arrays[0]] + [arrays[k] for k in order]

    def stay(*arrays):
        return [pltpu.with_memory_space_constraint(a, pltpu.HBM) for a in arrays]

    width = sz.x_blocks * LANES
    vectors = [v.reshape(1, -1) for v in (dt_bias, a_log, d_skip, norm_gain)]
    *sent, taps_x, taps_b, taps_c, bias, alog, skip, gain = call(
        pack_kernel,
        sz,
        [((sz.high, (sz.base + (0 if k in SPLIT else sz.s_blocks)) * LANES), BF16) for k in range(n)]
        + [((rows, STATE), BF16)] * len(SPLIT)
        + [((sz.high, sz.cols * LANES), BF16)] * sz.late
        + [((sz.taps, width), BF16)]
        + [((sz.taps, STATE), BF16)] * 2
        + [((1, sz.heads), F32)] * 3
        + [((1, norm_gain.shape[0]), F32)],
        [((sz.heads, rows), BF16), pltpu.SemaphoreType.DMA((8 + 4 * n,))],
        [HBM] * 11,
        "pack",
    )(*stay(x_in, b_in, c_in, dt_raw.T, conv_x, conv_b, conv_c, *vectors))
    came, split = sent[:n], sent[n : n + len(SPLIT)]
    end = n if sz.late else seq_total
    for k in ORDER:
        came[k] = send(came[k], k, 0, end)
    extra = [send(m, k, 0, end) for m, k in zip(split, SPLIT)]
    late = sent[n + len(SPLIT) :]
    late = [send(late[k - 1], k, n, seq_total) for k in ORDER if sz.late]

    padded = BLOCK + HALO
    edge_rows = sz.halo_rows
    if chain:
        place = lax.rem(lax.axis_index("seq"), n)
        ends = []
        for m in came:
            both = jnp.concatenate([m[rows - HALO : rows, : sz.base * LANES], m[rows : rows + HALO, :STATE]], axis=1)
            ends.append(both.reshape(HALO, sz.cols, LANES).swapaxes(0, 1).reshape(-1, LANES))
        tail = lax.dynamic_index_in_dim(jnp.stack(ends), lax.bitwise_xor(place, n - 1), 0, keepdims=False)
        halo = lax.ppermute(tail, "seq", onward(1, False)).astype(F32)
    else:
        halo = jnp.zeros((8, LANES), F32)

    convolved = [
        ((BLOCK, width), BF16),
        ((BLOCK, STATE), BF16),
        ((sz.stat_rows, BLOCK), F32),
        ((sz.base * HALO, LANES), F32),
    ]
    buffers = [((padded, width), F32), ((padded, STATE), F32), ((sz.heads, BLOCK), F32)]
    msg, *held = call(
        state_kernel,
        sz,
        [((sz.x_blocks * STATE + edge_rows, LANES), F32 if chain else BF16)] + convolved,
        buffers
        + [
            ((n * HALO, STATE), F32),
            ((edge_rows, LANES), F32),
        ],
        [VMEM] * 9,
        "state",
    )(bias, alog, *ordered(came, ORDER), taps_x, taps_b, halo)

    if chain:
        cut = sz.x_blocks * STATE
        grown = msg[:cut].reshape(sz.x_blocks, sz.s_blocks, 2, HEAD_DIM, LANES)
        fade = jnp.exp(held[2][: sz.per_group, BLOCK - 1]).reshape(sz.x_blocks, 1, 2, 1, 1)
        k = 1
        while k < sz.blocks:
            grown = grown + fade * lax.ppermute(grown, "seq", onward(k, False))
            fade = fade * lax.ppermute(fade, "seq", onward(k, False))
            k *= 2
        msg = jnp.concatenate([grown.reshape(cut, LANES), msg[cut:]], axis=0).astype(BF16)
    arrived = lax.ppermute(msg, "seq", onward(1, True))

    pieces = [((rows, width), BF16)] * n
    xc, bc, stats, first, *early, inner, growth, gains, cc, columns, first_c = call(
        inner_kernel,
        sz,
        convolved
        + pieces
        + [
            ((BLOCK, width), F32),
            ((BLOCK, width), F32),
            ((8, width), F32),
            ((BLOCK, STATE), BF16),
            ((EDGE, sz.stat_rows), F32),
            ((sz.s_blocks * HALO, LANES), F32),
        ],
        [((padded, STATE), F32), ((BLOCK, sz.stat_rows), F32)] + buffers,
        [VMEM] * (15 + len(SPLIT) + sz.late),
        "inner",
        aliases={i: i for i in range(4)},
        flops=1 << 30,
        touched=1 << 22,
    )(*held, skip, bias, alog, *ordered(came, ORDER), taps_x, taps_b, taps_c, halo, *extra, *late)

    for k in RETURN:
        early[k] = send(early[k], k, 0, n)

    back = call(
        outer_kernel,
        sz,
        pieces,
        [
            ((2 * HALO, sz.cols * LANES), F32),
            ((edge_rows, LANES), F32),
            ((BLOCK, STATE), BF16),
            ((BLOCK, width), F32),
        ],
        [VMEM] * 14,
        "outer",
    )(taps_x, taps_b, taps_c, xc, bc, cc, stats, columns, first, first_c, growth, gains, inner, arrived)
    back = list(back)
    for k in RETURN:
        back[k] = send(back[k], k, n, seq_total)

    out = call(
        norm_kernel,
        sz,
        [(x_in.shape, BF16)],
        [((n, rows, width), BF16), pltpu.SemaphoreType.DMA((n,))],
        [VMEM] * 10,
        "norm",
        outputs=[HBM],
    )(
        *ordered(back, RETURN), *ordered(early, RETURN), z_in, gain
    )
    return out[0]


def solution(mesh):
    rows, wide = P(("rep", "seq"), "head"), P(None, "head")
    placed = (rows,) * 5 + (P("head"),) * 3 + (wide,) * 3 + (P("head"),)
    return jax.shard_map(body, mesh=mesh, in_specs=placed, out_specs=rows, check_vma=False)
```

```python
import functools

import jax
import jax.numpy as jnp
from jax import lax
from jax.experimental import pallas as pl
from jax.experimental.pallas import tpu as pltpu
from jax.sharding import PartitionSpec as P


HEAD_DIM = 64
STATE = 256
BLOCK = 256
LANES = 128
HALO = 8
EDGE = 16
ORDER = (3, 2, 1)
RETURN = (3, 2, 1)
SPLIT = (1,)
F32 = jnp.float32
BF16 = jnp.bfloat16
VMEM = pl.BlockSpec(memory_space=pltpu.VMEM)
HBM = pl.BlockSpec(memory_space=pltpu.HBM)
NT = (((1,), (1,)), ((), ()))
TN = (((0,), (0,)), ((), ()))
NN = (((1,), (0,)), ((), ()))


def dot(a, b, dims):
    return lax.dot_general(a, b, dims, preferred_element_type=F32)


class Sizes:
    def __init__(self, x_in, b_in, dt_raw, seq_total, taps):
        self.rows = x_in.shape[0]
        self.heads = dt_raw.shape[1]
        self.groups = b_in.shape[1] // STATE
        self.per_group = self.heads // self.groups
        self.places = BLOCK // self.rows
        self.blocks = seq_total // self.places
        self.taps = taps
        self.x_blocks = self.per_group * HEAD_DIM // LANES
        self.s_blocks = STATE // LANES
        self.base = self.x_blocks + self.s_blocks
        self.cols = self.base + self.s_blocks
        self.high = self.rows + max(HALO, self.heads)
        self.dt_lanes = slice((self.base - 1) * LANES, self.base * LANES)
        self.halo_rows = -(-self.cols * (taps - 1) // 16) * 16
        self.pad_heads = max(8, self.per_group)
        self.stat_rows = 4 * self.per_group
        self.late = self.places - 1 if self.blocks == 2 else 0
        if self.places != self.groups or self.rows * 2 != LANES or self.places != 4:
            raise ValueError("unsupported shapes")


def lane(start):
    return pl.ds(pl.multiple_of(start, LANES), LANES)


def place_of(sz):
    return lax.rem(lax.axis_index("seq"), sz.places)


def by_partner(own, others, order):
    return [own] + [others[order.index(k)] for k in range(1, len(order) + 1)]


def silu_half(half):
    return half + half * jnp.tanh(half)


def lanes_of(array, group, width):
    return array.at[:, pl.ds(pl.multiple_of(group * width, LANES), width)]


def fetch_all(pairs, sem):
    copies = [pltpu.make_async_copy(source, target, sem.at[i]) for i, (source, target) in enumerate(pairs)]
    for copy in copies:
        copy.start()
    return copies


def c_part(sz, k, m, extra):
    if extra and k in SPLIT:
        return extra[SPLIT.index(k)]
    return m.at[0 : sz.rows, sz.base * LANES :]


def message_parts(sz, group, x, b, c, m, mc):
    rows, wide = sz.rows, sz.x_blocks * LANES
    tail = lanes_of(c, group, STATE).at[rows - HALO :, :]
    return [
        (lanes_of(x, group, wide), m.at[0:rows, 0:wide]),
        (lanes_of(b, group, STATE), m.at[0:rows, wide : sz.base * LANES]),
        (tail, m.at[rows : rows + HALO, 0:STATE]),
        (lanes_of(c, group, STATE), mc),
    ]


def pack_kernel(sz, x, b, c, dt, conv_x, conv_b, conv_c, bias, alog, skip, gain, m0, m1, m2, m3, *rest):
    extra, rest = rest[: len(SPLIT)], rest[len(SPLIT) :]
    late, rest = rest[: sz.late], rest[sz.late :]
    taps_x, taps_b, taps_c, bias_here, alog_here, skip_here, gain_here, dt_here, sem = rest
    place = place_of(sz)
    shared = [
        (dt, dt_here),
        (lanes_of(conv_x, place, sz.x_blocks * LANES), taps_x),
        (lanes_of(conv_b, place, STATE), taps_b),
        (lanes_of(conv_c, place, STATE), taps_c),
        (bias, bias_here),
        (alog, alog_here),
        (skip, skip_here),
        (gain, gain_here),
    ]

    def fill(messages, split):
        pairs = shared[:1]
        for k in (*ORDER, 0):
            m = messages[k]
            part = c_part(sz, k, m, extra if split else None)
            pairs = pairs + message_parts(sz, lax.bitwise_xor(place, k), x, b, c, m, part)
        copies = fetch_all(pairs + shared[1:], sem)
        copies[0].wait()
        here = dt_here[...].astype(F32)
        twice = jnp.concatenate([here, here], axis=1)
        spot = lax.broadcasted_iota(jnp.int32, twice.shape, 1)
        mine = lax.div(spot, sz.rows) == lax.rem(place, 2)
        spread = jnp.where(mine, twice, 0.0).astype(BF16)
        for m in messages:
            m[sz.rows : sz.rows + sz.heads, sz.dt_lanes] = spread
        for copy in copies[1:]:
            copy.wait()

    if sz.late:
        pl.when(in_first(sz))(lambda: fill((m0, m1, m2, m3), True))
        pl.when(in_last(sz))(lambda: fill((m0, *late), False))
    else:
        fill((m0, m1, m2, m3), True)


def conv_block(buffer, count, taps, t):
    n = len(taps)
    first = HALO - (n - 1)
    cols = slice(t * LANES, (t + 1) * LANES)
    total = taps[0] * buffer[first : first + count, cols]
    for i in range(1, n):
        total = total + taps[i] * buffer[first + i : first + i + count, cols]
    return total


def halved_taps(ref, t, n):
    return [0.5 * ref[i : i + 1, t * LANES : (t + 1) * LANES].astype(F32) for i in range(n)]


def gather(sz, buffer, place, base, count, messages):
    for k, m in enumerate(messages):
        source = lax.bitwise_xor(place, k)
        at = pl.ds(pl.multiple_of(HALO + source * sz.rows, 8), sz.rows)
        for t in range(count):
            cols = slice((base + t) * LANES, (base + t + 1) * LANES)
            buffer[at, t * LANES : (t + 1) * LANES] = m[0 : sz.rows, cols].astype(F32)


def of_heads(sz, ref, head0):
    shape = (sz.pad_heads, sz.heads)
    line = lax.broadcasted_iota(jnp.int32, shape, 0)
    spot = lax.broadcasted_iota(jnp.int32, shape, 1)
    row = jnp.broadcast_to(ref[...], shape)
    return jnp.sum(jnp.where(spot == line + head0, row, 0.0), axis=1, keepdims=True)


def convolve(sz, bias, alog, messages, taps_x, taps_b, halo, xc, bc, stats, first, xs, bs, dts):
    chain = sz.blocks > 2
    place = place_of(sz)
    m0, m1, m2, m3 = messages
    dt_at = slice(sz.rows, sz.rows + sz.heads)
    near, far = (
        p[dt_at, sz.dt_lanes].astype(F32) + q[dt_at, sz.dt_lanes].astype(F32)
        for p, q in ((m0, m1), (m2, m3))
    )
    side = lax.div(place, 2)
    dts[:, lane(side * LANES)] = near
    dts[:, lane((1 - side) * LANES)] = far
    head0 = place * sz.per_group
    raw = pltpu.roll(dts[...], lax.rem(sz.heads - head0, sz.heads), 0)[0 : sz.pad_heads]
    raw = raw + of_heads(sz, bias, head0)
    rates = jnp.maximum(raw, 0.0) + jnp.log1p(jnp.exp(-jnp.abs(raw)))
    decays = -jnp.exp(of_heads(sz, alog, head0)) * rates
    high = decays.astype(BF16).astype(F32)
    middle = (decays - high).astype(BF16).astype(F32)
    low = decays - high - middle
    parts = jnp.concatenate([high, middle, low], axis=0).astype(BF16)
    line = lax.broadcasted_iota(jnp.int32, (BLOCK, BLOCK), 0)
    spot = lax.broadcasted_iota(jnp.int32, (BLOCK, BLOCK), 1)
    upto = jnp.where(line <= spot, 1.0, 0.0).astype(BF16)
    sums = dot(parts, upto, NN)
    n = sz.pad_heads
    log_decay = sums[0:n] + sums[n : 2 * n] + sums[2 * n : 3 * n]
    weight = jnp.exp(log_decay[:, BLOCK - 1 : BLOCK] - log_decay) * rates
    g = sz.per_group
    stats[0:g, :] = log_decay[0:g]
    stats[g : 2 * g, :] = rates[0:g]
    stats[2 * g : 3 * g, :] = jnp.exp(log_decay)[0:g]
    stats[3 * g : 4 * g, :] = weight[0:g]
    gather(sz, xs, place, 0, sz.x_blocks, messages)
    gather(sz, bs, place, sz.x_blocks, sz.s_blocks, messages)
    for t in range(sz.base):
        buffer, u = (xs, t) if t < sz.x_blocks else (bs, t - sz.x_blocks)
        cols = slice(u * LANES, (u + 1) * LANES)
        if chain:
            buffer[0:HALO, cols] = halo[t * HALO : (t + 1) * HALO, :]
        else:
            buffer[0:HALO, cols] = jnp.zeros((HALO, LANES), F32)
    for t in range(sz.s_blocks):
        taps = halved_taps(taps_b, t, sz.taps)
        cols = slice(t * LANES, (t + 1) * LANES)
        bc[:, cols] = silu_half(conv_block(bs, BLOCK, taps, t)).astype(BF16)
    for t in range(sz.x_blocks):
        taps = halved_taps(taps_x, t, sz.taps)
        cols = slice(t * LANES, (t + 1) * LANES)
        xc[:, cols] = silu_half(conv_block(xs, BLOCK, taps, t)).astype(BF16)
    for t in range(sz.base):
        buffer, u = (xs, t) if t < sz.x_blocks else (bs, t - sz.x_blocks)
        cols = slice(u * LANES, (u + 1) * LANES)
        first[t * HALO : (t + 1) * HALO, :] = buffer[HALO : 2 * HALO, cols]
    return weight


def in_first(sz):
    return lax.axis_index("seq") < sz.places


def in_last(sz):
    return lax.axis_index("seq") >= (sz.blocks - 1) * sz.places


def state_kernel(sz, bias, alog, m0, ma, mb, mc, taps_x, taps_b, halo,
                 msg, xc, bc, stats, first, xs, bs, dts, tails, packed):
    messages = by_partner(m0, (ma, mb, mc), ORDER)

    def work():
        weight = convolve(sz, bias, alog, messages, taps_x, taps_b, halo, xc, bc, stats, first, xs, bs, dts)
        write_state(sz, messages, weight, msg, xc, bc, xs, bs, tails, packed)

    if not sz.late:
        work()
    else:
        pl.when(jnp.logical_not(in_last(sz)))(work)

        @pl.when(in_last(sz))
        def _():
            msg[...] = jnp.zeros(msg.shape, msg.dtype)


def write_state(sz, messages, weight, msg, xc, bc, xs, bs, tails, packed):
    place = place_of(sz)
    states = []
    for t in range(sz.x_blocks):
        cols = slice(t * LANES, (t + 1) * LANES)
        turned = jnp.transpose(xc[:, cols].astype(F32))
        up = turned[0:HEAD_DIM] * weight[2 * t : 2 * t + 1]
        down = turned[HEAD_DIM:LANES] * weight[2 * t + 1 : 2 * t + 2]
        weighted = jnp.concatenate([up, down], axis=0).astype(BF16)
        states.append(dot(weighted, bc[...], NN))
    for t in range(sz.x_blocks):
        for s in range(sz.s_blocks):
            row = (t * sz.s_blocks + s) * LANES
            part = states[t][:, s * LANES : (s + 1) * LANES]
            msg[row : row + LANES, :] = part.astype(msg.dtype)
    base, over = sz.x_blocks * STATE, sz.taps - 1
    for k, m in enumerate(messages):
        source = lax.bitwise_xor(place, k)
        at = pl.ds(pl.multiple_of(source * HALO, 8), HALO)
        tails[at, :] = m[sz.rows : sz.rows + HALO, 0:STATE].astype(F32)
    packed[...] = jnp.zeros(packed.shape, F32)
    for t in range(sz.cols):
        if t < sz.base:
            buffer, u = (xs, t) if t < sz.x_blocks else (bs, t - sz.x_blocks)
            cols = slice(u * LANES, (u + 1) * LANES)
            last = buffer[BLOCK : BLOCK + HALO, cols]
        else:
            cols = slice((t - sz.base) * LANES, (t - sz.base + 1) * LANES)
            last = tails[(sz.places - 1) * HALO :, cols]
        packed[t * over : (t + 1) * over, :] = last[HALO - over :]
    msg[base:, :] = packed[...].astype(msg.dtype)


def hand_out(sz, total, outs):
    place = place_of(sz)
    for k, o in enumerate(outs):
        target = lax.bitwise_xor(place, k)
        o[...] = total[pl.ds(pl.multiple_of(target * sz.rows, 8), sz.rows), :].astype(BF16)


def inner_kernel(sz, _xc, _bc, _stats, _first, skip, bias, alog, m0, ma, mb, mc, taps_x, taps_b, taps_c, halo, *rest):
    messages = by_partner(m0, (ma, mb, mc), ORDER)
    extra, rest = rest[: len(SPLIT)], rest[len(SPLIT) :]
    late, rest = rest[: sz.late], rest[sz.late :]
    xc, bc, stats, first, *early, out, growth, gains, cc, columns, first_c, cs, turned, xs, bs, dts = rest
    chain = sz.blocks > 2
    place = place_of(sz)

    def gather_c(messages, split):
        parts = [c_part(sz, k, m, extra if split else None) for k, m in enumerate(messages)]
        gather(sz, cs, place, 0, sz.s_blocks, parts)

    if sz.late:
        pl.when(in_first(sz))(lambda: gather_c(messages, True))

        @pl.when(in_last(sz))
        def _():
            late_messages = by_partner(m0, late, ORDER)
            convolve(sz, bias, alog, late_messages, taps_x, taps_b, halo, xc, bc, stats, first, xs, bs, dts)
            gather_c(late_messages, False)
    else:
        gather_c(messages, True)
    g = sz.per_group
    turned[...] = jnp.transpose(stats[...])
    columns[...] = turned[0:EDGE, :]
    skips = of_heads(sz, skip, place * g)
    for t in range(sz.s_blocks):
        cols = slice(t * LANES, (t + 1) * LANES)
        if chain:
            cs[0:HALO, cols] = halo[(sz.base + t) * HALO : (sz.base + t + 1) * HALO, :]
        else:
            cs[0:HALO, cols] = jnp.zeros((HALO, LANES), F32)
        first_c[t * HALO : (t + 1) * HALO, :] = cs[HALO : 2 * HALO, cols]
        taps = halved_taps(taps_c, t, sz.taps)
        cc[:, cols] = silu_half(conv_block(cs, BLOCK, taps, t)).astype(BF16)
    half = BLOCK // 2
    skip_keys = 0 if chain else jnp.where(in_first(sz), 0, EDGE)
    low_lanes = lax.broadcasted_iota(jnp.int32, (half, LANES), 1) < HEAD_DIM
    for t in range(sz.x_blocks):
        cols = slice(t * LANES, (t + 1) * LANES)
        gains[:, cols] = jnp.where(low_lanes[0:8], skips[2 * t : 2 * t + 1], skips[2 * t + 1 : 2 * t + 2])
    for r in range(2):
        width = half * (r + 1)
        at = slice(r * half, (r + 1) * half)
        scores = dot(cc[at, :], bc[0:width, :], NT)
        line = lax.broadcasted_iota(jnp.int32, (half, width), 0) + r * half
        spot = lax.broadcasted_iota(jnp.int32, (half, width), 1)
        keep = (spot <= line) & (spot >= skip_keys)
        for t in range(sz.x_blocks):
            cols = slice(t * LANES, (t + 1) * LANES)
            sums = []
            for h in (2 * t, 2 * t + 1):
                spread = turned[at, h : h + 1] - stats[h : h + 1, 0:width]
                rate = stats[g + h : g + h + 1, 0:width]
                mixing = scores * jnp.exp(jnp.where(keep, spread, -1e30)) * rate
                sums.append(dot(mixing.astype(BF16), xc[0:width, cols], NN))
            both = jnp.where(low_lanes, sums[0], sums[1])
            out[at, cols] = both + gains[0:1, cols] * xc[at, cols].astype(F32)
            rise = 2 * g + 2 * t
            growth[at, cols] = jnp.where(low_lanes, turned[at, rise : rise + 1], turned[at, rise + 1 : rise + 2])
    hand_out(sz, out, early)


def outer_kernel(sz, taps_x, taps_b, taps_c, xc, bc, cc, stats, columns, first, first_c, growth, gains,
                 inner, arrived, o0, o1, o2, o3, edge, ahead, c_all, total):
    chain = sz.blocks > 2
    place = place_of(sz)
    g = sz.per_group
    if chain:
        c_all[...] = cc[...]
    else:
        base = sz.x_blocks * STATE
        renewed, over = [], sz.taps - 1
        ahead[...] = arrived[base:, :].astype(F32)
        for t in range(sz.cols):
            cols = slice(t * LANES, (t + 1) * LANES)
            edge[HALO - over : HALO, cols] = ahead[t * over : (t + 1) * over, :]
            u = t - sz.base
            edge[HALO : 2 * HALO, cols] = (
                first[t * HALO : (t + 1) * HALO, :] if u < 0 else first_c[u * HALO : (u + 1) * HALO, :]
            )
        for t in range(sz.cols):
            which = (t >= sz.x_blocks) + (t >= sz.base)
            u = t - (0, sz.x_blocks, sz.base)[which]
            taps = halved_taps((taps_x, taps_b, taps_c)[which], u, sz.taps)
            fresh = silu_half(conv_block(edge, HALO, taps, t))
            old = (xc, bc, cc)[which][0:EDGE, u * LANES : (u + 1) * LANES].astype(F32)
            renewed.append(jnp.concatenate([fresh, old[HALO:EDGE]], axis=0).astype(BF16))
        for t in range(sz.s_blocks):
            cols = slice(t * LANES, (t + 1) * LANES)
            c_all[EDGE:, cols] = cc[EDGE:, cols]
            c_all[0:EDGE, cols] = renewed[sz.base + t]
        b_edge = jnp.concatenate(renewed[sz.x_blocks : sz.base], axis=1)
        edge_scores = dot(b_edge, c_all[...], NT)
        line = lax.broadcasted_iota(jnp.int32, (EDGE, BLOCK), 0)
        spot = lax.broadcasted_iota(jnp.int32, (EDGE, BLOCK), 1)
        keep = spot >= line
    for t in range(sz.x_blocks):
        cols = slice(t * LANES, (t + 1) * LANES)
        pieces = [
            arrived[(t * sz.s_blocks + s) * LANES : (t * sz.s_blocks + s + 1) * LANES, :]
            for s in range(sz.s_blocks)
        ]
        state = jnp.concatenate(pieces, axis=1)
        out = inner[:, cols] + dot(c_all[...], state, NT) * growth[:, cols]
        if not chain:
            mixed, values = [], []
            edge_low = lax.broadcasted_iota(jnp.int32, (EDGE, LANES), 1) < HEAD_DIM
            x_edge = renewed[t].astype(F32)
            for h in (2 * t, 2 * t + 1):
                spread = stats[h : h + 1, :] - columns[:, h : h + 1]
                rate = columns[:, g + h : g + h + 1]
                mixed.append(edge_scores * jnp.exp(jnp.where(keep, spread, -1e30)) * rate)
                mine = edge_low if h == 2 * t else jnp.logical_not(edge_low)
                values.append(jnp.where(mine, x_edge, 0.0))
            mixed = jnp.concatenate(mixed, axis=0).astype(BF16)
            values = jnp.concatenate(values, axis=0).astype(BF16)
            out = out + dot(mixed, values, TN)
            change = gains[0:1, cols] * (x_edge - xc[0:EDGE, cols].astype(F32))
            total[:, cols] = out
            total[0:EDGE, cols] = out[0:EDGE] + change
        else:
            total[:, cols] = out
    hand_out(sz, total, (o0, o1, o2, o3))


def norm_kernel(sz, o0, ra, rb, rc, e0, ea, eb, ec, z, gain, out, ready, sem):
    place = place_of(sz)
    width = sz.x_blocks * LANES
    copies = []
    early = by_partner(e0, (ea, eb, ec), RETURN)
    for k, part in enumerate(by_partner(o0, (ra, rb, rc), RETURN)):
        at = pl.ds(pl.multiple_of(lax.bitwise_xor(place, k) * width, LANES), width)
        gate = 0.5 * z[:, at].astype(F32)
        value = jnp.where(in_first(sz), early[k][...], part[...]).astype(F32) * silu_half(gate)
        mean = jnp.sum(value * value, axis=-1, keepdims=True) * (1.0 / width)
        ready[k] = (value * lax.rsqrt(mean + 1e-05) * gain[0:1, at]).astype(BF16)
        copies.append(pltpu.make_async_copy(ready.at[k], out.at[:, at], sem.at[k]))
        copies[-1].start()
    for copy in copies:
        copy.wait()


def call(kernel, sz, outs, scratch, specs, flops=0, touched=0, aliases=None, outputs=None):
    return pl.pallas_call(
        functools.partial(kernel, sz),
        out_shape=[jax.ShapeDtypeStruct(s, d) for s, d in outs],
        in_specs=specs,
        out_specs=outputs or [VMEM] * len(outs),
        input_output_aliases=aliases or {},
        scratch_shapes=[s if not isinstance(s, tuple) else pltpu.VMEM(*s) for s in scratch],
        compiler_params=pltpu.CompilerParams(vmem_limit_bytes=24 << 20),
        cost_estimate=pl.CostEstimate(flops=flops, bytes_accessed=touched, transcendentals=0),
    )


def body(x_in, b_in, c_in, z_in, dt_raw, dt_bias, a_log, d_skip, conv_x, conv_b, conv_c, norm_gain):
    seq_total = lax.axis_size("seq")
    sz = Sizes(x_in, b_in, dt_raw, seq_total, conv_x.shape[0])
    n, rows = sz.places, sz.rows
    chain = sz.blocks > 2
    cores = lax.axis_size("head")

    def swap(k, first, end):
        pairs = []
        for i in range(seq_total):
            for core in range(cores):
                there = (i - i % n + ((i % n) ^ k), core) if first <= i < end else (i, cores - 1 - core)
                pairs.append((i * cores + core, there[0] * cores + there[1]))
        return pairs

    def send(array, k, first, end):
        return lax.ppermute(array, ("seq", "head"), swap(k, first, end))

    def onward(k, wrap):
        pairs = [(i, i + n * k) for i in range(seq_total)]
        return [(i, j % seq_total) for i, j in pairs if wrap or j < seq_total]

    def ordered(arrays, order):
        return [arrays[0]] + [arrays[k] for k in order]

    def stay(*arrays):
        return [pltpu.with_memory_space_constraint(a, pltpu.HBM) for a in arrays]

    width = sz.x_blocks * LANES
    vectors = [v.reshape(1, -1) for v in (dt_bias, a_log, d_skip, norm_gain)]
    *sent, taps_x, taps_b, taps_c, bias, alog, skip, gain = call(
        pack_kernel,
        sz,
        [((sz.high, (sz.base + (0 if k in SPLIT else sz.s_blocks)) * LANES), BF16) for k in range(n)]
        + [((rows, STATE), BF16)] * len(SPLIT)
        + [((sz.high, sz.cols * LANES), BF16)] * sz.late
        + [((sz.taps, width), BF16)]
        + [((sz.taps, STATE), BF16)] * 2
        + [((1, sz.heads), F32)] * 3
        + [((1, norm_gain.shape[0]), F32)],
        [((sz.heads, rows), BF16), pltpu.SemaphoreType.DMA((8 + 4 * n,))],
        [HBM] * 11,
    )(*stay(x_in, b_in, c_in, dt_raw.T, conv_x, conv_b, conv_c, *vectors))
    came, split = sent[:n], sent[n : n + len(SPLIT)]
    end = n if sz.late else seq_total
    for k in ORDER:
        came[k] = send(came[k], k, 0, end)
    extra = [send(m, k, 0, end) for m, k in zip(split, SPLIT)]
    late = sent[n + len(SPLIT) :]
    late = [send(late[k - 1], k, n, seq_total) for k in ORDER if sz.late]

    padded = BLOCK + HALO
    edge_rows = sz.halo_rows
    if chain:
        place = lax.rem(lax.axis_index("seq"), n)
        ends = []
        for m in came:
            both = jnp.concatenate([m[rows - HALO : rows, : sz.base * LANES], m[rows : rows + HALO, :STATE]], axis=1)
            ends.append(both.reshape(HALO, sz.cols, LANES).swapaxes(0, 1).reshape(-1, LANES))
        tail = lax.dynamic_index_in_dim(jnp.stack(ends), lax.bitwise_xor(place, n - 1), 0, keepdims=False)
        halo = lax.ppermute(tail, "seq", onward(1, False)).astype(F32)
    else:
        halo = jnp.zeros((8, LANES), F32)

    convolved = [
        ((BLOCK, width), BF16),
        ((BLOCK, STATE), BF16),
        ((sz.stat_rows, BLOCK), F32),
        ((sz.base * HALO, LANES), F32),
    ]
    buffers = [((padded, width), F32), ((padded, STATE), F32), ((sz.heads, BLOCK), F32)]
    msg, *held = call(
        state_kernel,
        sz,
        [((sz.x_blocks * STATE + edge_rows, LANES), F32 if chain else BF16)] + convolved,
        buffers
        + [
            ((n * HALO, STATE), F32),
            ((edge_rows, LANES), F32),
        ],
        [VMEM] * 9,
    )(bias, alog, *ordered(came, ORDER), taps_x, taps_b, halo)

    if chain:
        cut = sz.x_blocks * STATE
        grown = msg[:cut].reshape(sz.x_blocks, sz.s_blocks, 2, HEAD_DIM, LANES)
        fade = jnp.exp(held[2][: sz.per_group, BLOCK - 1]).reshape(sz.x_blocks, 1, 2, 1, 1)
        k = 1
        while k < sz.blocks:
            grown = grown + fade * lax.ppermute(grown, "seq", onward(k, False))
            fade = fade * lax.ppermute(fade, "seq", onward(k, False))
            k *= 2
        msg = jnp.concatenate([grown.reshape(cut, LANES), msg[cut:]], axis=0).astype(BF16)
    arrived = lax.ppermute(msg, "seq", onward(1, True))

    pieces = [((rows, width), BF16)] * n
    xc, bc, stats, first, *early, inner, growth, gains, cc, columns, first_c = call(
        inner_kernel,
        sz,
        convolved
        + pieces
        + [
            ((BLOCK, width), F32),
            ((BLOCK, width), F32),
            ((8, width), F32),
            ((BLOCK, STATE), BF16),
            ((EDGE, sz.stat_rows), F32),
            ((sz.s_blocks * HALO, LANES), F32),
        ],
        [((padded, STATE), F32), ((BLOCK, sz.stat_rows), F32)] + buffers,
        [VMEM] * (15 + len(SPLIT) + sz.late),
        aliases={i: i for i in range(4)},
        flops=1 << 30,
        touched=1 << 22,
    )(*held, skip, bias, alog, *ordered(came, ORDER), taps_x, taps_b, taps_c, halo, *extra, *late)

    for k in RETURN:
        early[k] = send(early[k], k, 0, n)

    back = call(
        outer_kernel,
        sz,
        pieces,
        [
            ((2 * HALO, sz.cols * LANES), F32),
            ((edge_rows, LANES), F32),
            ((BLOCK, STATE), BF16),
            ((BLOCK, width), F32),
        ],
        [VMEM] * 14,
    )(taps_x, taps_b, taps_c, xc, bc, cc, stats, columns, first, first_c, growth, gains, inner, arrived)
    back = list(back)
    for k in RETURN:
        back[k] = send(back[k], k, n, seq_total)

    out = call(
        norm_kernel,
        sz,
        [(x_in.shape, BF16)],
        [((n, rows, width), BF16), pltpu.SemaphoreType.DMA((n,))],
        [VMEM] * 10,
        outputs=[HBM],
    )(
        *ordered(back, RETURN), *ordered(early, RETURN), z_in, gain
    )
    return out[0]


def solution(mesh):
    rows, wide = P(("rep", "seq"), "head"), P(None, "head")
    placed = (rows,) * 5 + (P("head"),) * 3 + (wide,) * 3 + (P("head"),)
    return jax.shard_map(body, mesh=mesh, in_specs=placed, out_specs=rows, check_vma=False)
```

```python
import functools

import jax
import jax.numpy as jnp
from jax import lax
from jax.experimental import pallas as pl
from jax.experimental.pallas import tpu as pltpu
from jax.sharding import PartitionSpec as P


HEAD_DIM = 64
STATE = 256
BLOCK = 256
LANES = 128
HALO = 8
EDGE = 16
ORDER = (3, 2, 1)
RETURN = (3, 2, 1)
SPLIT = (1,)
F32 = jnp.float32
BF16 = jnp.bfloat16
VMEM = pl.BlockSpec(memory_space=pltpu.VMEM)
HBM = pl.BlockSpec(memory_space=pltpu.HBM)
NT = (((1,), (1,)), ((), ()))
TN = (((0,), (0,)), ((), ()))
NN = (((1,), (0,)), ((), ()))


def dot(a, b, dims):
    return lax.dot_general(a, b, dims, preferred_element_type=F32)


class Sizes:
    def __init__(self, x_in, b_in, dt_raw, seq_total, taps):
        self.rows = x_in.shape[0]
        self.heads = dt_raw.shape[1]
        self.groups = b_in.shape[1] // STATE
        self.per_group = self.heads // self.groups
        self.places = BLOCK // self.rows
        self.blocks = seq_total // self.places
        self.taps = taps
        self.x_blocks = self.per_group * HEAD_DIM // LANES
        self.s_blocks = STATE // LANES
        self.base = self.x_blocks + self.s_blocks
        self.cols = self.base + self.s_blocks
        self.halo_rows = -(-self.cols * (taps - 1) // 16) * 16
        self.pad_heads = max(8, self.per_group)
        self.stat_rows = 4 * self.per_group
        self.late = self.places - 1 if self.blocks == 2 else 0
        if self.places != self.groups or self.rows * 2 != LANES or self.places != 4:
            raise ValueError("unsupported shapes")


def lane(start):
    return pl.ds(pl.multiple_of(start, LANES), LANES)


def place_of(sz):
    return lax.rem(lax.axis_index("seq"), sz.places)


def by_partner(own, others, order):
    return [own] + [others[order.index(k)] for k in range(1, len(order) + 1)]


def silu_half(half):
    return half + half * jnp.tanh(half)


def lanes_of(array, group, width):
    return array.at[:, pl.ds(pl.multiple_of(group * width, LANES), width)]


def layout(sz, k, apart):
    c_high = HALO if apart and k in SPLIT else sz.rows
    starts = [t * sz.rows for t in range(sz.base)] + [sz.base * sz.rows + u * c_high for u in range(sz.s_blocks)]
    end = starts[-1] + c_high
    return starts, end, end + sz.heads


def tail_rows(sz, k, t):
    starts, _, _ = layout(sz, k, True)
    last = starts[t] + (HALO if t >= sz.base and k in SPLIT else sz.rows)
    return slice(last - HALO, last)


def fetch_all(pairs, sem):
    copies = [pltpu.make_async_copy(source, target, sem.at[i]) for i, (source, target) in enumerate(pairs)]
    for copy in copies:
        copy.start()
    return copies


def message_parts(sz, k, group, x, b, c, m, extra):
    rows, apart = sz.rows, extra is not None
    starts, _, _ = layout(sz, k, apart)
    pairs = []
    for t in range(sz.cols):
        which = (t >= sz.x_blocks) + (t >= sz.base)
        u = t - (0, sz.x_blocks, sz.base)[which]
        first = group * (sz.x_blocks, sz.s_blocks, sz.s_blocks)[which] + u
        source = (x, b, c)[which].at[:, lane(first * LANES)]
        if which == 2 and apart and k in SPLIT:
            pairs.append((source, extra[SPLIT.index(k)].at[u * rows : (u + 1) * rows, :]))
            pairs.append((source.at[rows - HALO :, :], m.at[starts[t] : starts[t] + HALO, :]))
        else:
            pairs.append((source, m.at[starts[t] : starts[t] + rows, :]))
    return pairs


def pack_kernel(sz, x, b, c, dt, conv_x, conv_b, conv_c, bias, alog, skip, gain, m0, m1, m2, m3, *rest):
    extra, rest = rest[: len(SPLIT)], rest[len(SPLIT) :]
    late, rest = rest[: sz.late], rest[sz.late :]
    taps_x, taps_b, taps_c, bias_here, alog_here, skip_here, gain_here, dt_here, sem = rest
    place = place_of(sz)
    shared = [
        (dt, dt_here),
        (lanes_of(conv_x, place, sz.x_blocks * LANES), taps_x),
        (lanes_of(conv_b, place, STATE), taps_b),
        (lanes_of(conv_c, place, STATE), taps_c),
        (bias, bias_here),
        (alog, alog_here),
        (skip, skip_here),
        (gain, gain_here),
    ]

    def fill(messages, split):
        pairs = shared[:1]
        for k in (*ORDER, 0):
            m = messages[k]
            group = lax.bitwise_xor(place, k)
            pairs = pairs + message_parts(sz, k, group, x, b, c, m, extra if split else None)
        copies = fetch_all(pairs + shared[1:], sem)
        copies[0].wait()
        here = dt_here[...].astype(F32)
        twice = jnp.concatenate([here, here], axis=1)
        spot = lax.broadcasted_iota(jnp.int32, twice.shape, 1)
        mine = lax.div(spot, sz.rows) == lax.rem(place, 2)
        spread = jnp.where(mine, twice, 0.0).astype(BF16)
        for k, m in enumerate(messages):
            m[layout(sz, k, split)[1] :, :] = spread
        for copy in copies[1:]:
            copy.wait()

    if sz.late:
        pl.when(in_first(sz))(lambda: fill((m0, m1, m2, m3), True))
        pl.when(in_last(sz))(lambda: fill((m0, *late), False))
    else:
        fill((m0, m1, m2, m3), True)


def conv_block(buffer, count, taps, t):
    n = len(taps)
    first = HALO - (n - 1)
    cols = slice(t * LANES, (t + 1) * LANES)
    total = taps[0] * buffer[first : first + count, cols]
    for i in range(1, n):
        total = total + taps[i] * buffer[first + i : first + i + count, cols]
    return total


def halved_taps(ref, t, n):
    return [0.5 * ref[i : i + 1, t * LANES : (t + 1) * LANES].astype(F32) for i in range(n)]


def gather(sz, buffer, place, messages, starts):
    for k, m in enumerate(messages):
        source = lax.bitwise_xor(place, k)
        at = pl.ds(pl.multiple_of(HALO + source * sz.rows, 8), sz.rows)
        for t, row in enumerate(starts[k]):
            buffer[at, t * LANES : (t + 1) * LANES] = m[row : row + sz.rows, :].astype(F32)


def of_heads(sz, ref, head0):
    shape = (sz.pad_heads, sz.heads)
    line = lax.broadcasted_iota(jnp.int32, shape, 0)
    spot = lax.broadcasted_iota(jnp.int32, shape, 1)
    row = jnp.broadcast_to(ref[...], shape)
    return jnp.sum(jnp.where(spot == line + head0, row, 0.0), axis=1, keepdims=True)


def convolve(sz, bias, alog, messages, taps_x, taps_b, halo, xc, bc, stats, first, xs, bs, dts, apart):
    chain = sz.blocks > 2
    place = place_of(sz)
    places = [layout(sz, k, apart) for k in range(sz.places)]
    logits = [m[at[1] :, :].astype(F32) for m, at in zip(messages, places)]
    near, far = logits[0] + logits[1], logits[2] + logits[3]
    side = lax.div(place, 2)
    dts[:, lane(side * LANES)] = near
    dts[:, lane((1 - side) * LANES)] = far
    head0 = place * sz.per_group
    raw = pltpu.roll(dts[...], lax.rem(sz.heads - head0, sz.heads), 0)[0 : sz.pad_heads]
    raw = raw + of_heads(sz, bias, head0)
    rates = jnp.maximum(raw, 0.0) + jnp.log1p(jnp.exp(-jnp.abs(raw)))
    decays = -jnp.exp(of_heads(sz, alog, head0)) * rates
    high = decays.astype(BF16).astype(F32)
    middle = (decays - high).astype(BF16).astype(F32)
    low = decays - high - middle
    parts = jnp.concatenate([high, middle, low], axis=0).astype(BF16)
    line = lax.broadcasted_iota(jnp.int32, (BLOCK, BLOCK), 0)
    spot = lax.broadcasted_iota(jnp.int32, (BLOCK, BLOCK), 1)
    upto = jnp.where(line <= spot, 1.0, 0.0).astype(BF16)
    sums = dot(parts, upto, NN)
    n = sz.pad_heads
    log_decay = sums[0:n] + sums[n : 2 * n] + sums[2 * n : 3 * n]
    weight = jnp.exp(log_decay[:, BLOCK - 1 : BLOCK] - log_decay) * rates
    g = sz.per_group
    stats[0:g, :] = log_decay[0:g]
    stats[g : 2 * g, :] = rates[0:g]
    stats[2 * g : 3 * g, :] = jnp.exp(log_decay)[0:g]
    stats[3 * g : 4 * g, :] = weight[0:g]
    gather(sz, xs, place, messages, [at[0][: sz.x_blocks] for at in places])
    gather(sz, bs, place, messages, [at[0][sz.x_blocks : sz.base] for at in places])
    for t in range(sz.base):
        buffer, u = (xs, t) if t < sz.x_blocks else (bs, t - sz.x_blocks)
        cols = slice(u * LANES, (u + 1) * LANES)
        if chain:
            buffer[0:HALO, cols] = halo[t * HALO : (t + 1) * HALO, :]
        else:
            buffer[0:HALO, cols] = jnp.zeros((HALO, LANES), F32)
    for t in range(sz.s_blocks):
        taps = halved_taps(taps_b, t, sz.taps)
        cols = slice(t * LANES, (t + 1) * LANES)
        bc[:, cols] = silu_half(conv_block(bs, BLOCK, taps, t)).astype(BF16)
    for t in range(sz.x_blocks):
        taps = halved_taps(taps_x, t, sz.taps)
        cols = slice(t * LANES, (t + 1) * LANES)
        xc[:, cols] = silu_half(conv_block(xs, BLOCK, taps, t)).astype(BF16)
    for t in range(sz.base):
        buffer, u = (xs, t) if t < sz.x_blocks else (bs, t - sz.x_blocks)
        cols = slice(u * LANES, (u + 1) * LANES)
        first[t * HALO : (t + 1) * HALO, :] = buffer[HALO : 2 * HALO, cols]
    return weight


def in_first(sz):
    return lax.axis_index("seq") < sz.places


def in_last(sz):
    return lax.axis_index("seq") >= (sz.blocks - 1) * sz.places


def state_kernel(sz, bias, alog, m0, ma, mb, mc, taps_x, taps_b, halo,
                 msg, xc, bc, stats, first, xs, bs, dts, tails, packed):
    messages = by_partner(m0, (ma, mb, mc), ORDER)

    def work():
        weight = convolve(sz, bias, alog, messages, taps_x, taps_b, halo, xc, bc, stats, first, xs, bs, dts, True)
        write_state(sz, messages, weight, msg, xc, bc, xs, bs, tails, packed)

    if not sz.late:
        work()
    else:
        pl.when(jnp.logical_not(in_last(sz)))(work)

        @pl.when(in_last(sz))
        def _():
            msg[...] = jnp.zeros(msg.shape, msg.dtype)


def write_state(sz, messages, weight, msg, xc, bc, xs, bs, tails, packed):
    place = place_of(sz)
    states = []
    for t in range(sz.x_blocks):
        cols = slice(t * LANES, (t + 1) * LANES)
        turned = jnp.transpose(xc[:, cols].astype(F32))
        up = turned[0:HEAD_DIM] * weight[2 * t : 2 * t + 1]
        down = turned[HEAD_DIM:LANES] * weight[2 * t + 1 : 2 * t + 2]
        weighted = jnp.concatenate([up, down], axis=0).astype(BF16)
        states.append(dot(weighted, bc[...], NN))
    for t in range(sz.x_blocks):
        for s in range(sz.s_blocks):
            row = (t * sz.s_blocks + s) * LANES
            part = states[t][:, s * LANES : (s + 1) * LANES]
            msg[row : row + LANES, :] = part.astype(msg.dtype)
    base, over = sz.x_blocks * STATE, sz.taps - 1
    for k, m in enumerate(messages):
        source = lax.bitwise_xor(place, k)
        at = pl.ds(pl.multiple_of(source * HALO, 8), HALO)
        for u in range(sz.s_blocks):
            tails[at, u * LANES : (u + 1) * LANES] = m[tail_rows(sz, k, sz.base + u), :].astype(F32)
    packed[...] = jnp.zeros(packed.shape, F32)
    for t in range(sz.cols):
        if t < sz.base:
            buffer, u = (xs, t) if t < sz.x_blocks else (bs, t - sz.x_blocks)
            cols = slice(u * LANES, (u + 1) * LANES)
            last = buffer[BLOCK : BLOCK + HALO, cols]
        else:
            cols = slice((t - sz.base) * LANES, (t - sz.base + 1) * LANES)
            last = tails[(sz.places - 1) * HALO :, cols]
        packed[t * over : (t + 1) * over, :] = last[HALO - over :]
    msg[base:, :] = packed[...].astype(msg.dtype)


def hand_out(sz, total, outs):
    place = place_of(sz)
    for k, o in enumerate(outs):
        target = lax.bitwise_xor(place, k)
        o[...] = total[pl.ds(pl.multiple_of(target * sz.rows, 8), sz.rows), :].astype(BF16)


def inner_kernel(sz, _xc, _bc, _stats, _first, skip, bias, alog, m0, ma, mb, mc, taps_x, taps_b, taps_c, halo, *rest):
    messages = by_partner(m0, (ma, mb, mc), ORDER)
    extra, rest = rest[: len(SPLIT)], rest[len(SPLIT) :]
    late, rest = rest[: sz.late], rest[sz.late :]
    xc, bc, stats, first, *early, out, growth, gains, cc, columns, first_c, cs, turned, xs, bs, dts = rest
    chain = sz.blocks > 2
    place = place_of(sz)

    def gather_c(messages, split):
        parts, starts = [], []
        for k, m in enumerate(messages):
            apart = split and k in SPLIT
            parts.append(extra[SPLIT.index(k)] if apart else m)
            starts.append([u * sz.rows for u in range(sz.s_blocks)] if apart else layout(sz, k, False)[0][sz.base :])
        gather(sz, cs, place, parts, starts)

    if sz.late:
        pl.when(in_first(sz))(lambda: gather_c(messages, True))

        @pl.when(in_last(sz))
        def _():
            late_messages = by_partner(m0, late, ORDER)
            convolve(sz, bias, alog, late_messages, taps_x, taps_b, halo, xc, bc, stats, first, xs, bs, dts, False)
            gather_c(late_messages, False)
    else:
        gather_c(messages, True)
    g = sz.per_group
    turned[...] = jnp.transpose(stats[...])
    columns[...] = turned[0:EDGE, :]
    skips = of_heads(sz, skip, place * g)
    for t in range(sz.s_blocks):
        cols = slice(t * LANES, (t + 1) * LANES)
        if chain:
            cs[0:HALO, cols] = halo[(sz.base + t) * HALO : (sz.base + t + 1) * HALO, :]
        else:
            cs[0:HALO, cols] = jnp.zeros((HALO, LANES), F32)
        first_c[t * HALO : (t + 1) * HALO, :] = cs[HALO : 2 * HALO, cols]
        taps = halved_taps(taps_c, t, sz.taps)
        cc[:, cols] = silu_half(conv_block(cs, BLOCK, taps, t)).astype(BF16)
    half = BLOCK // 2
    skip_keys = 0 if chain else jnp.where(in_first(sz), 0, EDGE)
    low_lanes = lax.broadcasted_iota(jnp.int32, (half, LANES), 1) < HEAD_DIM
    for t in range(sz.x_blocks):
        cols = slice(t * LANES, (t + 1) * LANES)
        gains[:, cols] = jnp.where(low_lanes[0:8], skips[2 * t : 2 * t + 1], skips[2 * t + 1 : 2 * t + 2])
    for r in range(2):
        width = half * (r + 1)
        at = slice(r * half, (r + 1) * half)
        scores = dot(cc[at, :], bc[0:width, :], NT)
        line = lax.broadcasted_iota(jnp.int32, (half, width), 0) + r * half
        spot = lax.broadcasted_iota(jnp.int32, (half, width), 1)
        keep = (spot <= line) & (spot >= skip_keys)
        for t in range(sz.x_blocks):
            cols = slice(t * LANES, (t + 1) * LANES)
            sums = []
            for h in (2 * t, 2 * t + 1):
                spread = turned[at, h : h + 1] - stats[h : h + 1, 0:width]
                rate = stats[g + h : g + h + 1, 0:width]
                mixing = scores * jnp.exp(jnp.where(keep, spread, -1e30)) * rate
                sums.append(dot(mixing.astype(BF16), xc[0:width, cols], NN))
            both = jnp.where(low_lanes, sums[0], sums[1])
            out[at, cols] = both + gains[0:1, cols] * xc[at, cols].astype(F32)
            rise = 2 * g + 2 * t
            growth[at, cols] = jnp.where(low_lanes, turned[at, rise : rise + 1], turned[at, rise + 1 : rise + 2])
    hand_out(sz, out, early)


def outer_kernel(sz, taps_x, taps_b, taps_c, xc, bc, cc, stats, columns, first, first_c, growth, gains,
                 inner, arrived, o0, o1, o2, o3, edge, ahead, c_all, total):
    chain = sz.blocks > 2
    place = place_of(sz)
    g = sz.per_group
    if chain:
        c_all[...] = cc[...]
    else:
        base = sz.x_blocks * STATE
        renewed, over = [], sz.taps - 1
        ahead[...] = arrived[base:, :].astype(F32)
        for t in range(sz.cols):
            cols = slice(t * LANES, (t + 1) * LANES)
            edge[HALO - over : HALO, cols] = ahead[t * over : (t + 1) * over, :]
            u = t - sz.base
            edge[HALO : 2 * HALO, cols] = (
                first[t * HALO : (t + 1) * HALO, :] if u < 0 else first_c[u * HALO : (u + 1) * HALO, :]
            )
        for t in range(sz.cols):
            which = (t >= sz.x_blocks) + (t >= sz.base)
            u = t - (0, sz.x_blocks, sz.base)[which]
            taps = halved_taps((taps_x, taps_b, taps_c)[which], u, sz.taps)
            fresh = silu_half(conv_block(edge, HALO, taps, t))
            old = (xc, bc, cc)[which][0:EDGE, u * LANES : (u + 1) * LANES].astype(F32)
            renewed.append(jnp.concatenate([fresh, old[HALO:EDGE]], axis=0).astype(BF16))
        for t in range(sz.s_blocks):
            cols = slice(t * LANES, (t + 1) * LANES)
            c_all[EDGE:, cols] = cc[EDGE:, cols]
            c_all[0:EDGE, cols] = renewed[sz.base + t]
        b_edge = jnp.concatenate(renewed[sz.x_blocks : sz.base], axis=1)
        edge_scores = dot(b_edge, c_all[...], NT)
        line = lax.broadcasted_iota(jnp.int32, (EDGE, BLOCK), 0)
        spot = lax.broadcasted_iota(jnp.int32, (EDGE, BLOCK), 1)
        keep = spot >= line
    for t in range(sz.x_blocks):
        cols = slice(t * LANES, (t + 1) * LANES)
        pieces = [
            arrived[(t * sz.s_blocks + s) * LANES : (t * sz.s_blocks + s + 1) * LANES, :]
            for s in range(sz.s_blocks)
        ]
        state = jnp.concatenate(pieces, axis=1)
        out = inner[:, cols] + dot(c_all[...], state, NT) * growth[:, cols]
        if not chain:
            mixed, values = [], []
            edge_low = lax.broadcasted_iota(jnp.int32, (EDGE, LANES), 1) < HEAD_DIM
            x_edge = renewed[t].astype(F32)
            for h in (2 * t, 2 * t + 1):
                spread = stats[h : h + 1, :] - columns[:, h : h + 1]
                rate = columns[:, g + h : g + h + 1]
                mixed.append(edge_scores * jnp.exp(jnp.where(keep, spread, -1e30)) * rate)
                mine = edge_low if h == 2 * t else jnp.logical_not(edge_low)
                values.append(jnp.where(mine, x_edge, 0.0))
            mixed = jnp.concatenate(mixed, axis=0).astype(BF16)
            values = jnp.concatenate(values, axis=0).astype(BF16)
            out = out + dot(mixed, values, TN)
            change = gains[0:1, cols] * (x_edge - xc[0:EDGE, cols].astype(F32))
            total[:, cols] = out
            total[0:EDGE, cols] = out[0:EDGE] + change
        else:
            total[:, cols] = out
    hand_out(sz, total, (o0, o1, o2, o3))


def norm_kernel(sz, o0, ra, rb, rc, e0, ea, eb, ec, z, gain, out, ready, sem):
    place = place_of(sz)
    width = sz.x_blocks * LANES
    copies = []
    early = by_partner(e0, (ea, eb, ec), RETURN)
    for k, part in enumerate(by_partner(o0, (ra, rb, rc), RETURN)):
        at = pl.ds(pl.multiple_of(lax.bitwise_xor(place, k) * width, LANES), width)
        gate = 0.5 * z[:, at].astype(F32)
        value = jnp.where(in_first(sz), early[k][...], part[...]).astype(F32) * silu_half(gate)
        mean = jnp.sum(value * value, axis=-1, keepdims=True) * (1.0 / width)
        ready[k] = (value * lax.rsqrt(mean + 1e-05) * gain[0:1, at]).astype(BF16)
        copies.append(pltpu.make_async_copy(ready.at[k], out.at[:, at], sem.at[k]))
        copies[-1].start()
    for copy in copies:
        copy.wait()


def call(kernel, sz, outs, scratch, specs, flops=0, touched=0, aliases=None, outputs=None):
    return pl.pallas_call(
        functools.partial(kernel, sz),
        out_shape=[jax.ShapeDtypeStruct(s, d) for s, d in outs],
        in_specs=specs,
        out_specs=outputs or [VMEM] * len(outs),
        input_output_aliases=aliases or {},
        scratch_shapes=[s if not isinstance(s, tuple) else pltpu.VMEM(*s) for s in scratch],
        compiler_params=pltpu.CompilerParams(vmem_limit_bytes=24 << 20),
        cost_estimate=pl.CostEstimate(flops=flops, bytes_accessed=touched, transcendentals=0),
    )


def body(x_in, b_in, c_in, z_in, dt_raw, dt_bias, a_log, d_skip, conv_x, conv_b, conv_c, norm_gain):
    seq_total = lax.axis_size("seq")
    sz = Sizes(x_in, b_in, dt_raw, seq_total, conv_x.shape[0])
    n, rows = sz.places, sz.rows
    chain = sz.blocks > 2
    cores = lax.axis_size("head")

    def swap(k, first, end):
        pairs = []
        for i in range(seq_total):
            for core in range(cores):
                there = (i - i % n + ((i % n) ^ k), core) if first <= i < end else (i, cores - 1 - core)
                pairs.append((i * cores + core, there[0] * cores + there[1]))
        return pairs

    def send(array, k, first, end):
        return lax.ppermute(array, ("seq", "head"), swap(k, first, end))

    def onward(k, wrap):
        pairs = [(i, i + n * k) for i in range(seq_total)]
        return [(i, j % seq_total) for i, j in pairs if wrap or j < seq_total]

    def ordered(arrays, order):
        return [arrays[0]] + [arrays[k] for k in order]

    def stay(*arrays):
        return [pltpu.with_memory_space_constraint(a, pltpu.HBM) for a in arrays]

    width = sz.x_blocks * LANES
    vectors = [v.reshape(1, -1) for v in (dt_bias, a_log, d_skip, norm_gain)]
    *sent, taps_x, taps_b, taps_c, bias, alog, skip, gain = call(
        pack_kernel,
        sz,
        [((layout(sz, k, True)[2], LANES), BF16) for k in range(n)]
        + [((sz.s_blocks * rows, LANES), BF16)] * len(SPLIT)
        + [((layout(sz, 0, False)[2], LANES), BF16)] * sz.late
        + [((sz.taps, width), BF16)]
        + [((sz.taps, STATE), BF16)] * 2
        + [((1, sz.heads), F32)] * 3
        + [((1, norm_gain.shape[0]), F32)],
        [((sz.heads, rows), BF16), pltpu.SemaphoreType.DMA((8 + (sz.cols + sz.s_blocks) * n,))],
        [HBM] * 11,
    )(*stay(x_in, b_in, c_in, dt_raw.T, conv_x, conv_b, conv_c, *vectors))
    came, split = sent[:n], sent[n : n + len(SPLIT)]
    end = n if sz.late else seq_total
    for k in ORDER:
        came[k] = send(came[k], k, 0, end)
    extra = [send(m, k, 0, end) for m, k in zip(split, SPLIT)]
    late = sent[n + len(SPLIT) :]
    late = [send(late[k - 1], k, n, seq_total) for k in ORDER if sz.late]

    padded = BLOCK + HALO
    edge_rows = sz.halo_rows
    if chain:
        place = lax.rem(lax.axis_index("seq"), n)
        ends = []
        for k, m in enumerate(came):
            ends.append(jnp.concatenate([m[tail_rows(sz, k, t)] for t in range(sz.cols)], axis=0))
        tail = lax.dynamic_index_in_dim(jnp.stack(ends), lax.bitwise_xor(place, n - 1), 0, keepdims=False)
        halo = lax.ppermute(tail, "seq", onward(1, False)).astype(F32)
    else:
        halo = jnp.zeros((8, LANES), F32)

    convolved = [
        ((BLOCK, width), BF16),
        ((BLOCK, STATE), BF16),
        ((sz.stat_rows, BLOCK), F32),
        ((sz.base * HALO, LANES), F32),
    ]
    buffers = [((padded, width), F32), ((padded, STATE), F32), ((sz.heads, BLOCK), F32)]
    msg, *held = call(
        state_kernel,
        sz,
        [((sz.x_blocks * STATE + edge_rows, LANES), F32 if chain else BF16)] + convolved,
        buffers
        + [
            ((n * HALO, STATE), F32),
            ((edge_rows, LANES), F32),
        ],
        [VMEM] * 9,
    )(bias, alog, *ordered(came, ORDER), taps_x, taps_b, halo)

    if chain:
        cut = sz.x_blocks * STATE
        grown = msg[:cut].reshape(sz.x_blocks, sz.s_blocks, 2, HEAD_DIM, LANES)
        fade = jnp.exp(held[2][: sz.per_group, BLOCK - 1]).reshape(sz.x_blocks, 1, 2, 1, 1)
        k = 1
        while k < sz.blocks:
            grown = grown + fade * lax.ppermute(grown, "seq", onward(k, False))
            fade = fade * lax.ppermute(fade, "seq", onward(k, False))
            k *= 2
        msg = jnp.concatenate([grown.reshape(cut, LANES), msg[cut:]], axis=0).astype(BF16)
    arrived = lax.ppermute(msg, "seq", onward(1, True))

    pieces = [((rows, width), BF16)] * n
    xc, bc, stats, first, *early, inner, growth, gains, cc, columns, first_c = call(
        inner_kernel,
        sz,
        convolved
        + pieces
        + [
            ((BLOCK, width), F32),
            ((BLOCK, width), F32),
            ((8, width), F32),
            ((BLOCK, STATE), BF16),
            ((EDGE, sz.stat_rows), F32),
            ((sz.s_blocks * HALO, LANES), F32),
        ],
        [((padded, STATE), F32), ((BLOCK, sz.stat_rows), F32)] + buffers,
        [VMEM] * (15 + len(SPLIT) + sz.late),
        aliases={i: i for i in range(4)},
        flops=1 << 30,
        touched=1 << 22,
    )(*held, skip, bias, alog, *ordered(came, ORDER), taps_x, taps_b, taps_c, halo, *extra, *late)

    for k in RETURN:
        early[k] = send(early[k], k, 0, n)

    back = call(
        outer_kernel,
        sz,
        pieces,
        [
            ((2 * HALO, sz.cols * LANES), F32),
            ((edge_rows, LANES), F32),
            ((BLOCK, STATE), BF16),
            ((BLOCK, width), F32),
        ],
        [VMEM] * 14,
    )(taps_x, taps_b, taps_c, xc, bc, cc, stats, columns, first, first_c, growth, gains, inner, arrived)
    back = list(back)
    for k in RETURN:
        back[k] = send(back[k], k, n, seq_total)

    out = call(
        norm_kernel,
        sz,
        [(x_in.shape, BF16)],
        [((n, rows, width), BF16), pltpu.SemaphoreType.DMA((n,))],
        [VMEM] * 10,
        outputs=[HBM],
    )(
        *ordered(back, RETURN), *ordered(early, RETURN), z_in, gain
    )
    return out[0]


def solution(mesh):
    rows, wide = P(("rep", "seq"), "head"), P(None, "head")
    placed = (rows,) * 5 + (P("head"),) * 3 + (wide,) * 3 + (P("head"),)
    return jax.shard_map(body, mesh=mesh, in_specs=placed, out_specs=rows, check_vma=False)
```

```python
import functools

import jax
import jax.numpy as jnp
from jax import lax
from jax.experimental import pallas as pl
from jax.experimental.pallas import tpu as pltpu
from jax.sharding import PartitionSpec as P


HEAD_DIM = 64
STATE = 256
BLOCK = 256
LANES = 128
HALO = 8
EDGE = 16
ORDER = (3, 2, 1)
RETURN = (3, 2, 1)
SPLIT = (1,)
F32 = jnp.float32
BF16 = jnp.bfloat16
VMEM = pl.BlockSpec(memory_space=pltpu.VMEM)
HBM = pl.BlockSpec(memory_space=pltpu.HBM)
NT = (((1,), (1,)), ((), ()))
TN = (((0,), (0,)), ((), ()))
NN = (((1,), (0,)), ((), ()))


def dot(a, b, dims):
    return lax.dot_general(a, b, dims, preferred_element_type=F32)


class Sizes:
    def __init__(self, x_in, b_in, dt_raw, seq_total, taps):
        self.rows = x_in.shape[0]
        self.heads = dt_raw.shape[1]
        self.groups = b_in.shape[1] // STATE
        self.per_group = self.heads // self.groups
        self.places = BLOCK // self.rows
        self.blocks = seq_total // self.places
        self.taps = taps
        self.x_blocks = self.per_group * HEAD_DIM // LANES
        self.s_blocks = STATE // LANES
        self.base = self.x_blocks + self.s_blocks
        self.cols = self.base + self.s_blocks
        self.halo_rows = -(-self.cols * (taps - 1) // 16) * 16
        self.pad_heads = max(8, self.per_group)
        self.stat_rows = 4 * self.per_group
        self.late = self.places - 1 if self.blocks == 2 else 0
        if self.places != self.groups or self.rows * 2 != LANES or self.places != 4:
            raise ValueError("unsupported shapes")


def lane(start):
    return pl.ds(pl.multiple_of(start, LANES), LANES)


def place_of(sz):
    return lax.rem(lax.axis_index("seq"), sz.places)


def by_partner(own, others, order):
    return [own] + [others[order.index(k)] for k in range(1, len(order) + 1)]


def silu_half(half):
    return half + half * jnp.tanh(half)


def lanes_of(array, group, width):
    return array.at[:, pl.ds(pl.multiple_of(group * width, LANES), width)]


def layout(sz, k, apart):
    c_high = HALO if apart and k in SPLIT else sz.rows
    starts = [t * sz.rows for t in range(sz.base)] + [sz.base * sz.rows + u * c_high for u in range(sz.s_blocks)]
    end = starts[-1] + c_high
    return starts, end, end + sz.heads


def tail_rows(sz, k, t):
    starts, _, _ = layout(sz, k, True)
    last = starts[t] + (HALO if t >= sz.base and k in SPLIT else sz.rows)
    return slice(last - HALO, last)


def fetch_all(pairs, sem):
    copies = [pltpu.make_async_copy(source, target, sem.at[i]) for i, (source, target) in enumerate(pairs)]
    for copy in copies:
        copy.start()
    return copies


def message_parts(sz, k, group, x, b, c, m, extra):
    rows, apart = sz.rows, extra is not None
    starts, _, _ = layout(sz, k, apart)
    pairs = []
    for t in range(sz.cols):
        which = (t >= sz.x_blocks) + (t >= sz.base)
        u = t - (0, sz.x_blocks, sz.base)[which]
        first = group * (sz.x_blocks, sz.s_blocks, sz.s_blocks)[which] + u
        source = (x, b, c)[which].at[:, lane(first * LANES)]
        if which == 2 and apart and k in SPLIT:
            pairs.append((source, extra[SPLIT.index(k)].at[u * rows : (u + 1) * rows, :]))
            pairs.append((source.at[rows - HALO :, :], m.at[starts[t] : starts[t] + HALO, :]))
        else:
            pairs.append((source, m.at[starts[t] : starts[t] + rows, :]))
    return pairs


def pack_kernel(sz, x, b, c, dt, conv_x, conv_b, conv_c, bias, alog, skip, gain, m0, m1, m2, m3, *rest):
    extra, rest = rest[: len(SPLIT)], rest[len(SPLIT) :]
    late, rest = rest[: sz.late], rest[sz.late :]
    taps_x, taps_b, taps_c, bias_here, alog_here, skip_here, gain_here, dt_here, sem = rest
    place = place_of(sz)
    shared = [
        (dt, dt_here),
        (lanes_of(conv_x, place, sz.x_blocks * LANES), taps_x),
        (lanes_of(conv_b, place, STATE), taps_b),
        (lanes_of(conv_c, place, STATE), taps_c),
        (bias, bias_here),
        (alog, alog_here),
        (skip, skip_here),
        (gain, gain_here),
    ]

    def fill(messages, split):
        pairs = shared[:1]
        for k in (*ORDER, 0):
            m = messages[k]
            group = lax.bitwise_xor(place, k)
            pairs = pairs + message_parts(sz, k, group, x, b, c, m, extra if split else None)
        copies = fetch_all(pairs + shared[1:], sem)
        copies[0].wait()
        here = dt_here[...].astype(F32)
        twice = jnp.concatenate([here, here], axis=1)
        spot = lax.broadcasted_iota(jnp.int32, twice.shape, 1)
        mine = lax.div(spot, sz.rows) == lax.rem(place, 2)
        spread = jnp.where(mine, twice, 0.0).astype(BF16)
        for k, m in enumerate(messages):
            m[layout(sz, k, split)[1] :, :] = spread
        for copy in copies[1:]:
            copy.wait()

    if sz.late:
        pl.when(in_first(sz))(lambda: fill((m0, m1, m2, m3), True))
        pl.when(in_last(sz))(lambda: fill((m0, *late), False))
    else:
        fill((m0, m1, m2, m3), True)


def conv_block(buffer, count, taps, t):
    n = len(taps)
    first = HALO - (n - 1)
    cols = slice(t * LANES, (t + 1) * LANES)
    total = taps[0] * buffer[first : first + count, cols]
    for i in range(1, n):
        total = total + taps[i] * buffer[first + i : first + i + count, cols]
    return total


def conv_rows(sz, pairs, source, skip, count):
    row = pl.multiple_of(source * sz.rows + skip, 16)
    for buffer, taps_ref, result in pairs:
        for t in range(result.shape[1] // LANES):
            cols = slice(t * LANES, (t + 1) * LANES)
            taps = halved_taps(taps_ref, t, sz.taps)
            window = buffer[pl.ds(row, count + HALO), cols]
            at = HALO - (sz.taps - 1)
            total = taps[0] * window[at : at + count]
            for i in range(1, sz.taps):
                total = total + taps[i] * window[at + i : at + i + count]
            result[pl.ds(row, count), cols] = silu_half(total).astype(BF16)


def halved_taps(ref, t, n):
    return [0.5 * ref[i : i + 1, t * LANES : (t + 1) * LANES].astype(F32) for i in range(n)]


def gather(sz, buffer, place, messages, starts, only=None):
    for k, m in enumerate(messages):
        if only is not None and k not in only:
            continue
        source = lax.bitwise_xor(place, k)
        at = pl.ds(pl.multiple_of(HALO + source * sz.rows, 8), sz.rows)
        for t, row in enumerate(starts[k]):
            buffer[at, t * LANES : (t + 1) * LANES] = m[row : row + sz.rows, :].astype(F32)


def of_heads(sz, ref, head0):
    shape = (sz.pad_heads, sz.heads)
    line = lax.broadcasted_iota(jnp.int32, shape, 0)
    spot = lax.broadcasted_iota(jnp.int32, shape, 1)
    row = jnp.broadcast_to(ref[...], shape)
    return jnp.sum(jnp.where(spot == line + head0, row, 0.0), axis=1, keepdims=True)


def convolve(sz, bias, alog, messages, taps_x, taps_b, halo, xc, bc, stats, first, xs, bs, dts, apart, begun=()):
    chain = sz.blocks > 2
    place = place_of(sz)
    places = [layout(sz, k, apart) for k in range(sz.places)]
    logits = [m[at[1] :, :].astype(F32) for m, at in zip(messages, places)]
    near, far = logits[0] + logits[1], logits[2] + logits[3]
    side = lax.div(place, 2)
    dts[:, lane(side * LANES)] = near
    dts[:, lane((1 - side) * LANES)] = far
    head0 = place * sz.per_group
    raw = pltpu.roll(dts[...], lax.rem(sz.heads - head0, sz.heads), 0)[0 : sz.pad_heads]
    raw = raw + of_heads(sz, bias, head0)
    rates = jnp.maximum(raw, 0.0) + jnp.log1p(jnp.exp(-jnp.abs(raw)))
    decays = -jnp.exp(of_heads(sz, alog, head0)) * rates
    high = decays.astype(BF16).astype(F32)
    middle = (decays - high).astype(BF16).astype(F32)
    low = decays - high - middle
    parts = jnp.concatenate([high, middle, low], axis=0).astype(BF16)
    line = lax.broadcasted_iota(jnp.int32, (BLOCK, BLOCK), 0)
    spot = lax.broadcasted_iota(jnp.int32, (BLOCK, BLOCK), 1)
    upto = jnp.where(line <= spot, 1.0, 0.0).astype(BF16)
    sums = dot(parts, upto, NN)
    n = sz.pad_heads
    log_decay = sums[0:n] + sums[n : 2 * n] + sums[2 * n : 3 * n]
    weight = jnp.exp(log_decay[:, BLOCK - 1 : BLOCK] - log_decay) * rates
    g = sz.per_group
    stats[0:g, :] = log_decay[0:g]
    stats[g : 2 * g, :] = rates[0:g]
    stats[2 * g : 3 * g, :] = jnp.exp(log_decay)[0:g]
    stats[3 * g : 4 * g, :] = weight[0:g]
    rest = [k for k in range(sz.places) if k not in begun]
    gather(sz, xs, place, messages, [at[0][: sz.x_blocks] for at in places], rest)
    gather(sz, bs, place, messages, [at[0][sz.x_blocks : sz.base] for at in places], rest)
    for t in range(sz.base):
        buffer, u = (xs, t) if t < sz.x_blocks else (bs, t - sz.x_blocks)
        cols = slice(u * LANES, (u + 1) * LANES)
        if chain:
            buffer[0:HALO, cols] = halo[t * HALO : (t + 1) * HALO, :]
        else:
            buffer[0:HALO, cols] = jnp.zeros((HALO, LANES), F32)
    if begun:
        pairs = ((bs, taps_b, bc), (xs, taps_x, xc))
        for k in range(sz.places):
            conv_rows(sz, pairs, lax.bitwise_xor(place, k), 0, EDGE if k in begun else sz.rows)
    else:
        for t in range(sz.s_blocks):
            taps = halved_taps(taps_b, t, sz.taps)
            cols = slice(t * LANES, (t + 1) * LANES)
            bc[:, cols] = silu_half(conv_block(bs, BLOCK, taps, t)).astype(BF16)
        for t in range(sz.x_blocks):
            taps = halved_taps(taps_x, t, sz.taps)
            cols = slice(t * LANES, (t + 1) * LANES)
            xc[:, cols] = silu_half(conv_block(xs, BLOCK, taps, t)).astype(BF16)
    for t in range(sz.base):
        buffer, u = (xs, t) if t < sz.x_blocks else (bs, t - sz.x_blocks)
        cols = slice(u * LANES, (u + 1) * LANES)
        first[t * HALO : (t + 1) * HALO, :] = buffer[HALO : 2 * HALO, cols]
    return weight


def in_first(sz):
    return lax.axis_index("seq") < sz.places


def in_last(sz):
    return lax.axis_index("seq") >= (sz.blocks - 1) * sz.places


def begin_kernel(sz, m0, ma, mb, taps_x, taps_b, xs, bs, xc, bc):
    place = place_of(sz)

    @pl.when(in_first(sz))
    def _():
        messages = [None] * sz.places
        messages[0], messages[ORDER[0]], messages[ORDER[1]] = m0, ma, mb
        begun = [k for k in range(sz.places) if k != ORDER[-1]]
        starts = [layout(sz, k, True)[0] for k in range(sz.places)]
        gather(sz, xs, place, messages, [at[: sz.x_blocks] for at in starts], begun)
        gather(sz, bs, place, messages, [at[sz.x_blocks : sz.base] for at in starts], begun)
        for k in begun:
            source = lax.bitwise_xor(place, k)
            conv_rows(sz, ((bs, taps_b, bc), (xs, taps_x, xc)), source, EDGE, sz.rows - EDGE)


def state_kernel(sz, *refs):
    if sz.late:
        refs = refs[4:]
    bias, alog, m0, ma, mb, mc, taps_x, taps_b, halo, xs, bs, xc, bc, msg, stats, first, dts, tails, packed = refs
    messages = by_partner(m0, (ma, mb, mc), ORDER)
    begun = [k for k in range(sz.places) if k != ORDER[-1]] if sz.late else []

    def work():
        weight = convolve(sz, bias, alog, messages, taps_x, taps_b, halo, xc, bc, stats, first, xs, bs, dts, True, begun)
        write_state(sz, messages, weight, msg, xc, bc, xs, bs, tails, packed)

    if not sz.late:
        work()
    else:
        pl.when(jnp.logical_not(in_last(sz)))(work)

        @pl.when(in_last(sz))
        def _():
            msg[...] = jnp.zeros(msg.shape, msg.dtype)


def write_state(sz, messages, weight, msg, xc, bc, xs, bs, tails, packed):
    place = place_of(sz)
    states = []
    for t in range(sz.x_blocks):
        cols = slice(t * LANES, (t + 1) * LANES)
        turned = jnp.transpose(xc[:, cols].astype(F32))
        up = turned[0:HEAD_DIM] * weight[2 * t : 2 * t + 1]
        down = turned[HEAD_DIM:LANES] * weight[2 * t + 1 : 2 * t + 2]
        weighted = jnp.concatenate([up, down], axis=0).astype(BF16)
        states.append(dot(weighted, bc[...], NN))
    for t in range(sz.x_blocks):
        for s in range(sz.s_blocks):
            row = (t * sz.s_blocks + s) * LANES
            part = states[t][:, s * LANES : (s + 1) * LANES]
            msg[row : row + LANES, :] = part.astype(msg.dtype)
    base, over = sz.x_blocks * STATE, sz.taps - 1
    for k, m in enumerate(messages):
        source = lax.bitwise_xor(place, k)
        at = pl.ds(pl.multiple_of(source * HALO, 8), HALO)
        for u in range(sz.s_blocks):
            tails[at, u * LANES : (u + 1) * LANES] = m[tail_rows(sz, k, sz.base + u), :].astype(F32)
    packed[...] = jnp.zeros(packed.shape, F32)
    for t in range(sz.cols):
        if t < sz.base:
            buffer, u = (xs, t) if t < sz.x_blocks else (bs, t - sz.x_blocks)
            cols = slice(u * LANES, (u + 1) * LANES)
            last = buffer[BLOCK : BLOCK + HALO, cols]
        else:
            cols = slice((t - sz.base) * LANES, (t - sz.base + 1) * LANES)
            last = tails[(sz.places - 1) * HALO :, cols]
        packed[t * over : (t + 1) * over, :] = last[HALO - over :]
    msg[base:, :] = packed[...].astype(msg.dtype)


def hand_out(sz, total, outs):
    place = place_of(sz)
    for k, o in enumerate(outs):
        target = lax.bitwise_xor(place, k)
        o[...] = total[pl.ds(pl.multiple_of(target * sz.rows, 8), sz.rows), :].astype(BF16)


def inner_kernel(sz, _xc, _bc, _stats, _first, skip, bias, alog, m0, ma, mb, mc, taps_x, taps_b, taps_c, halo, *rest):
    messages = by_partner(m0, (ma, mb, mc), ORDER)
    extra, rest = rest[: len(SPLIT)], rest[len(SPLIT) :]
    late, rest = rest[: sz.late], rest[sz.late :]
    xc, bc, stats, first, *early, out, growth, gains, cc, columns, first_c, cs, turned, xs, bs, dts = rest
    chain = sz.blocks > 2
    place = place_of(sz)

    def gather_c(messages, split):
        parts, starts = [], []
        for k, m in enumerate(messages):
            apart = split and k in SPLIT
            parts.append(extra[SPLIT.index(k)] if apart else m)
            starts.append([u * sz.rows for u in range(sz.s_blocks)] if apart else layout(sz, k, False)[0][sz.base :])
        gather(sz, cs, place, parts, starts)

    if sz.late:
        pl.when(in_first(sz))(lambda: gather_c(messages, True))

        @pl.when(in_last(sz))
        def _():
            late_messages = by_partner(m0, late, ORDER)
            convolve(sz, bias, alog, late_messages, taps_x, taps_b, halo, xc, bc, stats, first, xs, bs, dts, False)
            gather_c(late_messages, False)
    else:
        gather_c(messages, True)
    g = sz.per_group
    turned[...] = jnp.transpose(stats[...])
    columns[...] = turned[0:EDGE, :]
    skips = of_heads(sz, skip, place * g)
    for t in range(sz.s_blocks):
        cols = slice(t * LANES, (t + 1) * LANES)
        if chain:
            cs[0:HALO, cols] = halo[(sz.base + t) * HALO : (sz.base + t + 1) * HALO, :]
        else:
            cs[0:HALO, cols] = jnp.zeros((HALO, LANES), F32)
        first_c[t * HALO : (t + 1) * HALO, :] = cs[HALO : 2 * HALO, cols]
        taps = halved_taps(taps_c, t, sz.taps)
        cc[:, cols] = silu_half(conv_block(cs, BLOCK, taps, t)).astype(BF16)
    half = BLOCK // 2
    skip_keys = 0 if chain else jnp.where(in_first(sz), 0, EDGE)
    low_lanes = lax.broadcasted_iota(jnp.int32, (half, LANES), 1) < HEAD_DIM
    for t in range(sz.x_blocks):
        cols = slice(t * LANES, (t + 1) * LANES)
        gains[:, cols] = jnp.where(low_lanes[0:8], skips[2 * t : 2 * t + 1], skips[2 * t + 1 : 2 * t + 2])
    for r in range(2):
        width = half * (r + 1)
        at = slice(r * half, (r + 1) * half)
        scores = dot(cc[at, :], bc[0:width, :], NT)
        line = lax.broadcasted_iota(jnp.int32, (half, width), 0) + r * half
        spot = lax.broadcasted_iota(jnp.int32, (half, width), 1)
        keep = (spot <= line) & (spot >= skip_keys)
        for t in range(sz.x_blocks):
            cols = slice(t * LANES, (t + 1) * LANES)
            sums = []
            for h in (2 * t, 2 * t + 1):
                spread = turned[at, h : h + 1] - stats[h : h + 1, 0:width]
                rate = stats[g + h : g + h + 1, 0:width]
                mixing = scores * jnp.exp(jnp.where(keep, spread, -1e30)) * rate
                sums.append(dot(mixing.astype(BF16), xc[0:width, cols], NN))
            both = jnp.where(low_lanes, sums[0], sums[1])
            out[at, cols] = both + gains[0:1, cols] * xc[at, cols].astype(F32)
            rise = 2 * g + 2 * t
            growth[at, cols] = jnp.where(low_lanes, turned[at, rise : rise + 1], turned[at, rise + 1 : rise + 2])
    hand_out(sz, out, early)


def outer_kernel(sz, taps_x, taps_b, taps_c, xc, bc, cc, stats, columns, first, first_c, growth, gains,
                 inner, arrived, o0, o1, o2, o3, edge, ahead, c_head, total):
    chain = sz.blocks > 2
    g, half = sz.per_group, BLOCK // 2
    if not chain:
        base = sz.x_blocks * STATE
        renewed, over = [], sz.taps - 1
        ahead[...] = arrived[base:, :].astype(F32)
        for t in range(sz.cols):
            cols = slice(t * LANES, (t + 1) * LANES)
            edge[HALO - over : HALO, cols] = ahead[t * over : (t + 1) * over, :]
            u = t - sz.base
            edge[HALO : 2 * HALO, cols] = (
                first[t * HALO : (t + 1) * HALO, :] if u < 0 else first_c[u * HALO : (u + 1) * HALO, :]
            )
        for t in range(sz.cols):
            which = (t >= sz.x_blocks) + (t >= sz.base)
            u = t - (0, sz.x_blocks, sz.base)[which]
            taps = halved_taps((taps_x, taps_b, taps_c)[which], u, sz.taps)
            fresh = silu_half(conv_block(edge, HALO, taps, t))
            old = (xc, bc, cc)[which][0:EDGE, u * LANES : (u + 1) * LANES].astype(F32)
            renewed.append(jnp.concatenate([fresh, old[HALO:EDGE]], axis=0).astype(BF16))
        for t in range(sz.s_blocks):
            cols = slice(t * LANES, (t + 1) * LANES)
            c_head[EDGE:, cols] = cc[EDGE:half, cols]
            c_head[0:EDGE, cols] = renewed[sz.base + t]
        b_edge = jnp.concatenate(renewed[sz.x_blocks : sz.base], axis=1)
        edge_scores = jnp.concatenate([dot(b_edge, c_head[...], NT), dot(b_edge, cc[half:, :], NT)], axis=1)
        line = lax.broadcasted_iota(jnp.int32, (EDGE, BLOCK), 0)
        spot = lax.broadcasted_iota(jnp.int32, (EDGE, BLOCK), 1)
        keep = spot >= line
    for t in range(sz.x_blocks):
        cols = slice(t * LANES, (t + 1) * LANES)
        pieces = [
            arrived[(t * sz.s_blocks + s) * LANES : (t * sz.s_blocks + s + 1) * LANES, :]
            for s in range(sz.s_blocks)
        ]
        state = jnp.concatenate(pieces, axis=1)
        out = inner[:, cols] + dot(cc[...], state, NT) * growth[:, cols]
        if not chain:
            mixed, values = [], []
            edge_low = lax.broadcasted_iota(jnp.int32, (EDGE, LANES), 1) < HEAD_DIM
            x_edge = renewed[t].astype(F32)
            for h in (2 * t, 2 * t + 1):
                spread = stats[h : h + 1, :] - columns[:, h : h + 1]
                rate = columns[:, g + h : g + h + 1]
                mixed.append(edge_scores * jnp.exp(jnp.where(keep, spread, -1e30)) * rate)
                mine = edge_low if h == 2 * t else jnp.logical_not(edge_low)
                values.append(jnp.where(mine, x_edge, 0.0))
            mixed = jnp.concatenate(mixed, axis=0).astype(BF16)
            values = jnp.concatenate(values, axis=0).astype(BF16)
            within = dot(mixed, values, TN)
            total[EDGE:, cols] = out[EDGE:] + within[EDGE:]
            fresh = dot(c_head[0:EDGE, :], state, NT) * growth[0:EDGE, cols]
            change = gains[0:1, cols] * (x_edge - xc[0:EDGE, cols].astype(F32))
            total[0:EDGE, cols] = inner[0:EDGE, cols] + fresh + within[0:EDGE] + change
        else:
            total[:, cols] = out
    hand_out(sz, total, (o0, o1, o2, o3))


def norm_kernel(sz, o0, ra, rb, rc, e0, ea, eb, ec, z, gain, out, ready, sem):
    place = place_of(sz)
    width = sz.x_blocks * LANES
    copies = []
    early = by_partner(e0, (ea, eb, ec), RETURN)
    for k, part in enumerate(by_partner(o0, (ra, rb, rc), RETURN)):
        at = pl.ds(pl.multiple_of(lax.bitwise_xor(place, k) * width, LANES), width)
        gate = 0.5 * z[:, at].astype(F32)
        value = jnp.where(in_first(sz), early[k][...], part[...]).astype(F32) * silu_half(gate)
        mean = jnp.sum(value * value, axis=-1, keepdims=True) * (1.0 / width)
        ready[k] = (value * lax.rsqrt(mean + 1e-05) * gain[0:1, at]).astype(BF16)
        copies.append(pltpu.make_async_copy(ready.at[k], out.at[:, at], sem.at[k]))
        copies[-1].start()
    for copy in copies:
        copy.wait()


def call(kernel, sz, outs, scratch, specs, flops=0, touched=0, aliases=None, outputs=None):
    return pl.pallas_call(
        functools.partial(kernel, sz),
        out_shape=[jax.ShapeDtypeStruct(s, d) for s, d in outs],
        in_specs=specs,
        out_specs=outputs or [VMEM] * len(outs),
        input_output_aliases=aliases or {},
        scratch_shapes=[s if not isinstance(s, tuple) else pltpu.VMEM(*s) for s in scratch],
        compiler_params=pltpu.CompilerParams(vmem_limit_bytes=24 << 20),
        cost_estimate=pl.CostEstimate(flops=flops, bytes_accessed=touched, transcendentals=0),
    )


def body(x_in, b_in, c_in, z_in, dt_raw, dt_bias, a_log, d_skip, conv_x, conv_b, conv_c, norm_gain):
    seq_total = lax.axis_size("seq")
    sz = Sizes(x_in, b_in, dt_raw, seq_total, conv_x.shape[0])
    n, rows = sz.places, sz.rows
    chain = sz.blocks > 2
    cores = lax.axis_size("head")

    def swap(k, first, end):
        pairs = []
        for i in range(seq_total):
            for core in range(cores):
                there = (i - i % n + ((i % n) ^ k), core) if first <= i < end else (i, cores - 1 - core)
                pairs.append((i * cores + core, there[0] * cores + there[1]))
        return pairs

    def send(array, k, first, end):
        return lax.ppermute(array, ("seq", "head"), swap(k, first, end))

    def onward(k, wrap):
        pairs = [(i, i + n * k) for i in range(seq_total)]
        return [(i, j % seq_total) for i, j in pairs if wrap or j < seq_total]

    def ordered(arrays, order):
        return [arrays[0]] + [arrays[k] for k in order]

    def stay(*arrays):
        return [pltpu.with_memory_space_constraint(a, pltpu.HBM) for a in arrays]

    width = sz.x_blocks * LANES
    vectors = [v.reshape(1, -1) for v in (dt_bias, a_log, d_skip, norm_gain)]
    *sent, taps_x, taps_b, taps_c, bias, alog, skip, gain = call(
        pack_kernel,
        sz,
        [((layout(sz, k, True)[2], LANES), BF16) for k in range(n)]
        + [((sz.s_blocks * rows, LANES), BF16)] * len(SPLIT)
        + [((layout(sz, 0, False)[2], LANES), BF16)] * sz.late
        + [((sz.taps, width), BF16)]
        + [((sz.taps, STATE), BF16)] * 2
        + [((1, sz.heads), F32)] * 3
        + [((1, norm_gain.shape[0]), F32)],
        [((sz.heads, rows), BF16), pltpu.SemaphoreType.DMA((8 + (sz.cols + sz.s_blocks) * n,))],
        [HBM] * 11,
    )(*stay(x_in, b_in, c_in, dt_raw.T, conv_x, conv_b, conv_c, *vectors))
    came, split = sent[:n], sent[n : n + len(SPLIT)]
    end = n if sz.late else seq_total
    for k in ORDER:
        came[k] = send(came[k], k, 0, end)
    extra = [send(m, k, 0, end) for m, k in zip(split, SPLIT)]
    late = sent[n + len(SPLIT) :]
    late = [send(late[k - 1], k, n, seq_total) for k in ORDER if sz.late]

    padded = BLOCK + HALO
    edge_rows = sz.halo_rows
    if chain:
        place = lax.rem(lax.axis_index("seq"), n)
        ends = []
        for k, m in enumerate(came):
            ends.append(jnp.concatenate([m[tail_rows(sz, k, t)] for t in range(sz.cols)], axis=0))
        tail = lax.dynamic_index_in_dim(jnp.stack(ends), lax.bitwise_xor(place, n - 1), 0, keepdims=False)
        halo = lax.ppermute(tail, "seq", onward(1, False)).astype(F32)
    else:
        halo = jnp.zeros((8, LANES), F32)

    convolved = [
        ((BLOCK, width), BF16),
        ((BLOCK, STATE), BF16),
        ((sz.stat_rows, BLOCK), F32),
        ((sz.base * HALO, LANES), F32),
    ]
    buffers = [((padded, width), F32), ((padded, STATE), F32), ((sz.heads, BLOCK), F32)]
    parts = [((padded, width), F32), ((padded, STATE), F32), *convolved[:2]]
    start = []
    if sz.late:
        start = call(begin_kernel, sz, parts, [], [VMEM] * 5, flops=1 << 28, touched=1 << 20)(
            *ordered(came, ORDER)[:3], taps_x, taps_b
        )
    _, _, xc, bc, msg, stats, first = call(
        state_kernel,
        sz,
        parts + [((sz.x_blocks * STATE + edge_rows, LANES), F32 if chain else BF16)] + convolved[2:],
        [
            ((sz.heads, BLOCK), F32),
            ((n * HALO, STATE), F32),
            ((edge_rows, LANES), F32),
        ],
        [VMEM] * (9 + len(start)),
        aliases={i: i for i in range(len(start))},
    )(*start, bias, alog, *ordered(came, ORDER), taps_x, taps_b, halo)
    held = [xc, bc, stats, first]

    if chain:
        cut = sz.x_blocks * STATE
        grown = msg[:cut].reshape(sz.x_blocks, sz.s_blocks, 2, HEAD_DIM, LANES)
        fade = jnp.exp(held[2][: sz.per_group, BLOCK - 1]).reshape(sz.x_blocks, 1, 2, 1, 1)
        k = 1
        while k < sz.blocks:
            grown = grown + fade * lax.ppermute(grown, "seq", onward(k, False))
            fade = fade * lax.ppermute(fade, "seq", onward(k, False))
            k *= 2
        msg = jnp.concatenate([grown.reshape(cut, LANES), msg[cut:]], axis=0).astype(BF16)
    arrived = lax.ppermute(msg, "seq", onward(1, True))

    pieces = [((rows, width), BF16)] * n
    xc, bc, stats, first, *early, inner, growth, gains, cc, columns, first_c = call(
        inner_kernel,
        sz,
        convolved
        + pieces
        + [
            ((BLOCK, width), F32),
            ((BLOCK, width), F32),
            ((8, width), F32),
            ((BLOCK, STATE), BF16),
            ((EDGE, sz.stat_rows), F32),
            ((sz.s_blocks * HALO, LANES), F32),
        ],
        [((padded, STATE), F32), ((BLOCK, sz.stat_rows), F32)] + buffers,
        [VMEM] * (15 + len(SPLIT) + sz.late),
        aliases={i: i for i in range(4)},
        flops=1 << 30,
        touched=1 << 22,
    )(*held, skip, bias, alog, *ordered(came, ORDER), taps_x, taps_b, taps_c, halo, *extra, *late)

    for k in RETURN:
        early[k] = send(early[k], k, 0, n)

    back = call(
        outer_kernel,
        sz,
        pieces,
        [
            ((2 * HALO, sz.cols * LANES), F32),
            ((edge_rows, LANES), F32),
            ((BLOCK // 2, STATE), BF16),
            ((BLOCK, width), F32),
        ],
        [VMEM] * 14,
    )(taps_x, taps_b, taps_c, xc, bc, cc, stats, columns, first, first_c, growth, gains, inner, arrived)
    back = list(back)
    for k in RETURN:
        back[k] = send(back[k], k, n, seq_total)

    out = call(
        norm_kernel,
        sz,
        [(x_in.shape, BF16)],
        [((n, rows, width), BF16), pltpu.SemaphoreType.DMA((n,))],
        [VMEM] * 10,
        outputs=[HBM],
    )(
        *ordered(back, RETURN), *ordered(early, RETURN), z_in, gain
    )
    return out[0]


def solution(mesh):
    rows, wide = P(("rep", "seq"), "head"), P(None, "head")
    placed = (rows,) * 5 + (P("head"),) * 3 + (wide,) * 3 + (P("head"),)
    return jax.shard_map(body, mesh=mesh, in_specs=placed, out_specs=rows, check_vma=False)
```
